128 devices in a mesh: group: 4 (over y_lo, core), mp: 32 (over z, x, y_hi).
Axes of the slice: x: 4, y: 4 (y_hi: 2, y_lo: 2; y = y_hi * 2 + y_lo), z: 4, core: 2. Of those that a mesh axis runs over, the one named last changes fastest.
Arguments:
- tokens: bfloat16 [5120, 2048], P(('group', 'mp')), may hold values from -6 to 6
- lengths: int32 [4, 8], P('group'), may hold values from 1 to 512, 1280 in all within a row
- query_gain: float32 [2048], replicated, may hold values from 0.5 to 8
- key_gain: float32 [2048], replicated, may hold values from 0.5 to 8
- attn_post_gain: float32 [2048], replicated, may hold values from 0.5 to 1.5
- mlp_post_gain: float32 [2048], replicated, may hold values from 0.5 to 1.5
- query_weight: float32 [2048, 2048], P(('mp', 'group')), may hold values from -4 to 4
- key_weight: float32 [2048, 2048], P(('mp', 'group')), may hold values from -4 to 4
- value_weight: float32 [2048, 2048], P(('mp', 'group')), may hold values from -0.125 to 0.125
- output_weight: float32 [2048, 2048], P(('mp', 'group')), may hold values from -0.125 to 0.125
- gate_weight: float32 [2048, 8192], P(('mp', 'group')), may hold values from -0.125 to 0.125
- up_weight: float32 [2048, 8192], P(('mp', 'group')), may hold values from -0.125 to 0.125
- down_weight: float32 [8192, 2048], P(('mp', 'group')), may hold values from -0.0625 to 0.0625
Outputs:
- layer_out: bfloat16 [5120, 2048], P(('group', 'mp'))
The draws below stay inside these ranges and needn't reach their ends.
Inputs may be any that keep to these rules, and one draw needn't show every extreme that they name: In each group the 8 prompt lengths sum to 1280; the longest is exactly 512.
All inputs are finite; a program needn't handle non-finite values.
Results may differ from the reference program's by a relative error of at most 0.034.
Values may be sent and summed in bfloat16 or wider, within the bound.
A program may use at most 64 MiB of HBM per device.

```python
import math
import jax
import jax.numpy as jnp
import numpy as np
from jax import lax

D = 2048
HEADS = 16
HEAD_DIM = 128
FF = 8192
TOK_GRP = 1280
MOST = 512
REQS = 8
GROUPS = 4
TOKENS = 5120
N_GROUP = 4


def gain_draw(key, salt):
    base = jnp.exp(jax.random.uniform(jax.random.fold_in(key, salt), (D,), jnp.float32, math.log(0.5), math.log(2.0)))
    return base


def column_ramped(key, salt):
    base = jax.random.truncated_normal(jax.random.fold_in(key, salt), -6.0, 6.0, (D, D), jnp.float32) / math.sqrt(D)
    ramp = jnp.exp(jnp.arange(D, dtype=jnp.float32) * (math.log(3.0) / (D - 1)))
    return base * ramp[None, :]


def draw_query_gain(key, part):
    return gain_draw(key, 11)


def draw_key_gain(key, part):
    return gain_draw(key, 31)


def draw_query_weight(key, part):
    return column_ramped(key, 51)


def draw_key_weight(key, part):
    return column_ramped(key, 71)


def steps_of(own_key, shape, shards, smallest, high):
    def one(dim, parts):
        steps = jax.random.uniform(jax.random.fold_in(jax.random.fold_in(own_key, 6), dim), (parts,), jnp.float32, smallest / len(shards), high / len(shards))
        return jnp.repeat(jnp.exp(steps), shape[dim] // parts).reshape((-1,) + (1,) * (len(shape) - dim - 1))

    factor_of = one(*shards[0])
    for cut in shards[1:]:
        factor_of = factor_of * one(*cut)
    return factor_of


def length_profile(number_of, total, bound, lean):
    weights = [(1 << 20) // math.isqrt(grade ** lean) + 1 for grade in range(2, number_of + 1)]
    rest, given = total - bound - (number_of - 1), [1] * (number_of - 1)
    while rest > 0:
        free = [i for i in range(number_of - 1) if given[i] < bound]
        mass, budget = sum([weights[i] for i in free]), rest
        for i in free:
            addition = min(bound - given[i], max(1, budget * weights[i] // mass), rest)
            given[i] = given[i] + addition
            rest = rest - addition
    return np.array([bound] + given)


def ragged_sizes(rng, amount, total, limit, slope):
    if amount == 2:
        one = jax.random.randint(rng, (), max(1, total - limit), min(limit, total - 1) + 1)
        return jnp.stack([one, total - one])
    tallies = jnp.asarray(length_profile(amount, total, limit, slope), jnp.int32)
    twos = (amount - 1) // 2
    source_of, sink = tallies[1:1 + 2 * twos:2], tallies[2:2 + 2 * twos:2]
    room = jnp.minimum(source_of - 1, limit - sink)
    shifted = jax.random.randint(jax.random.fold_in(rng, 1), (twos,), 0, 1 << 20) % (room + 1)
    tallies = tallies.at[1:1 + 2 * twos:2].set(source_of - shifted).at[2:2 + 2 * twos:2].set(sink + shifted)
    return tallies[jax.random.permutation(jax.random.fold_in(rng, 2), amount)]


def gaussian(stream_key, shape, width, bound, cuts=(), kind=jnp.bfloat16):
    values = jax.random.normal(stream_key, shape, jnp.float32) * width
    if len(cuts) > 0:
        values = steps_of(stream_key, shape, cuts, -0.22, 0.18) * values
    return jnp.clip(values, min=-bound, max=bound).astype(kind)


def setup_inputs(seed: int = 0) -> dict:
    arg_keys = jax.random.split(jax.random.key(seed), 14)
    return {
        "tokens": gaussian(arg_keys[0], (TOKENS, D), 1.0, 6.0, ((0, 128),)),
        "lengths": jax.vmap(lambda own: ragged_sizes(own, REQS, TOK_GRP, MOST, 2))(jax.random.split(arg_keys[1], GROUPS)).reshape((GROUPS, REQS)).astype(jnp.int32),
        "query_gain": draw_query_gain(jax.random.fold_in(arg_keys[13], 71), 0),
        "key_gain": draw_key_gain(jax.random.fold_in(arg_keys[13], 71), 0),
        "attn_post_gain": jnp.clip(1.0 + 0.1 * jax.random.normal(arg_keys[4], (D,), jnp.float32), 0.5, 1.5),
        "mlp_post_gain": jnp.clip(1.0 + 0.1 * jax.random.normal(arg_keys[5], (D,), jnp.float32), 0.5, 1.5),
        "query_weight": draw_query_weight(jax.random.fold_in(arg_keys[13], 71), 0),
        "key_weight": draw_key_weight(jax.random.fold_in(arg_keys[13], 71), 0),
        "value_weight": gaussian(arg_keys[8], (D, D), D ** -0.5, 0.125, ((0, 128),), jnp.float32),
        "output_weight": gaussian(arg_keys[9], (D, D), D ** -0.5, 0.125, ((0, 128),), jnp.float32),
        "gate_weight": gaussian(arg_keys[10], (D, FF), D ** -0.5, 0.125, ((0, 128),), jnp.float32),
        "up_weight": gaussian(arg_keys[11], (D, FF), D ** -0.5, 0.125, ((0, 128),), jnp.float32),
        "down_weight": gaussian(arg_keys[12], (FF, D), FF ** -0.5, 0.0625, ((0, 128),), jnp.float32),
    }


NORM_EPSILON = 1e-06
ROPE_BASE = 500000.0

def token_layout(prompt_lens, row_count):
    seg_ends = jnp.cumsum(prompt_lens).astype(jnp.int32)
    starts = (seg_ends - prompt_lens).astype(jnp.int32)
    indices = jnp.arange(row_count, dtype=jnp.int32)
    segment = lax.optimization_barrier(jnp.sum((indices[:, None] >= seg_ends[None, :]).astype(jnp.int32), axis=1)).astype(jnp.int32)
    member = segment[:, None] == jnp.arange(prompt_lens.shape[0], dtype=jnp.int32)[None, :]
    opening = lax.optimization_barrier(jnp.sum(jnp.where(member, starts[None, :], 0), axis=1)).astype(jnp.int32)
    return (segment, (indices - opening).astype(jnp.int32))

def rotary(head_values, position, head_size):
    half_size = head_size // 2
    frequency = jnp.exp(jnp.arange(half_size, dtype=jnp.float32) * (-2.0 * math.log(ROPE_BASE) / head_size))
    angles = position.astype(jnp.float32)[:, None] * frequency[None, :]
    cosines = jnp.cos(angles)
    sines = jnp.sin(angles)
    front_half = head_values[..., :half_size]
    back_half = head_values[..., half_size:]
    return jnp.concatenate([front_half * cosines - back_half * sines, back_half * cosines + front_half * sines], axis=-1)

def head_attention(queries, keys_rot, values_h, segment, head_size):
    scores = lax.dot_general(queries, keys_rot, (((1,), (1,)), ((), ())), preferred_element_type=jnp.float32)
    scores = scores * (1.0 / math.sqrt(head_size))
    indices = jnp.arange(queries.shape[0], dtype=jnp.int32)
    allowed = (segment[:, None] == segment[None, :]) & (indices[None, :] <= indices[:, None])
    scores = jnp.where(allowed, scores, -1e+30)
    row_max = lax.optimization_barrier(jnp.max(scores, axis=1, keepdims=True))
    weights = jnp.exp(scores - row_max)
    weights = weights / lax.optimization_barrier(jnp.sum(weights, axis=1, keepdims=True))
    probabilities = weights.astype(jnp.bfloat16)
    return jnp.dot(probabilities, values_h, preferred_element_type=jnp.float32).astype(jnp.bfloat16)

def rms_scale(values_in, gain):
    return values_in * lax.rsqrt(lax.optimization_barrier(jnp.mean(values_in * values_in, axis=-1, keepdims=True)) + NORM_EPSILON) * gain

def reference(tokens, lengths, query_gain, key_gain, attn_post_gain, mlp_post_gain, query_weight, key_weight, value_weight, output_weight, gate_weight, up_weight, down_weight):
    query_server = query_weight.astype(jnp.bfloat16)
    key_server = key_weight.astype(jnp.bfloat16)
    value_server = value_weight.astype(jnp.bfloat16)
    output_server = output_weight.astype(jnp.bfloat16)
    gate_server = gate_weight.astype(jnp.bfloat16)
    up_server = up_weight.astype(jnp.bfloat16)
    down_server = down_weight.astype(jnp.bfloat16)

    def heads_first(flat):
        return flat.reshape(TOK_GRP, HEADS, HEAD_DIM).transpose(1, 0, 2)

    def one_group(inputs):
        group_x, prompt_lens = inputs
        segment, position = token_layout(prompt_lens, TOK_GRP)
        q_raw = jnp.dot(group_x, query_server, preferred_element_type=jnp.float32)
        k_raw = jnp.dot(group_x, key_server, preferred_element_type=jnp.float32)
        v_raw = jnp.dot(group_x, value_server, preferred_element_type=jnp.float32)
        q_normed = rms_scale(q_raw, query_gain)
        k_normed = rms_scale(k_raw, key_gain)
        queries = rotary(heads_first(q_normed), position, HEAD_DIM).astype(jnp.bfloat16)
        keys_rot = rotary(heads_first(k_normed), position, HEAD_DIM).astype(jnp.bfloat16)
        values_h = heads_first(v_raw.astype(jnp.bfloat16))

        def per_head(triple):
            return head_attention(triple[0], triple[1], triple[2], segment, HEAD_DIM)
        attended = lax.map(per_head, (queries, keys_rot, values_h))
        attended = attended.transpose(1, 0, 2).reshape(TOK_GRP, D)
        attn_out = jnp.dot(attended, output_server, preferred_element_type=jnp.float32)
        hidden = (group_x.astype(jnp.float32) + rms_scale(attn_out, attn_post_gain)).astype(jnp.bfloat16)
        gate_proj = jnp.dot(hidden, gate_server, preferred_element_type=jnp.float32)
        up_proj = jnp.dot(hidden, up_server, preferred_element_type=jnp.float32)
        activated = (jax.nn.silu(gate_proj) * up_proj).astype(jnp.bfloat16)
        mlp_out = jnp.dot(activated, down_server, preferred_element_type=jnp.float32)
        return (hidden.astype(jnp.float32) + rms_scale(mlp_out, mlp_post_gain)).astype(jnp.bfloat16)
    result = lax.map(one_group, (tokens.reshape(N_GROUP, TOK_GRP, D), lengths))
    return result.reshape(TOKENS, D)
```

```python
import math

import jax
import jax.numpy as jnp
from jax import lax
from jax.sharding import Mesh, PartitionSpec as P

HEAD_DIM = 128
NORM_EPSILON = 1e-06
ROPE_BASE = 500000.0
PLANE = ("z", "x")
COLUMN = ("yhi", "ylo", "core")


def segments(prompt_lens, rows):
    seg_ends = jnp.cumsum(prompt_lens)
    starts = seg_ends - prompt_lens
    segment = jnp.sum((rows[:, None] >= seg_ends[None, :]).astype(jnp.int32), axis=1)
    member = segment[:, None] == jnp.arange(prompt_lens.shape[0], dtype=jnp.int32)[None, :]
    opening = jnp.sum(jnp.where(member, starts[None, :], 0), axis=1)
    return segment, rows - opening


def rotary(values_in, cosines, sines):
    half = HEAD_DIM // 2
    front, back = values_in[:, :half], values_in[:, half:]
    return jnp.concatenate(
        [front * cosines - back * sines, back * cosines + front * sines], axis=-1
    )


def rms_scale(values_in, gain):
    return (
        values_in
        * lax.rsqrt(jnp.mean(values_in * values_in, axis=-1, keepdims=True) + NORM_EPSILON)
        * gain
    )


def sum_scatter(partial, tok_rows):
    blocks = partial.astype(jnp.bfloat16).reshape(-1, tok_rows, partial.shape[1])
    got = lax.all_to_all(blocks, PLANE, split_axis=0, concat_axis=0, tiled=True)
    return jnp.sum(got.astype(jnp.float32), axis=0)


def column_blocks(weights, parts):
    rows = weights[0].shape[0]
    split = [w.astype(jnp.bfloat16).reshape(rows, parts, -1) for w in weights]
    blocks = jnp.concatenate(split, axis=2).transpose(1, 0, 2)
    got = lax.all_to_all(blocks, PLANE, split_axis=0, concat_axis=0, tiled=True)
    whole = lax.all_gather(got, COLUMN, axis=1, tiled=True)
    return whole.reshape(-1, whole.shape[2])


def row_blocks(weight):
    return lax.all_gather(weight.astype(jnp.bfloat16), COLUMN, axis=0, tiled=True)


def per_device(
    tokens,
    lengths,
    query_gain,
    key_gain,
    attn_post_gain,
    mlp_post_gain,
    query_weight,
    key_weight,
    value_weight,
    output_weight,
    gate_weight,
    up_weight,
    down_weight,
):
    features = tokens.shape[1]
    parts = lax.axis_size("z") * lax.axis_size("x")
    place = lax.axis_index("z") * lax.axis_size("x") + lax.axis_index("x")
    half = lax.axis_index("yhi")
    tok_rows = tokens.shape[0]
    set_rows = tok_rows * parts
    qkv = column_blocks([query_weight, key_weight, value_weight], parts)
    output_block = row_blocks(output_weight)
    mlp_weights = column_blocks([gate_weight, up_weight], parts)
    down_block = row_blocks(down_weight)
    gathered = lax.all_gather(tokens, PLANE, axis=0, tiled=True)
    projected = jnp.dot(gathered, qkv, preferred_element_type=jnp.float32)
    q_raw, k_raw, v_raw = jnp.split(projected, 3, axis=1)
    squares = jnp.stack([jnp.sum(q_raw * q_raw, axis=1), jnp.sum(k_raw * k_raw, axis=1)])
    totals = jnp.sum(lax.all_gather(squares, PLANE, axis=0, tiled=False), axis=0)
    q_part = lax.dynamic_slice_in_dim(query_gain, place * HEAD_DIM, HEAD_DIM)
    k_part = lax.dynamic_slice_in_dim(key_gain, place * HEAD_DIM, HEAD_DIM)
    q_normed = q_raw * lax.rsqrt(totals[0] / features + NORM_EPSILON)[:, None] * q_part
    k_normed = k_raw * lax.rsqrt(totals[1] / features + NORM_EPSILON)[:, None] * k_part
    index = jnp.arange(set_rows, dtype=jnp.int32)

    def rows_of(which):
        return (index // tok_rows * 2 + which) * tok_rows + index % tok_rows

    my_rows = rows_of(half)
    segment, position = segments(lengths[0], my_rows)
    frequency = jnp.exp(
        jnp.arange(HEAD_DIM // 2, dtype=jnp.float32) * (-2.0 * math.log(ROPE_BASE) / HEAD_DIM)
    )
    angles = position.astype(jnp.float32)[:, None] * frequency[None, :]
    cosines, sines = jnp.cos(angles), jnp.sin(angles)
    queries = rotary(q_normed, cosines, sines).astype(jnp.bfloat16)
    keys_rot = rotary(k_normed, cosines, sines).astype(jnp.bfloat16)
    kv_mine = jnp.concatenate([keys_rot, v_raw.astype(jnp.bfloat16)], axis=1)
    kv_other = lax.ppermute(kv_mine, "yhi", [(0, 1), (1, 0)])
    kv = jnp.concatenate([kv_mine, kv_other], axis=0)
    key_rows = jnp.concatenate([my_rows, rows_of(1 - half)])
    key_segment, _ = segments(lengths[0], key_rows)
    scores = lax.dot_general(
        queries, kv[:, :HEAD_DIM], (((1,), (1,)), ((), ())), preferred_element_type=jnp.float32
    ) * (1.0 / math.sqrt(HEAD_DIM))
    allowed = (segment[:, None] == key_segment[None, :]) & (key_rows[None, :] <= my_rows[:, None])
    scores = jnp.where(allowed, scores, -1e30)
    weights = jnp.exp(scores - jnp.max(scores, axis=1, keepdims=True))
    weights = weights / jnp.sum(weights, axis=1, keepdims=True)
    attended = jnp.dot(
        weights.astype(jnp.bfloat16), kv[:, HEAD_DIM:], preferred_element_type=jnp.float32
    ).astype(jnp.bfloat16)
    attn_out = sum_scatter(
        jnp.dot(attended, output_block, preferred_element_type=jnp.float32), tok_rows
    )
    hidden = (tokens.astype(jnp.float32) + rms_scale(attn_out, attn_post_gain)).astype(jnp.bfloat16)
    both_proj = jnp.dot(
        lax.all_gather(hidden, PLANE, axis=0, tiled=True),
        mlp_weights,
        preferred_element_type=jnp.float32,
    )
    width = both_proj.shape[1] // 2
    activated = (jax.nn.silu(both_proj[:, :width]) * both_proj[:, width:]).astype(jnp.bfloat16)
    mlp_out = sum_scatter(
        jnp.dot(activated, down_block, preferred_element_type=jnp.float32), tok_rows
    )
    return (hidden.astype(jnp.float32) + rms_scale(mlp_out, mlp_post_gain)).astype(jnp.bfloat16)


def solution(mesh):
    fine = Mesh(mesh.devices.reshape(2, 2, 4, 4, 2), ("ylo", "core", "z", "x", "yhi"))
    tok = P(("ylo", "core", "z", "x", "yhi"), None)
    weight = P(("z", "x", "yhi", "ylo", "core"), None)
    return jax.shard_map(
        per_device,
        mesh=fine,
        in_specs=(tok, P(("ylo", "core"), None), P(), P(), P(), P()) + (weight,) * 7,
        out_specs=tok,
        check_vma=False,
    )
```

```python
import math

import jax
import jax.numpy as jnp
from jax import lax
from jax.experimental import pallas as pl
from jax.experimental.pallas import tpu as pltpu
from jax.sharding import Mesh, PartitionSpec as P

HEAD_DIM = 128
NORM_EPSILON = 1e-06
ROPE_BASE = 500000.0
SIDE = 4
PLANE = SIDE * SIDE
COLUMN = 8
MESH = pl.DeviceIdType.MESH
F32 = jnp.float32
BF16 = jnp.bfloat16
HIGHEST = lax.Precision.HIGHEST


def remote(src, dst, send_sem, recv_sem, device):
    return pltpu.make_async_remote_copy(
        src_ref=src,
        dst_ref=dst,
        send_sem=send_sem,
        recv_sem=recv_sem,
        device_id=device,
        device_id_type=MESH,
    )


def plane_device(place):
    return {"z": place // SIDE, "x": lax.rem(place, SIDE)}


def dot(a, b):
    return jnp.dot(a, b, preferred_element_type=F32)


def kernel(
    lengths,
    tokens,
    query_gain,
    key_gain,
    attn_gain,
    mlp_gain,
    query_w,
    key_w,
    value_w,
    output_w,
    gate_w,
    up_w,
    down_w,
    out,
    stage_qkv,
    stage_mlp,
    qkv_all,
    mlp_all,
    out_all,
    down_all,
    tok_all,
    x_rows,
    proj,
    sq_all,
    kv,
    queries,
    cosines,
    sines,
    opening,
    part_a,
    got_a,
    hid_all,
    part_b,
    got_b,
    act,
    total,
    s_qkv,
    r_qkv,
    s_tok,
    r_tok,
    s_mlp,
    r_mlp,
    s_sq,
    r_sq,
    s_pa,
    r_pa,
    s_hid,
    r_hid,
    s_pb,
    r_pb,
    c_send,
    c_recv,
    s_kv,
    r_kv,
):
    z, x = lax.axis_index("z"), lax.axis_index("x")
    yhi, ylo, core = lax.axis_index("yhi"), lax.axis_index("ylo"), lax.axis_index("core")
    me = z * SIDE + x
    y = yhi * 2 + ylo
    slot = y * 2 + core
    rows = tokens.shape[0]
    set_rows = rows * PLANE
    group_rows = rows * SIDE
    features = tokens.shape[1]
    hidden_width = act.shape[1]

    def y_peer(step):
        other = lax.rem(y + step, SIDE)
        return other, {"yhi": other // 2, "ylo": lax.rem(other, 2)}

    sibling = {"core": 1 - core}

    barrier = pltpu.get_barrier_semaphore()

    @pl.loop(1, PLANE)
    def _(i):
        pl.semaphore_signal(
            barrier, inc=1, device_id=plane_device(lax.rem(me + i, PLANE)), device_id_type=MESH
        )

    @pl.loop(1, SIDE)
    def _(i):
        pl.semaphore_signal(barrier, inc=1, device_id=y_peer(i)[1], device_id_type=MESH)

    pl.semaphore_signal(barrier, inc=1, device_id=sibling, device_id_type=MESH)

    for p in range(PLANE):
        cols = slice(p * HEAD_DIM, (p + 1) * HEAD_DIM)
        for k, w in enumerate((query_w, key_w, value_w)):
            stage_qkv[p, :, k * HEAD_DIM : (k + 1) * HEAD_DIM] = w[:, cols].astype(BF16)
    pl.semaphore_wait(barrier, PLANE - 1 + SIDE)

    def plane_copy(i, src, dst, send, recv):
        peer = lax.rem(me + i, PLANE)
        return remote(src(peer), dst(me), send.at[i], recv.at[me], plane_device(peer))

    def plane_start(src, dst, send, recv):
        @pl.loop(1, PLANE)
        def _(i):
            plane_copy(i, src, dst, send, recv).start()

    def plane_wait_send(src, dst, send, recv):
        @pl.loop(1, PLANE)
        def _(i):
            plane_copy(i, src, dst, send, recv).wait_send()

    def wait_from(peer, dst, send, recv):
        remote(dst(peer), dst(peer), send.at[0], recv.at[peer], plane_device(peer)).wait_recv()

    def plane_wait_recv(dst, send, recv):
        @pl.loop(1, PLANE)
        def _(i):
            wait_from(lax.rem(me + PLANE - i, PLANE), dst, send, recv)

    qkv_move = (lambda p: stage_qkv.at[p], lambda p: qkv_all.at[p, slot], s_qkv, r_qkv)
    plane_start(*qkv_move)
    tok_move = (lambda p: tokens, lambda p: tok_all.at[p], s_tok, r_tok)
    plane_start(*tok_move)
    qkv_all[me, slot] = stage_qkv[me]
    tok_all[me] = tokens[...]

    for p in range(PLANE):
        cols = slice(p * hidden_width, (p + 1) * hidden_width)
        for k, w in enumerate((gate_w, up_w)):
            stage_mlp[p, :, k * hidden_width : (k + 1) * hidden_width] = w[:, cols].astype(BF16)
    mlp_move = (lambda p: stage_mlp.at[p], lambda p: mlp_all.at[p, slot], s_mlp, r_mlp)
    plane_start(*mlp_move)
    mlp_all[me, slot] = stage_mlp[me]
    out_all[slot] = output_w[...].astype(BF16)
    down_all[slot] = down_w[...].astype(BF16)

    def column_y(kind, view, i):
        other, device = y_peer(i)
        return remote(view(slot), view(slot), c_send.at[kind, i], c_recv.at[kind, slot], device)

    def column_core(kind, view, i):
        held = y_peer(i)[0] * 2 + core
        return remote(
            view(held), view(held), c_send.at[kind, SIDE + i], c_recv.at[kind, held], sibling
        )

    def column_start(kind, view):
        @pl.loop(1, SIDE)
        def _(i):
            column_y(kind, view, i).start()

        column_core(kind, view, 0).start()

    def column_wait(kind, view, held):
        remote(
            view(held), view(held), c_send.at[kind, 0], c_recv.at[kind, held], sibling
        ).wait_recv()

    def column_pass(kind, view):
        @pl.loop(1, SIDE)
        def _(i):
            column_wait(kind, view, y_peer(i)[0] * 2 + core)
            column_core(kind, view, i).start()

    def column_finish(kind, view):
        @pl.loop(0, SIDE)
        def _(i):
            column_wait(kind, view, y_peer(i)[0] * 2 + 1 - core)

    def column_wait_send(kind, view):
        @pl.loop(1, SIDE)
        def _(i):
            column_y(kind, view, i).wait_send()

        @pl.loop(0, SIDE)
        def _(i):
            column_core(kind, view, i).wait_send()

    column = (
        (0, lambda q: qkv_all.at[:, q]),
        (1, lambda q: out_all.at[q]),
        (2, lambda q: mlp_all.at[:, q]),
        (3, lambda q: down_all.at[q]),
    )
    plane_wait_recv(*qkv_move[1:])
    column_start(*column[0])
    column_start(*column[1])

    def numbered(index, which):
        return index + ((index * 1639) >> 16) * rows + which * rows

    flat = lax.broadcasted_iota(jnp.int32, (set_rows, HEAD_DIM), 0)
    row = numbered(flat, yhi)
    start = jnp.zeros_like(row)
    end = jnp.int32(0)
    for r in range(lengths.shape[1]):
        end = end + lengths[0, r]
        start = start + jnp.where(row >= end, lengths[0, r], 0)
    opening[...] = start
    lane = lax.broadcasted_iota(jnp.int32, (1, HEAD_DIM), 1)
    half = HEAD_DIM // 2
    step = jnp.where(lane < half, lane, lane - half).astype(F32)
    frequency = jnp.exp(step * (-2.0 * math.log(ROPE_BASE) / HEAD_DIM))
    angle = (row - start).astype(F32) * frequency
    cosines[...] = jnp.cos(angle)
    sines[...] = jnp.sin(angle) * jnp.where(lane < half, -1.0, 1.0)

    column_pass(*column[0])
    plane_wait_recv(*mlp_move[1:])
    column_start(*column[2])
    column_start(*column[3])

    plane_wait_recv(*tok_move[1:])

    def pair(ref, first):
        return jnp.concatenate([ref[first].astype(F32), ref[first + 1].astype(F32)], axis=0).astype(
            BF16
        )

    @pl.loop(0, PLANE // 2)
    def _(j):
        x_rows[pl.ds(pl.multiple_of(j * 2 * rows, 2 * rows), 2 * rows), :] = pair(tok_all, 2 * j)

    column_finish(*column[0])

    def chunk(i):
        return pl.ds(pl.multiple_of(i * group_rows, group_rows), group_rows)

    @pl.loop(0, SIDE)
    def _(i):
        proj[chunk(i), :] = dot(x_rows[chunk(i), :], qkv_all[...].reshape(features, 3 * HEAD_DIM))

    both = proj[:, : 2 * HEAD_DIM]
    pick = (
        lax.broadcasted_iota(jnp.int32, (8, 2 * HEAD_DIM), 1) // HEAD_DIM
        == lax.broadcasted_iota(jnp.int32, (8, 2 * HEAD_DIM), 0)
    ).astype(F32)
    sq_all[me] = lax.dot_general(
        pick, both * both, (((1,), (1,)), ((), ())), precision=HIGHEST, preferred_element_type=F32
    )
    sq_move = (lambda p: sq_all.at[me], lambda p: sq_all.at[p], s_sq, r_sq)
    plane_start(*sq_move)
    kv[0, :, HEAD_DIM:] = proj[:, 2 * HEAD_DIM :].astype(BF16)
    plane_wait_recv(*sq_move[1:])
    sums = sq_all[0]
    for p in range(1, PLANE):
        sums = sums + sq_all[p]
    scale = jnp.transpose(lax.rsqrt(sums / features + NORM_EPSILON))

    def rotated(values_in, column_scale, gain):
        normed = values_in * column_scale * gain
        return normed * cosines[...] + pltpu.roll(normed, half, 1) * sines[...]

    kv[0, :, :HEAD_DIM] = rotated(
        proj[:, HEAD_DIM : 2 * HEAD_DIM], scale[:, 1:2], key_gain[...]
    ).astype(BF16)
    kv_copy = remote(kv.at[0], kv.at[1], s_kv, r_kv, {"yhi": 1 - yhi})
    kv_copy.start()
    queries[...] = rotated(proj[:, :HEAD_DIM], scale[:, 0:1], query_gain[...]).astype(BF16)
    column_pass(*column[1])
    column_finish(*column[1])
    kv_copy.wait_recv()

    lane_index = lax.broadcasted_iota(jnp.int32, (1, set_rows), 1)
    pa_move = (lambda p: part_a.at[p], lambda p: got_a.at[p], s_pa, r_pa)
    pb_move = (lambda p: part_b.at[p], lambda p: got_b.at[p], s_pb, r_pb)

    def send_group(group, part, got, send, recv):
        @pl.loop(0, SIDE)
        def _(b):
            peer = group * SIDE + lax.rem(x + b, SIDE)

            @pl.when(peer != me)
            def _():
                remote(
                    part.at[peer],
                    got.at[me],
                    send.at[lax.rem(peer - me + PLANE, PLANE)],
                    recv.at[me],
                    plane_device(peer),
                ).start()

    @pl.loop(1, SIDE + 1)
    def _(i):
        group = lax.rem(z + i, SIDE)
        here = chunk(group)
        key_row = jnp.concatenate([numbered(lane_index, yhi), numbered(lane_index, 1 - yhi)], axis=1)
        own = lax.broadcasted_iota(jnp.int32, (group_rows, 1), 0) + group * group_rows
        own_row = numbered(own, yhi)
        first = opening[here, :][:, 0:1]
        scores = lax.dot_general(
            queries[here, :],
            kv[:, :, :HEAD_DIM].reshape(2 * set_rows, HEAD_DIM),
            (((1,), (1,)), ((), ())),
            preferred_element_type=F32,
        ) * (1.0 / math.sqrt(HEAD_DIM))
        scores = jnp.where((key_row >= first) & (key_row <= own_row), scores, -1e30)
        weights = jnp.exp(scores - jnp.max(scores, axis=1, keepdims=True))
        weights = weights / jnp.sum(weights, axis=1, keepdims=True)
        attended = dot(
            weights.astype(BF16), kv[:, :, HEAD_DIM:].reshape(2 * set_rows, HEAD_DIM)
        ).astype(BF16)
        summed = dot(attended, out_all[...].reshape(HEAD_DIM, features))
        for b in range(SIDE):
            part_a[group * SIDE + b] = summed[b * rows : (b + 1) * rows].astype(BF16)
        send_group(group, part_a, got_a, s_pa, r_pa)

    got_a[me] = part_a[me]
    column_pass(*column[2])
    column_pass(*column[3])
    plane_wait_recv(*pa_move[1:])

    def summed_norm(got, gain):
        width = features // 4
        for c in range(4):
            cols = slice(c * width, (c + 1) * width)
            acc = got[0, :, cols].astype(F32)
            for p in range(1, PLANE):
                acc = acc + got[p, :, cols].astype(F32)
            total[:, cols] = acc
        values_in = total[...]
        mean = jnp.mean(values_in * values_in, axis=-1, keepdims=True)
        return values_in * lax.rsqrt(mean + NORM_EPSILON) * gain[...]

    hid_all[me] = (tokens[...].astype(F32) + summed_norm(got_a, attn_gain)).astype(BF16)
    hid_move = (lambda p: hid_all.at[me], lambda p: hid_all.at[p], s_hid, r_hid)
    plane_start(*hid_move)
    column_finish(*column[2])
    column_finish(*column[3])

    @pl.loop(0, SIDE)
    def _(i):
        group = lax.rem(z + i, SIDE)

        @pl.loop(0, SIDE)
        def _(b):
            peer = group * SIDE + b

            @pl.when(peer != me)
            def _():
                wait_from(peer, *hid_move[1:])

        values_in = jnp.concatenate(
            [pair(hid_all, group * SIDE), pair(hid_all, group * SIDE + 2)], axis=0
        )
        tile = 256
        for c in range(hidden_width // tile):
            lo = c * tile
            gate = dot(values_in, mlp_all[:, :, :, lo : lo + tile].reshape(features, tile))
            lo = lo + hidden_width
            up = dot(values_in, mlp_all[:, :, :, lo : lo + tile].reshape(features, tile))
            act[:, c * tile : (c + 1) * tile] = (gate / (1.0 + jnp.exp(-gate)) * up).astype(BF16)
        wide = 512
        for c in range(features // wide):
            cols = slice(c * wide, (c + 1) * wide)
            summed = dot(act[...], down_all[:, :, cols].reshape(hidden_width, wide))
            for b in range(SIDE):
                part_b[group * SIDE + b, :, cols] = summed[b * rows : (b + 1) * rows].astype(BF16)
        send_group(group, part_b, got_b, s_pb, r_pb)

    got_b[me] = part_b[me]
    plane_wait_recv(*pb_move[1:])
    out[...] = (hid_all[me].astype(F32) + summed_norm(got_b, mlp_gain)).astype(BF16)

    for move in (qkv_move, tok_move, mlp_move, sq_move, pa_move, hid_move, pb_move):
        plane_wait_send(*move)
    for kind, view in column:
        column_wait_send(kind, view)
    kv_copy.wait_send()


def per_device(tokens, lengths, query_gain, key_gain, attn_gain, mlp_gain, *weights):
    place = lax.axis_index("z") * SIDE + lax.axis_index("x")
    q_part = lax.dynamic_slice_in_dim(query_gain, place * HEAD_DIM, HEAD_DIM)[None]
    k_part = lax.dynamic_slice_in_dim(key_gain, place * HEAD_DIM, HEAD_DIM)[None]
    rows, features = tokens.shape
    depth = weights[0].shape[0]
    ff = weights[4].shape[1] // PLANE
    down_depth = weights[6].shape[0]
    set_rows = rows * PLANE
    vmem = pl.BlockSpec(memory_space=pltpu.VMEM)
    dma = pltpu.SemaphoreType.DMA
    blocks = (PLANE, rows, features)
    return pl.pallas_call(
        kernel,
        out_shape=jax.ShapeDtypeStruct(tokens.shape, BF16),
        in_specs=[pl.BlockSpec(memory_space=pltpu.SMEM)] + [vmem] * 12,
        out_specs=vmem,
        scratch_shapes=[
            pltpu.VMEM((PLANE, depth, 3 * HEAD_DIM), BF16),
            pltpu.VMEM((PLANE, depth, 2 * ff), BF16),
            pltpu.VMEM((PLANE, COLUMN, depth, 3 * HEAD_DIM), BF16),
            pltpu.VMEM((PLANE, COLUMN, depth, 2 * ff), BF16),
            pltpu.VMEM((COLUMN, depth, features), BF16),
            pltpu.VMEM((COLUMN, down_depth, features), BF16),
            pltpu.VMEM(blocks, BF16),
            pltpu.VMEM((set_rows, features), BF16),
            pltpu.VMEM((set_rows, 3 * HEAD_DIM), F32),
            pltpu.VMEM((PLANE, 8, set_rows), F32),
            pltpu.VMEM((2, set_rows, 2 * HEAD_DIM), BF16),
            pltpu.VMEM((set_rows, HEAD_DIM), BF16),
            pltpu.VMEM((set_rows, HEAD_DIM), F32),
            pltpu.VMEM((set_rows, HEAD_DIM), F32),
            pltpu.VMEM((set_rows, HEAD_DIM), jnp.int32),
            pltpu.VMEM(blocks, BF16),
            pltpu.VMEM(blocks, BF16),
            pltpu.VMEM(blocks, BF16),
            pltpu.VMEM(blocks, BF16),
            pltpu.VMEM(blocks, BF16),
            pltpu.VMEM((rows * SIDE, ff), BF16),
            pltpu.VMEM((rows, features), F32),
        ]
        + [dma((PLANE,))] * 14
        + [dma((4, COLUMN)), dma((4, COLUMN)), dma(()), dma(())],
        compiler_params=pltpu.CompilerParams(
            collective_id=0, has_side_effects=True, vmem_limit_bytes=60 << 20
        ),
    )(lengths, tokens, q_part, k_part, attn_gain[None], mlp_gain[None], *weights)


def solution(mesh):
    fine = Mesh(mesh.devices.reshape(2, 2, 4, 4, 2), ("ylo", "core", "z", "x", "yhi"))
    tok = P(("ylo", "core", "z", "x", "yhi"), None)
    weight = P(("z", "x", "yhi", "ylo", "core"), None)
    return jax.shard_map(
        per_device,
        mesh=fine,
        in_specs=(tok, P(("ylo", "core"), None), P(), P(), P(), P()) + (weight,) * 7,
        out_specs=tok,
        check_vma=False,
    )
```

```python
import math

import jax
import jax.numpy as jnp
from jax import lax
from jax.experimental import pallas as pl
from jax.experimental.pallas import tpu as pltpu
from jax.sharding import Mesh, PartitionSpec as P

HEAD_DIM = 128
NORM_EPSILON = 1e-06
ROPE_BASE = 500000.0
SIDE = 4
PLANE = SIDE * SIDE
COLUMN = 8
MESH = pl.DeviceIdType.MESH
F32 = jnp.float32
BF16 = jnp.bfloat16
HIGHEST = lax.Precision.HIGHEST


def remote(src, dst, send_sem, recv_sem, device):
    return pltpu.make_async_remote_copy(
        src_ref=src,
        dst_ref=dst,
        send_sem=send_sem,
        recv_sem=recv_sem,
        device_id=device,
        device_id_type=MESH,
    )


def plane_device(place):
    return {"z": place // SIDE, "x": lax.rem(place, SIDE)}


def dot(a, b):
    return jnp.dot(a, b, preferred_element_type=F32)


def kernel(
    lengths,
    tokens,
    query_gain,
    key_gain,
    attn_gain,
    mlp_gain,
    query_w,
    key_w,
    value_w,
    output_w,
    gate_w,
    up_w,
    down_w,
    out,
    stage_qkv,
    stage_mlp,
    qkv_all,
    mlp_all,
    out_all,
    down_all,
    tok_all,
    hid_all,
    proj,
    sq_all,
    scales,
    kv,
    queries,
    cosines,
    sines,
    opening,
    part_a,
    part_b,
    got_a,
    got_b,
    pass_a,
    pass_b,
    last_a,
    last_b,
    act,
    total,
    s_qkv,
    r_qkv,
    s_mlp,
    r_mlp,
    s_sq,
    r_sq,
    s_tok,
    r_tok,
    s_hid,
    r_hid,
    s_one_a,
    r_one_a,
    s_two_a,
    r_two_a,
    s_one_b,
    r_one_b,
    s_two_b,
    r_two_b,
    c_send,
    c_recv,
    s_kv,
    r_kv,
):
    z, x = lax.axis_index("z"), lax.axis_index("x")
    yhi, ylo, core = lax.axis_index("yhi"), lax.axis_index("ylo"), lax.axis_index("core")
    me = z * SIDE + x
    y = yhi * 2 + ylo
    slot = y * 2 + core
    rows = tokens.shape[0]
    set_rows = rows * PLANE
    group_rows = rows * SIDE
    features = tokens.shape[1]
    wide = features // 2
    hidden_width = act.shape[1]

    def y_peer(step):
        other = lax.rem(y + step, SIDE)
        return other, {"yhi": other // 2, "ylo": lax.rem(other, 2)}

    sibling = {"core": 1 - core}
    partner = {"yhi": 1 - yhi}

    barrier = pltpu.get_barrier_semaphore()

    @pl.loop(1, PLANE)
    def _(i):
        pl.semaphore_signal(
            barrier, inc=1, device_id=plane_device(lax.rem(me + i, PLANE)), device_id_type=MESH
        )

    @pl.loop(1, SIDE)
    def _(i):
        pl.semaphore_signal(barrier, inc=1, device_id=y_peer(i)[1], device_id_type=MESH)

    pl.semaphore_signal(barrier, inc=1, device_id=sibling, device_id_type=MESH)

    for p in range(PLANE):
        cols = slice(p * HEAD_DIM, (p + 1) * HEAD_DIM)
        for k, w in enumerate((query_w, key_w, value_w)):
            stage_qkv[p, :, k * HEAD_DIM : (k + 1) * HEAD_DIM] = w[:, cols].astype(BF16)
    for h in range(2):
        tok_all[h, me] = tokens[:, h * wide : (h + 1) * wide]
    pl.semaphore_wait(barrier, PLANE - 1 + SIDE)

    def plane_copy(i, src, dst, send, recv):
        peer = lax.rem(me + i, PLANE)
        return remote(src(peer), dst(me), send.at[i], recv.at[me], plane_device(peer))

    def plane_start(src, dst, send, recv):
        @pl.loop(1, PLANE)
        def _(i):
            plane_copy(i, src, dst, send, recv).start()

    def plane_wait_send(src, dst, send, recv):
        @pl.loop(1, PLANE)
        def _(i):
            plane_copy(i, src, dst, send, recv).wait_send()

    def plane_wait_recv(dst, send, recv):
        @pl.loop(1, PLANE)
        def _(i):
            peer = lax.rem(me + PLANE - i, PLANE)
            remote(dst(peer), dst(peer), send.at[0], recv.at[peer], plane_device(peer)).wait_recv()

    def along(h, order, i):
        if h == order:
            return z * SIDE + lax.rem(x + i, SIDE)
        return lax.rem(z + i, SIDE) * SIDE + x

    def gather_copy(ref, send, recv, h, order, j, i):
        held = along(h, 0, SIDE - j) if order == 1 else me
        return remote(
            ref.at[h, held],
            ref.at[h, held],
            send.at[h, order, j, i],
            recv.at[h, held],
            plane_device(along(h, order, i)),
        )

    def gather_wait(ref, send, recv, h, held):
        remote(
            ref.at[h, held], ref.at[h, held], send.at[0, 0, 0, 0], recv.at[h, held], sibling
        ).wait_recv()

    def gather_start(ref, send, recv):
        for order in range(2):

            @pl.loop(1, SIDE)
            def _(i):
                for h in range(2):
                    gather_copy(ref, send, recv, h, order, 0, i).start()

    def gather_relay(ref, send, recv):
        @pl.loop(1, SIDE)
        def _(j):
            for h in range(2):
                gather_wait(ref, send, recv, h, along(h, 0, SIDE - j))

                @pl.loop(1, SIDE)
                def _(i):
                    gather_copy(ref, send, recv, h, 1, j, i).start()

    def gather_wait_group(ref, send, recv, group):
        @pl.when(group != z)
        def _():
            @pl.loop(0, SIDE)
            def _(b):
                gather_wait(ref, send, recv, 0, group * SIDE + b)

        @pl.loop(1, SIDE)
        def _(i):
            gather_wait(ref, send, recv, 1, group * SIDE + lax.rem(x + i, SIDE))

    def gather_wait_send(ref, send, recv):
        @pl.loop(1, SIDE)
        def _(i):
            for h in range(2):
                gather_copy(ref, send, recv, h, 0, 0, i).wait_send()

                @pl.loop(0, SIDE)
                def _(j):
                    gather_copy(ref, send, recv, h, 1, j, i).wait_send()

    def gathered(ref, group):
        halves = []
        for h in range(2):
            blocks = [ref[h, group * SIDE + b].astype(F32) for b in range(SIDE)]
            halves.append(jnp.concatenate(blocks, axis=0).astype(BF16))
        return jnp.concatenate(halves, axis=1)

    def sum_first(group, part, got, send, recv):
        def tall():
            return remote(
                part.at[0, pl.ds(group * SIDE, SIDE)],
                got.at[0, z],
                send.at[0, 0, group],
                recv.at[0, 0, z],
                {"z": group},
            )

        def flat(i):
            other = lax.rem(x + i, SIDE)
            return remote(
                part.at[1, group * SIDE + other],
                got.at[1, x, group],
                send.at[1, i, group],
                recv.at[1, x, group],
                {"x": other},
            )

        return tall, flat

    def sum_start(group, move):
        tall, flat = sum_first(group, *move)

        @pl.when(group != z)
        def _():
            tall().start()

        @pl.loop(1, SIDE)
        def _(i):
            flat(i).start()

    def sum_wait_send(move):
        @pl.loop(1, SIDE)
        def _(i):
            sum_first(lax.rem(z + i, SIDE), *move)[0]().wait_send()

        @pl.loop(0, SIDE)
        def _(group):
            @pl.loop(1, SIDE)
            def _(i):
                sum_first(group, *move)[1](i).wait_send()

    def second_copy(h, i, passed, last, send, recv):
        own = x if h == 0 else z
        other = lax.rem(own + i, SIDE)
        return remote(
            passed.at[h, other],
            last.at[h, own],
            send.at[h, i],
            recv.at[h, own],
            {"x": other} if h == 0 else {"z": other},
        )

    def sum_finish(move, second):
        part, got, send, recv = move
        passed, last, send_two, recv_two = second

        @pl.loop(1, SIDE)
        def _(i):
            other = lax.rem(z + i, SIDE)
            remote(
                got.at[0, other], got.at[0, other], send.at[0, 0, 0], recv.at[0, 0, other], sibling
            ).wait_recv()

        @pl.loop(1, SIDE + 1)
        def _(i):
            other = lax.rem(x + i, SIDE)
            acc = part[0, z * SIDE + other].astype(F32)
            for j in range(1, SIDE):
                acc = acc + got[0, lax.rem(z + j, SIDE), other].astype(F32)
            passed[0, other] = acc.astype(BF16)

            @pl.when(i < SIDE)
            def _():
                second_copy(0, i, *second).start()

        @pl.loop(1, SIDE + 1)
        def _(i):
            other = lax.rem(z + i, SIDE)

            @pl.loop(1, SIDE)
            def _(j):
                source = lax.rem(x + j, SIDE)
                remote(
                    got.at[1, source, other],
                    got.at[1, source, other],
                    send.at[0, 0, 0],
                    recv.at[1, source, other],
                    sibling,
                ).wait_recv()

            acc = part[1, other * SIDE + x].astype(F32)
            for j in range(1, SIDE):
                acc = acc + got[1, lax.rem(x + j, SIDE), other].astype(F32)
            passed[1, other] = acc.astype(BF16)

            @pl.when(i < SIDE)
            def _():
                second_copy(1, i, *second).start()

        for h in range(2):
            own = x if h == 0 else z

            @pl.loop(1, SIDE)
            def _(i):
                other = lax.rem(own + i, SIDE)
                remote(
                    last.at[h, other],
                    last.at[h, other],
                    send_two.at[h, 0],
                    recv_two.at[h, other],
                    sibling,
                ).wait_recv()

            acc = passed[h, own].astype(F32)
            for i in range(1, SIDE):
                acc = acc + last[h, lax.rem(own + i, SIDE)].astype(F32)
            total[:, h * wide : (h + 1) * wide] = acc

    def second_wait_send(second):
        @pl.loop(1, SIDE)
        def _(i):
            for h in range(2):
                second_copy(h, i, *second).wait_send()

    def normed(gain):
        values_in = total[...]
        mean = jnp.mean(values_in * values_in, axis=-1, keepdims=True)
        return values_in * lax.rsqrt(mean + NORM_EPSILON) * gain[...]

    def column_y(kind, view, i):
        other, device = y_peer(i)
        return remote(view(slot), view(slot), c_send.at[kind, i], c_recv.at[kind, slot], device)

    def column_core(kind, view, i):
        held = y_peer(i)[0] * 2 + core
        return remote(
            view(held), view(held), c_send.at[kind, SIDE + i], c_recv.at[kind, held], sibling
        )

    def column_start(kind, view):
        @pl.loop(1, SIDE)
        def _(i):
            column_y(kind, view, i).start()

        column_core(kind, view, 0).start()

    def column_wait(kind, view, held):
        remote(
            view(held), view(held), c_send.at[kind, 0], c_recv.at[kind, held], sibling
        ).wait_recv()

    def column_pass(kind, view):
        @pl.loop(1, SIDE)
        def _(i):
            column_wait(kind, view, y_peer(i)[0] * 2 + core)
            column_core(kind, view, i).start()

    def column_finish(kind, view):
        @pl.loop(0, SIDE)
        def _(i):
            column_wait(kind, view, y_peer(i)[0] * 2 + 1 - core)

    def column_wait_send(kind, view):
        @pl.loop(1, SIDE)
        def _(i):
            column_y(kind, view, i).wait_send()

        @pl.loop(0, SIDE)
        def _(i):
            column_core(kind, view, i).wait_send()

    column = (
        (0, lambda q: qkv_all.at[:, q]),
        (1, lambda q: out_all.at[q]),
        (2, lambda q: mlp_all.at[:, q]),
        (3, lambda q: down_all.at[q]),
    )
    qkv_move = (lambda p: stage_qkv.at[p], lambda p: qkv_all.at[p, slot], s_qkv, r_qkv)
    mlp_move = (lambda p: stage_mlp.at[p], lambda p: mlp_all.at[p, slot], s_mlp, r_mlp)
    sq_move = (lambda p: sq_all.at[me], lambda p: sq_all.at[p], s_sq, r_sq)
    tok_move = (tok_all, s_tok, r_tok)
    hid_move = (hid_all, s_hid, r_hid)
    one_a = (part_a, got_a, s_one_a, r_one_a)
    two_a = (pass_a, last_a, s_two_a, r_two_a)
    one_b = (part_b, got_b, s_one_b, r_one_b)
    two_b = (pass_b, last_b, s_two_b, r_two_b)

    plane_start(*qkv_move)
    gather_start(*tok_move)
    qkv_all[me, slot] = stage_qkv[me]
    out_all[slot] = output_w[...].astype(BF16)
    down_all[slot] = down_w[...].astype(BF16)

    def numbered(index, which):
        return index + ((index * 1639) >> 16) * rows + which * rows

    flat = lax.broadcasted_iota(jnp.int32, (set_rows, HEAD_DIM), 0)
    row = numbered(flat, yhi)
    start = jnp.zeros_like(row)
    end = jnp.int32(0)
    for r in range(lengths.shape[1]):
        end = end + lengths[0, r]
        start = start + jnp.where(row >= end, lengths[0, r], 0)
    opening[...] = start
    lane = lax.broadcasted_iota(jnp.int32, (1, HEAD_DIM), 1)
    half = HEAD_DIM // 2
    step = jnp.where(lane < half, lane, lane - half).astype(F32)
    frequency = jnp.exp(step * (-2.0 * math.log(ROPE_BASE) / HEAD_DIM))
    angle = (row - start).astype(F32) * frequency
    cosines[...] = jnp.cos(angle)
    sines[...] = jnp.sin(angle) * jnp.where(lane < half, -1.0, 1.0)
    plane_wait_recv(*qkv_move[1:])
    column_start(*column[0])
    column_start(*column[1])
    column_start(*column[3])
    gather_relay(*tok_move)
    for p in range(PLANE):
        cols = slice(p * hidden_width, (p + 1) * hidden_width)
        for k, w in enumerate((gate_w, up_w)):
            stage_mlp[p, :, k * hidden_width : (k + 1) * hidden_width] = w[:, cols].astype(BF16)
    column_pass(*column[0])
    column_finish(*column[0])

    def chunk(i):
        return pl.ds(pl.multiple_of(i * group_rows, group_rows), group_rows)

    def rotated(values_in, gain, here):
        scaled = values_in * gain
        return (scaled * cosines[here, :] + pltpu.roll(scaled, half, 1) * sines[here, :]).astype(
            BF16
        )

    @pl.loop(0, SIDE)
    def _(i):
        group = lax.rem(z + i, SIDE)
        here = chunk(group)
        gather_wait_group(*tok_move, group)
        made = dot(gathered(tok_all, group), qkv_all[...].reshape(features, 3 * HEAD_DIM))
        query, key = made[:, :HEAD_DIM], made[:, HEAD_DIM : 2 * HEAD_DIM]
        proj[here, :HEAD_DIM] = query * query
        proj[here, HEAD_DIM:] = key * key
        queries[here, :] = rotated(query, query_gain[...], here)
        kv[0, here, :HEAD_DIM] = rotated(key, key_gain[...], here)
        kv[0, here, HEAD_DIM:] = made[:, 2 * HEAD_DIM :].astype(BF16)

    pick = (
        lax.broadcasted_iota(jnp.int32, (8, 2 * HEAD_DIM), 1) // HEAD_DIM
        == lax.broadcasted_iota(jnp.int32, (8, 2 * HEAD_DIM), 0)
    ).astype(F32)
    sq_all[me] = lax.dot_general(
        pick, proj[...], (((1,), (1,)), ((), ())), precision=HIGHEST, preferred_element_type=F32
    )
    plane_start(*sq_move)
    kv_copy = remote(kv.at[0], kv.at[1], s_kv.at[0], r_kv.at[0], partner)
    kv_copy.start()
    plane_start(*mlp_move)
    mlp_all[me, slot] = stage_mlp[me]
    column_pass(*column[1])
    plane_wait_recv(*sq_move[1:])
    sums = sq_all[0]
    for p in range(1, PLANE):
        sums = sums + sq_all[p]
    scales[0] = lax.rsqrt(sums / features + NORM_EPSILON)
    scale_copy = remote(scales.at[0], scales.at[1], s_kv.at[1], r_kv.at[1], partner)
    scale_copy.start()
    query_scale = jnp.transpose(scales[0]) * (1.0 / math.sqrt(HEAD_DIM))
    proj[:, :8] = query_scale
    column_finish(*column[1])
    kv_copy.wait_recv()
    scale_copy.wait_recv()

    lane_index = lax.broadcasted_iota(jnp.int32, (1, set_rows), 1)

    @pl.loop(1, SIDE + 1)
    def _(i):
        group = lax.rem(z + i, SIDE)
        here = chunk(group)
        key_row = jnp.concatenate([numbered(lane_index, yhi), numbered(lane_index, 1 - yhi)], axis=1)
        key_scale = jnp.concatenate([scales[0, 1:2, :], scales[1, 1:2, :]], axis=1)
        own = lax.broadcasted_iota(jnp.int32, (group_rows, 1), 0) + group * group_rows
        own_row = numbered(own, yhi)
        first = opening[here, :][:, 0:1]
        scores = lax.dot_general(
            queries[here, :],
            kv[:, :, :HEAD_DIM].reshape(2 * set_rows, HEAD_DIM),
            (((1,), (1,)), ((), ())),
            preferred_element_type=F32,
        )
        scores = scores * proj[here, :HEAD_DIM][:, 0:1] * key_scale
        scores = jnp.where((key_row >= first) & (key_row <= own_row), scores, -1e30)
        weights = jnp.exp(scores - jnp.max(scores, axis=1, keepdims=True))
        weights = weights / jnp.sum(weights, axis=1, keepdims=True)
        attended = dot(
            weights.astype(BF16), kv[:, :, HEAD_DIM:].reshape(2 * set_rows, HEAD_DIM)
        ).astype(BF16)
        summed = dot(attended, out_all[...].reshape(HEAD_DIM, features))
        for b in range(SIDE):
            for h in range(2):
                part_a[h, group * SIDE + b] = summed[
                    b * rows : (b + 1) * rows, h * wide : (h + 1) * wide
                ].astype(BF16)
        sum_start(group, one_a)

    plane_wait_recv(*mlp_move[1:])
    column_start(*column[2])
    column_pass(*column[3])
    sum_finish(one_a, two_a)
    hidden = (tokens[...].astype(F32) + normed(attn_gain)).astype(BF16)
    for h in range(2):
        hid_all[h, me] = hidden[:, h * wide : (h + 1) * wide]
    gather_start(*hid_move)
    gather_relay(*hid_move)
    column_pass(*column[2])
    column_finish(*column[2])
    column_finish(*column[3])

    @pl.loop(0, SIDE)
    def _(i):
        group = lax.rem(z + i, SIDE)
        gather_wait_group(*hid_move, group)
        values_in = gathered(hid_all, group)
        tile = 256
        for c in range(hidden_width // tile):
            lo = c * tile
            gate = dot(values_in, mlp_all[:, :, :, lo : lo + tile].reshape(features, tile))
            lo = lo + hidden_width
            up = dot(values_in, mlp_all[:, :, :, lo : lo + tile].reshape(features, tile))
            act[:, c * tile : (c + 1) * tile] = (gate / (1.0 + jnp.exp(-gate)) * up).astype(BF16)
        across = 512
        for c in range(features // across):
            cols = slice(c * across, (c + 1) * across)
            summed = dot(act[...], down_all[:, :, cols].reshape(hidden_width, across))
            h, lo = c * across // wide, c * across % wide
            for b in range(SIDE):
                part_b[h, group * SIDE + b, :, lo : lo + across] = summed[
                    b * rows : (b + 1) * rows
                ].astype(BF16)
        sum_start(group, one_b)

    sum_finish(one_b, two_b)
    base = jnp.concatenate([hid_all[0, me], hid_all[1, me]], axis=1).astype(F32)
    out[...] = (base + normed(mlp_gain)).astype(BF16)

    for move in (qkv_move, mlp_move, sq_move):
        plane_wait_send(*move)
    for move in (tok_move, hid_move):
        gather_wait_send(*move)
    for one, two in ((one_a, two_a), (one_b, two_b)):
        sum_wait_send(one)
        second_wait_send(two)
    for kind, view in column:
        column_wait_send(kind, view)
    kv_copy.wait_send()
    scale_copy.wait_send()


def per_device(tokens, lengths, query_gain, key_gain, attn_gain, mlp_gain, *weights):
    place = lax.axis_index("z") * SIDE + lax.axis_index("x")
    q_part = lax.dynamic_slice_in_dim(query_gain, place * HEAD_DIM, HEAD_DIM)[None]
    k_part = lax.dynamic_slice_in_dim(key_gain, place * HEAD_DIM, HEAD_DIM)[None]
    rows, features = tokens.shape
    depth = weights[0].shape[0]
    ff = weights[4].shape[1] // PLANE
    down_depth = weights[6].shape[0]
    set_rows = rows * PLANE
    vmem = pl.BlockSpec(memory_space=pltpu.VMEM)
    dma = pltpu.SemaphoreType.DMA
    half = (rows, features // 2)
    return pl.pallas_call(
        kernel,
        out_shape=jax.ShapeDtypeStruct(tokens.shape, BF16),
        in_specs=[pl.BlockSpec(memory_space=pltpu.SMEM)] + [vmem] * 12,
        out_specs=vmem,
        scratch_shapes=[
            pltpu.VMEM((PLANE, depth, 3 * HEAD_DIM), BF16),
            pltpu.VMEM((PLANE, depth, 2 * ff), BF16),
            pltpu.VMEM((PLANE, COLUMN, depth, 3 * HEAD_DIM), BF16),
            pltpu.VMEM((PLANE, COLUMN, depth, 2 * ff), BF16),
            pltpu.VMEM((COLUMN, depth, features), BF16),
            pltpu.VMEM((COLUMN, down_depth, features), BF16),
            pltpu.VMEM((2, PLANE) + half, BF16),
            pltpu.VMEM((2, PLANE) + half, BF16),
            pltpu.VMEM((set_rows, 2 * HEAD_DIM), F32),
            pltpu.VMEM((PLANE, 8, set_rows), F32),
            pltpu.VMEM((2, 8, set_rows), F32),
            pltpu.VMEM((2, set_rows, 2 * HEAD_DIM), BF16),
            pltpu.VMEM((set_rows, HEAD_DIM), BF16),
            pltpu.VMEM((set_rows, HEAD_DIM), F32),
            pltpu.VMEM((set_rows, HEAD_DIM), F32),
            pltpu.VMEM((set_rows, HEAD_DIM), jnp.int32),
            pltpu.VMEM((2, PLANE) + half, BF16),
            pltpu.VMEM((2, PLANE) + half, BF16),
            pltpu.VMEM((2, SIDE, SIDE) + half, BF16),
            pltpu.VMEM((2, SIDE, SIDE) + half, BF16),
            pltpu.VMEM((2, SIDE) + half, BF16),
            pltpu.VMEM((2, SIDE) + half, BF16),
            pltpu.VMEM((2, SIDE) + half, BF16),
            pltpu.VMEM((2, SIDE) + half, BF16),
            pltpu.VMEM((rows * SIDE, ff), BF16),
            pltpu.VMEM((rows, features), F32),
        ]
        + [dma((PLANE,))] * 6
        + [dma((2, 2, SIDE, SIDE)), dma((2, PLANE))] * 2
        + [dma((2, SIDE, SIDE)), dma((2, SIDE, SIDE)), dma((2, SIDE)), dma((2, SIDE))] * 2
        + [dma((4, COLUMN)), dma((4, COLUMN)), dma((2,)), dma((2,))],
        compiler_params=pltpu.CompilerParams(
            collective_id=0, has_side_effects=True, vmem_limit_bytes=60 << 20
        ),
    )(lengths, tokens, q_part, k_part, attn_gain[None], mlp_gain[None], *weights)


def solution(mesh):
    fine = Mesh(mesh.devices.reshape(2, 2, 4, 4, 2), ("ylo", "core", "z", "x", "yhi"))
    tok = P(("ylo", "core", "z", "x", "yhi"), None)
    weight = P(("z", "x", "yhi", "ylo", "core"), None)
    return jax.shard_map(
        per_device,
        mesh=fine,
        in_specs=(tok, P(("ylo", "core"), None), P(), P(), P(), P()) + (weight,) * 7,
        out_specs=tok,
        check_vma=False,
    )
```

```python
import math

import jax
import jax.numpy as jnp
from jax import lax
from jax.experimental import pallas as pl
from jax.experimental.pallas import tpu as pltpu
from jax.sharding import Mesh, PartitionSpec as P

HEAD_DIM = 128
NORM_EPSILON = 1e-06
ROPE_BASE = 500000.0
SIDE = 4
PLANE = SIDE * SIDE
COLUMN = 8
MESH = pl.DeviceIdType.MESH
F32 = jnp.float32
BF16 = jnp.bfloat16
HIGHEST = lax.Precision.HIGHEST


def remote(src, dst, send_sem, recv_sem, device):
    return pltpu.make_async_remote_copy(
        src_ref=src,
        dst_ref=dst,
        send_sem=send_sem,
        recv_sem=recv_sem,
        device_id=device,
        device_id_type=MESH,
    )


def plane_device(place):
    return {"z": place // SIDE, "x": lax.rem(place, SIDE)}


def dot(a, b):
    return jnp.dot(a, b, preferred_element_type=F32)


def kernel(
    lengths,
    tokens,
    query_gain_in,
    key_gain_in,
    attn_gain_in,
    mlp_gain_in,
    query_in,
    key_in,
    value_in,
    output_in,
    gate_in,
    up_in,
    down_in,
    out,
    query_gain,
    key_gain,
    attn_gain,
    mlp_gain,
    query_w,
    key_w,
    value_w,
    output_w,
    gate_w,
    up_w,
    down_w,
    stage_qkv,
    stage_mlp,
    qkv_all,
    mlp_all,
    out_all,
    down_all,
    tok_all,
    hid_all,
    proj,
    sq_all,
    scales,
    key_scale,
    kv,
    queries,
    cosines,
    sines,
    opening,
    part_a,
    part_b,
    got_a,
    got_b,
    pass_a,
    pass_b,
    last_a,
    last_b,
    act,
    total,
    s_qkv,
    r_qkv,
    s_mlp,
    r_mlp,
    s_sq,
    r_sq,
    s_tok,
    r_tok,
    s_hid,
    r_hid,
    s_one_a,
    r_one_a,
    s_two_a,
    r_two_a,
    s_one_b,
    r_one_b,
    s_two_b,
    r_two_b,
    c_send,
    c_recv,
    s_kv,
    r_kv,
    s_scale,
    r_scale,
    fetch,
):
    z, x = lax.axis_index("z"), lax.axis_index("x")
    yhi, ylo, core = lax.axis_index("yhi"), lax.axis_index("ylo"), lax.axis_index("core")
    me = z * SIDE + x
    y = yhi * 2 + ylo
    slot = y * 2 + core
    rows = tokens.shape[0]
    set_rows = rows * PLANE
    group_rows = rows * SIDE
    features = tokens.shape[1]
    wide = features // 2
    hidden_width = act.shape[1]

    def y_peer(step):
        other = lax.rem(y + step, SIDE)
        return other, {"yhi": other // 2, "ylo": lax.rem(other, 2)}

    sibling = {"core": 1 - core}
    partner = {"yhi": 1 - yhi}

    barrier = pltpu.get_barrier_semaphore()

    @pl.loop(1, PLANE)
    def _(i):
        pl.semaphore_signal(
            barrier, inc=1, device_id=plane_device(lax.rem(me + i, PLANE)), device_id_type=MESH
        )

    @pl.loop(1, SIDE)
    def _(i):
        pl.semaphore_signal(barrier, inc=1, device_id=y_peer(i)[1], device_id_type=MESH)

    pl.semaphore_signal(barrier, inc=1, device_id=sibling, device_id_type=MESH)

    inputs = [(tokens.at[:, pl.ds(h * wide, wide)], tok_all.at[h, me]) for h in range(2)] + [
        (query_in, query_w),
        (key_in, key_w),
        (value_in, value_w),
        (output_in, output_w),
        (down_in, down_w),
        (query_gain_in, query_gain),
        (key_gain_in, key_gain),
        (attn_gain_in, attn_gain),
        (mlp_gain_in, mlp_gain),
        (gate_in, gate_w),
        (up_in, up_w),
    ]
    fetches = [pltpu.make_async_copy(*pair, fetch.at[i]) for i, pair in enumerate(inputs)]
    for copy in fetches:
        copy.start()

    for copy in fetches[2:5]:
        copy.wait()
    for p in range(PLANE):
        cols = slice(p * HEAD_DIM, (p + 1) * HEAD_DIM)
        for k, w in enumerate((query_w, key_w, value_w)):
            stage_qkv[p, :, k * HEAD_DIM : (k + 1) * HEAD_DIM] = w[:, cols].astype(BF16)
    for copy in fetches[:2]:
        copy.wait()
    pl.semaphore_wait(barrier, PLANE - 1 + SIDE)

    def plane_copy(i, src, dst, send, recv):
        peer = lax.rem(me + i, PLANE)
        return remote(src(peer), dst(me), send.at[i], recv.at[me], plane_device(peer))

    def plane_start(src, dst, send, recv):
        @pl.loop(1, PLANE)
        def _(i):
            plane_copy(i, src, dst, send, recv).start()

    def plane_wait_send(src, dst, send, recv):
        @pl.loop(1, PLANE)
        def _(i):
            plane_copy(i, src, dst, send, recv).wait_send()

    def plane_wait_recv(dst, send, recv):
        @pl.loop(1, PLANE)
        def _(i):
            peer = lax.rem(me + PLANE - i, PLANE)
            remote(dst(peer), dst(peer), send.at[0], recv.at[peer], plane_device(peer)).wait_recv()

    def along(h, order, i):
        if h == order:
            return z * SIDE + lax.rem(x + i, SIDE)
        return lax.rem(z + i, SIDE) * SIDE + x

    def gather_copy(ref, send, recv, h, order, j, i):
        held = along(h, 0, SIDE - j) if order == 1 else me
        return remote(
            ref.at[h, held],
            ref.at[h, held],
            send.at[h, order, j, i],
            recv.at[h, held],
            plane_device(along(h, order, i)),
        )

    def gather_wait(ref, send, recv, h, held):
        remote(
            ref.at[h, held], ref.at[h, held], send.at[0, 0, 0, 0], recv.at[h, held], sibling
        ).wait_recv()

    def gather_start(ref, send, recv):
        for order in range(2):

            @pl.loop(1, SIDE)
            def _(i):
                for h in range(2):
                    gather_copy(ref, send, recv, h, order, 0, i).start()

    def gather_relay(ref, send, recv):
        @pl.loop(1, SIDE)
        def _(j):
            for h in range(2):
                gather_wait(ref, send, recv, h, along(h, 0, SIDE - j))

                @pl.loop(1, SIDE)
                def _(i):
                    gather_copy(ref, send, recv, h, 1, j, i).start()

    def gather_wait_group(ref, send, recv, group):
        @pl.when(group != z)
        def _():
            @pl.loop(0, SIDE)
            def _(b):
                gather_wait(ref, send, recv, 0, group * SIDE + b)

        @pl.loop(1, SIDE)
        def _(i):
            gather_wait(ref, send, recv, 1, group * SIDE + lax.rem(x + i, SIDE))

    def gather_wait_send(ref, send, recv):
        @pl.loop(1, SIDE)
        def _(i):
            for h in range(2):
                gather_copy(ref, send, recv, h, 0, 0, i).wait_send()

                @pl.loop(0, SIDE)
                def _(j):
                    gather_copy(ref, send, recv, h, 1, j, i).wait_send()

    def gathered(ref, group):
        halves = []
        for h in range(2):
            blocks = [ref[h, group * SIDE + b].astype(F32) for b in range(SIDE)]
            halves.append(jnp.concatenate(blocks, axis=0).astype(BF16))
        return jnp.concatenate(halves, axis=1)

    def sum_first(group, part, got, send, recv):
        def tall():
            return remote(
                part.at[0, pl.ds(group * SIDE, SIDE)],
                got.at[0, z],
                send.at[0, 0, group],
                recv.at[0, 0, z],
                {"z": group},
            )

        def flat(i):
            other = lax.rem(x + i, SIDE)
            return remote(
                part.at[1, group * SIDE + other],
                got.at[1, x, group],
                send.at[1, i, group],
                recv.at[1, x, group],
                {"x": other},
            )

        return tall, flat

    def sum_start(group, move):
        tall, flat = sum_first(group, *move)

        @pl.when(group != z)
        def _():
            tall().start()

        @pl.loop(1, SIDE)
        def _(i):
            flat(i).start()

    def sum_wait_send(move):
        @pl.loop(1, SIDE)
        def _(i):
            sum_first(lax.rem(z + i, SIDE), *move)[0]().wait_send()

        @pl.loop(0, SIDE)
        def _(group):
            @pl.loop(1, SIDE)
            def _(i):
                sum_first(group, *move)[1](i).wait_send()

    def second_copy(h, i, passed, last, send, recv):
        own = x if h == 0 else z
        other = lax.rem(own + i, SIDE)
        return remote(
            passed.at[h, other],
            last.at[h, own],
            send.at[h, i],
            recv.at[h, own],
            {"x": other} if h == 0 else {"z": other},
        )

    def sum_finish(move, second):
        part, got, send, recv = move
        passed, last, send_two, recv_two = second

        @pl.loop(1, SIDE)
        def _(i):
            other = lax.rem(z + i, SIDE)
            remote(
                got.at[0, other], got.at[0, other], send.at[0, 0, 0], recv.at[0, 0, other], sibling
            ).wait_recv()

        @pl.loop(1, SIDE + 1)
        def _(i):
            other = lax.rem(x + i, SIDE)
            acc = part[0, z * SIDE + other].astype(F32)
            for j in range(1, SIDE):
                acc = acc + got[0, lax.rem(z + j, SIDE), other].astype(F32)
            passed[0, other] = acc.astype(BF16)

            @pl.when(i < SIDE)
            def _():
                second_copy(0, i, *second).start()

        @pl.loop(1, SIDE + 1)
        def _(i):
            other = lax.rem(z + i, SIDE)

            @pl.loop(1, SIDE)
            def _(j):
                source = lax.rem(x + j, SIDE)
                remote(
                    got.at[1, source, other],
                    got.at[1, source, other],
                    send.at[0, 0, 0],
                    recv.at[1, source, other],
                    sibling,
                ).wait_recv()

            acc = part[1, other * SIDE + x].astype(F32)
            for j in range(1, SIDE):
                acc = acc + got[1, lax.rem(x + j, SIDE), other].astype(F32)
            passed[1, other] = acc.astype(BF16)

            @pl.when(i < SIDE)
            def _():
                second_copy(1, i, *second).start()

        for h in range(2):
            own = x if h == 0 else z

            @pl.loop(1, SIDE)
            def _(i):
                other = lax.rem(own + i, SIDE)
                remote(
                    last.at[h, other],
                    last.at[h, other],
                    send_two.at[h, 0],
                    recv_two.at[h, other],
                    sibling,
                ).wait_recv()

            acc = passed[h, own].astype(F32)
            for i in range(1, SIDE):
                acc = acc + last[h, lax.rem(own + i, SIDE)].astype(F32)
            total[:, h * wide : (h + 1) * wide] = acc

    def second_wait_send(second):
        @pl.loop(1, SIDE)
        def _(i):
            for h in range(2):
                second_copy(h, i, *second).wait_send()

    def normed(gain):
        values_in = total[...]
        mean = jnp.mean(values_in * values_in, axis=-1, keepdims=True)
        return values_in * lax.rsqrt(mean + NORM_EPSILON) * gain[...]

    def column_y(kind, view, i):
        other, device = y_peer(i)
        return remote(view(slot), view(slot), c_send.at[kind, i], c_recv.at[kind, slot], device)

    def column_core(kind, view, i):
        held = y_peer(i)[0] * 2 + core
        return remote(
            view(held), view(held), c_send.at[kind, SIDE + i], c_recv.at[kind, held], sibling
        )

    def column_start(kind, view):
        @pl.loop(1, SIDE)
        def _(i):
            column_y(kind, view, i).start()

        column_core(kind, view, 0).start()

    def column_wait(kind, view, held):
        remote(
            view(held), view(held), c_send.at[kind, 0], c_recv.at[kind, held], sibling
        ).wait_recv()

    def column_pass(kind, view):
        @pl.loop(1, SIDE)
        def _(i):
            column_wait(kind, view, y_peer(i)[0] * 2 + core)
            column_core(kind, view, i).start()

    def column_finish(kind, view):
        @pl.loop(0, SIDE)
        def _(i):
            column_wait(kind, view, y_peer(i)[0] * 2 + 1 - core)

    def column_wait_send(kind, view):
        @pl.loop(1, SIDE)
        def _(i):
            column_y(kind, view, i).wait_send()

        @pl.loop(0, SIDE)
        def _(i):
            column_core(kind, view, i).wait_send()

    column = (
        (0, lambda q: qkv_all.at[:, q]),
        (1, lambda q: out_all.at[q]),
        (2, lambda q: mlp_all.at[:, q]),
        (3, lambda q: down_all.at[q]),
    )
    qkv_move = (lambda p: stage_qkv.at[p], lambda p: qkv_all.at[p, slot], s_qkv, r_qkv)
    mlp_move = (lambda p: stage_mlp.at[p], lambda p: mlp_all.at[p, slot], s_mlp, r_mlp)
    sq_move = (lambda p: sq_all.at[me], lambda p: sq_all.at[p], s_sq, r_sq)
    tok_move = (tok_all, s_tok, r_tok)
    hid_move = (hid_all, s_hid, r_hid)
    one_a = (part_a, got_a, s_one_a, r_one_a)
    two_a = (pass_a, last_a, s_two_a, r_two_a)
    one_b = (part_b, got_b, s_one_b, r_one_b)
    two_b = (pass_b, last_b, s_two_b, r_two_b)

    plane_start(*qkv_move)
    gather_start(*tok_move)
    qkv_all[me, slot] = stage_qkv[me]
    for copy in fetches[5:]:
        copy.wait()
    out_all[slot] = output_w[...].astype(BF16)
    down_all[slot] = down_w[...].astype(BF16)

    def numbered(index, which):
        return index + ((index * 1639) >> 16) * rows + which * rows

    flat = lax.broadcasted_iota(jnp.int32, (set_rows, HEAD_DIM), 0)
    row = numbered(flat, yhi)
    start = jnp.zeros_like(row)
    end = jnp.int32(0)
    for r in range(lengths.shape[1]):
        end = end + lengths[0, r]
        start = start + jnp.where(row >= end, lengths[0, r], 0)
    opening[...] = start
    lane = lax.broadcasted_iota(jnp.int32, (1, HEAD_DIM), 1)
    half = HEAD_DIM // 2
    step = jnp.where(lane < half, lane, lane - half).astype(F32)
    frequency = jnp.exp(step * (-2.0 * math.log(ROPE_BASE) / HEAD_DIM))
    angle = (row - start).astype(F32) * frequency
    cosines[...] = jnp.cos(angle)
    sines[...] = jnp.sin(angle) * jnp.where(lane < half, -1.0, 1.0)
    plane_wait_recv(*qkv_move[1:])
    column_start(*column[0])
    column_start(*column[1])
    gather_relay(*tok_move)
    for p in range(PLANE):
        cols = slice(p * hidden_width, (p + 1) * hidden_width)
        for k, w in enumerate((gate_w, up_w)):
            stage_mlp[p, :, k * hidden_width : (k + 1) * hidden_width] = w[:, cols].astype(BF16)
    column_pass(*column[0])
    column_finish(*column[0])

    def chunk(i):
        return pl.ds(pl.multiple_of(i * group_rows, group_rows), group_rows)

    def rotated(values_in, gain, here):
        scaled = values_in * gain
        return (scaled * cosines[here, :] + pltpu.roll(scaled, half, 1) * sines[here, :]).astype(
            BF16
        )

    def kv_copy(group):
        here = chunk(group)
        return remote(
            kv.at[0, here], kv.at[1, here], s_kv.at[group], r_kv.at[group], partner
        )

    sq_all[me] = jnp.zeros_like(sq_all[me])

    @pl.loop(0, SIDE)
    def _(i):
        group = lax.rem(z + i, SIDE)
        here = chunk(group)
        gather_wait_group(*tok_move, group)
        made = dot(gathered(tok_all, group), qkv_all[...].reshape(features, 3 * HEAD_DIM))
        query, key = made[:, :HEAD_DIM], made[:, HEAD_DIM : 2 * HEAD_DIM]
        queries[here, :] = rotated(query, query_gain[pl.ds(me, 1), :], here)
        kv[0, here, :HEAD_DIM] = rotated(key, key_gain[pl.ds(me, 1), :], here)
        kv[0, here, HEAD_DIM:] = made[:, 2 * HEAD_DIM :].astype(BF16)
        kv_copy(group).start()
        pick = (
            lax.broadcasted_iota(jnp.int32, (8, 2 * HEAD_DIM), 1) // HEAD_DIM * SIDE + group
            == lax.broadcasted_iota(jnp.int32, (8, 2 * HEAD_DIM), 0)
        ).astype(F32)
        both = made[:, : 2 * HEAD_DIM]
        sq_all[me] += lax.dot_general(
            pick,
            both * both,
            (((1,), (1,)), ((), ())),
            precision=HIGHEST,
            preferred_element_type=F32,
        )

    plane_start(*sq_move)
    column_start(*column[3])
    plane_start(*mlp_move)
    mlp_all[me, slot] = stage_mlp[me]
    column_pass(*column[1])
    plane_wait_recv(*sq_move[1:])
    sums = sq_all[0]
    for p in range(1, PLANE):
        sums = sums + sq_all[p]
    scales[0] = lax.rsqrt(sums / features + NORM_EPSILON)
    scale_copy = remote(scales.at[0], scales.at[1], s_scale, r_scale, partner)
    scale_copy.start()
    proj[:, :8] = jnp.transpose(scales[0]) * (1.0 / math.sqrt(HEAD_DIM))
    column_finish(*column[1])

    @pl.loop(0, SIDE)
    def _(group):
        kv_copy(group).wait_recv()

    scale_copy.wait_recv()
    for k in range(2):
        for g in range(SIDE):
            lo = k * set_rows + g * group_rows
            key_scale[:, lo : lo + group_rows] = scales[k, SIDE + g : SIDE + g + 1, :]

    lane_index = lax.broadcasted_iota(jnp.int32, (1, set_rows), 1)

    @pl.loop(1, SIDE + 1)
    def _(i):
        group = lax.rem(z + i, SIDE)
        here = chunk(group)
        key_row = jnp.concatenate([numbered(lane_index, yhi), numbered(lane_index, 1 - yhi)], axis=1)
        query_lane = lax.broadcasted_iota(jnp.int32, (group_rows, 8), 1)
        query_scale = jnp.sum(
            jnp.where(query_lane == group, proj[:, :8], 0.0), axis=1, keepdims=True
        )
        own = lax.broadcasted_iota(jnp.int32, (group_rows, 1), 0) + group * group_rows
        own_row = numbered(own, yhi)
        first = opening[here, :][:, 0:1]
        scores = lax.dot_general(
            queries[here, :],
            kv[:, :, :HEAD_DIM].reshape(2 * set_rows, HEAD_DIM),
            (((1,), (1,)), ((), ())),
            preferred_element_type=F32,
        )
        scores = scores * query_scale * key_scale[...]
        scores = jnp.where((key_row >= first) & (key_row <= own_row), scores, -1e30)
        weights = jnp.exp(scores - jnp.max(scores, axis=1, keepdims=True))
        weights = weights / jnp.sum(weights, axis=1, keepdims=True)
        attended = dot(
            weights.astype(BF16), kv[:, :, HEAD_DIM:].reshape(2 * set_rows, HEAD_DIM)
        ).astype(BF16)
        summed = dot(attended, out_all[...].reshape(HEAD_DIM, features))
        for b in range(SIDE):
            for h in range(2):
                part_a[h, group * SIDE + b] = summed[
                    b * rows : (b + 1) * rows, h * wide : (h + 1) * wide
                ].astype(BF16)
        sum_start(group, one_a)

    plane_wait_recv(*mlp_move[1:])
    column_start(*column[2])
    column_pass(*column[3])
    sum_finish(one_a, two_a)
    base = jnp.concatenate([tok_all[0, me], tok_all[1, me]], axis=1).astype(F32)
    hidden = (base + normed(attn_gain)).astype(BF16)
    for h in range(2):
        hid_all[h, me] = hidden[:, h * wide : (h + 1) * wide]
    gather_start(*hid_move)
    gather_relay(*hid_move)
    column_pass(*column[2])
    column_finish(*column[2])
    column_finish(*column[3])

    @pl.loop(0, SIDE)
    def _(i):
        group = lax.rem(z + i, SIDE)
        gather_wait_group(*hid_move, group)
        values_in = gathered(hid_all, group)
        tile = 256
        for c in range(hidden_width // tile):
            lo = c * tile
            gate = dot(values_in, mlp_all[:, :, :, lo : lo + tile].reshape(features, tile))
            lo = lo + hidden_width
            up = dot(values_in, mlp_all[:, :, :, lo : lo + tile].reshape(features, tile))
            act[:, c * tile : (c + 1) * tile] = (gate / (1.0 + jnp.exp(-gate)) * up).astype(BF16)
        across = 512
        for c in range(features // across):
            cols = slice(c * across, (c + 1) * across)
            summed = dot(act[...], down_all[:, :, cols].reshape(hidden_width, across))
            h, lo = c * across // wide, c * across % wide
            for b in range(SIDE):
                part_b[h, group * SIDE + b, :, lo : lo + across] = summed[
                    b * rows : (b + 1) * rows
                ].astype(BF16)
        sum_start(group, one_b)

    sum_finish(one_b, two_b)
    base = jnp.concatenate([hid_all[0, me], hid_all[1, me]], axis=1).astype(F32)
    out[...] = (base + normed(mlp_gain)).astype(BF16)

    for move in (qkv_move, mlp_move, sq_move):
        plane_wait_send(*move)
    for move in (tok_move, hid_move):
        gather_wait_send(*move)
    for one, two in ((one_a, two_a), (one_b, two_b)):
        sum_wait_send(one)
        second_wait_send(two)
    for kind, view in column:
        column_wait_send(kind, view)
    scale_copy.wait_send()

    @pl.loop(0, SIDE)
    def _(group):
        kv_copy(group).wait_send()


def per_device(tokens, lengths, query_gain, key_gain, attn_gain, mlp_gain, *weights):
    rows, features = tokens.shape
    depth = weights[0].shape[0]
    ff = weights[4].shape[1] // PLANE
    down_depth = weights[6].shape[0]
    set_rows = rows * PLANE
    vmem = pl.BlockSpec(memory_space=pltpu.VMEM)
    anywhere = pl.BlockSpec(memory_space=pl.ANY)
    dma = pltpu.SemaphoreType.DMA
    half = (rows, features // 2)
    return pl.pallas_call(
        kernel,
        out_shape=jax.ShapeDtypeStruct(tokens.shape, BF16),
        in_specs=[pl.BlockSpec(memory_space=pltpu.SMEM)] + [anywhere] * 12,
        out_specs=vmem,
        scratch_shapes=[
            pltpu.VMEM((PLANE, HEAD_DIM), F32),
            pltpu.VMEM((PLANE, HEAD_DIM), F32),
            pltpu.VMEM((1, features), F32),
            pltpu.VMEM((1, features), F32),
        ]
        + [pltpu.VMEM(w.shape, F32) for w in weights]
        + [
            pltpu.VMEM((PLANE, depth, 3 * HEAD_DIM), BF16),
            pltpu.VMEM((PLANE, depth, 2 * ff), BF16),
            pltpu.VMEM((PLANE, COLUMN, depth, 3 * HEAD_DIM), BF16),
            pltpu.VMEM((PLANE, COLUMN, depth, 2 * ff), BF16),
            pltpu.VMEM((COLUMN, depth, features), BF16),
            pltpu.VMEM((COLUMN, down_depth, features), BF16),
            pltpu.VMEM((2, PLANE) + half, BF16),
            pltpu.VMEM((2, PLANE) + half, BF16),
            pltpu.VMEM((rows * SIDE, HEAD_DIM), F32),
            pltpu.VMEM((PLANE, 8, rows * SIDE), F32),
            pltpu.VMEM((2, 8, rows * SIDE), F32),
            pltpu.VMEM((1, 2 * set_rows), F32),
            pltpu.VMEM((2, set_rows, 2 * HEAD_DIM), BF16),
            pltpu.VMEM((set_rows, HEAD_DIM), BF16),
            pltpu.VMEM((set_rows, HEAD_DIM), F32),
            pltpu.VMEM((set_rows, HEAD_DIM), F32),
            pltpu.VMEM((set_rows, HEAD_DIM), jnp.int32),
            pltpu.VMEM((2, PLANE) + half, BF16),
            pltpu.VMEM((2, PLANE) + half, BF16),
            pltpu.VMEM((2, SIDE, SIDE) + half, BF16),
            pltpu.VMEM((2, SIDE, SIDE) + half, BF16),
            pltpu.VMEM((2, SIDE) + half, BF16),
            pltpu.VMEM((2, SIDE) + half, BF16),
            pltpu.VMEM((2, SIDE) + half, BF16),
            pltpu.VMEM((2, SIDE) + half, BF16),
            pltpu.VMEM((rows * SIDE, ff), BF16),
            pltpu.VMEM((rows, features), F32),
        ]
        + [dma((PLANE,))] * 6
        + [dma((2, 2, SIDE, SIDE)), dma((2, PLANE))] * 2
        + [dma((2, SIDE, SIDE)), dma((2, SIDE, SIDE)), dma((2, SIDE)), dma((2, SIDE))] * 2
        + [dma((4, COLUMN)), dma((4, COLUMN)), dma((SIDE,)), dma((SIDE,))]
        + [dma(()), dma(()), dma((16,))],
        compiler_params=pltpu.CompilerParams(
            collective_id=0, has_side_effects=True, vmem_limit_bytes=60 << 20
        ),
    )(
        lengths,
        tokens,
        query_gain.reshape(PLANE, HEAD_DIM),
        key_gain.reshape(PLANE, HEAD_DIM),
        attn_gain[None],
        mlp_gain[None],
        *weights,
    )


def solution(mesh):
    fine = Mesh(mesh.devices.reshape(2, 2, 4, 4, 2), ("ylo", "core", "z", "x", "yhi"))
    tok = P(("ylo", "core", "z", "x", "yhi"), None)
    weight = P(("z", "x", "yhi", "ylo", "core"), None)
    return jax.shard_map(
        per_device,
        mesh=fine,
        in_specs=(tok, P(("ylo", "core"), None), P(), P(), P(), P()) + (weight,) * 7,
        out_specs=tok,
        check_vma=False,
    )
```

```python
import math

import jax
import jax.numpy as jnp
from jax import lax
from jax.experimental import pallas as pl
from jax.experimental.pallas import tpu as pltpu
from jax.sharding import Mesh, PartitionSpec as P

HEAD_DIM = 128
NORM_EPSILON = 1e-06
ROPE_BASE = 500000.0
SIDE = 4
PLANE = SIDE * SIDE
COLUMN = 8
MESH = pl.DeviceIdType.MESH
F32 = jnp.float32
BF16 = jnp.bfloat16
HIGHEST = lax.Precision.HIGHEST


def remote(src, dst, send_sem, recv_sem, device):
    return pltpu.make_async_remote_copy(
        src_ref=src,
        dst_ref=dst,
        send_sem=send_sem,
        recv_sem=recv_sem,
        device_id=device,
        device_id_type=MESH,
    )


def plane_device(place):
    return {"z": place // SIDE, "x": lax.rem(place, SIDE)}


def dot(a, b):
    return jnp.dot(a, b, preferred_element_type=F32)


def kernel(
    lengths,
    tokens,
    query_gain_in,
    key_gain_in,
    attn_gain_in,
    mlp_gain_in,
    query_in,
    key_in,
    value_in,
    output_in,
    gate_in,
    up_in,
    down_in,
    out,
    query_gain,
    key_gain,
    attn_gain,
    mlp_gain,
    query_w,
    key_w,
    value_w,
    output_w,
    gate_w,
    up_w,
    down_w,
    stage_qkv,
    stage_mlp,
    qkv_all,
    mlp_all,
    out_all,
    down_all,
    tok_all,
    hid_all,
    proj,
    sq_all,
    scales,
    key_scale,
    kv,
    queries,
    cosines,
    sines,
    opening,
    part_a,
    part_b,
    got_a,
    got_b,
    pass_a,
    pass_b,
    last_a,
    last_b,
    act,
    total,
    s_qkv,
    r_qkv,
    s_mlp,
    r_mlp,
    s_sq,
    r_sq,
    s_tok,
    r_tok,
    s_hid,
    r_hid,
    s_one_a,
    r_one_a,
    s_two_a,
    r_two_a,
    s_one_b,
    r_one_b,
    s_two_b,
    r_two_b,
    c_send,
    c_recv,
    s_kv,
    r_kv,
    s_scale,
    r_scale,
    fetch,
    entered,
):
    z, x = lax.axis_index("z"), lax.axis_index("x")
    yhi, ylo, core = lax.axis_index("yhi"), lax.axis_index("ylo"), lax.axis_index("core")
    me = z * SIDE + x
    y = yhi * 2 + ylo
    slot = y * 2 + core
    rows = tokens.shape[0]
    set_rows = rows * PLANE
    group_rows = rows * SIDE
    features = tokens.shape[1]
    wide = features // 2
    hidden_width = act.shape[1]

    def y_peer(step):
        other = lax.rem(y + step, SIDE)
        return other, {"yhi": other // 2, "ylo": lax.rem(other, 2)}

    sibling = {"core": 1 - core}
    partner = {"yhi": 1 - yhi}

    barrier = pltpu.get_barrier_semaphore()

    @pl.loop(1, SIDE)
    def _(i):
        for device in ({"x": lax.rem(x + i, SIDE)}, {"z": lax.rem(z + i, SIDE)}, y_peer(i)[1]):
            pl.semaphore_signal(barrier, inc=1, device_id=device, device_id_type=MESH)

    pl.semaphore_signal(barrier, inc=1, device_id=sibling, device_id_type=MESH)

    inputs = [(tokens.at[:, pl.ds(h * wide, wide)], tok_all.at[h, me]) for h in range(2)] + [
        (query_in, query_w),
        (key_in, key_w),
        (value_in, value_w),
        (output_in, output_w),
        (down_in, down_w),
        (query_gain_in, query_gain),
        (key_gain_in, key_gain),
        (attn_gain_in, attn_gain),
        (mlp_gain_in, mlp_gain),
        (gate_in, gate_w),
        (up_in, up_w),
    ]
    fetches = [pltpu.make_async_copy(*pair, fetch.at[i]) for i, pair in enumerate(inputs)]
    for copy in fetches:
        copy.start()

    for copy in fetches[2:5]:
        copy.wait()
    for p in range(PLANE):
        cols = slice(p * HEAD_DIM, (p + 1) * HEAD_DIM)
        for k, w in enumerate((query_w, key_w, value_w)):
            stage_qkv[p, :, k * HEAD_DIM : (k + 1) * HEAD_DIM] = w[:, cols].astype(BF16)
    for copy in fetches[:2]:
        copy.wait()
    pl.semaphore_wait(barrier, 3 * (SIDE - 1) + 1)

    @pl.loop(1, SIDE)
    def _(i):
        pl.semaphore_signal(
            entered, inc=1, device_id={"x": lax.rem(x + i, SIDE)}, device_id_type=MESH
        )

    def plane_copy(i, src, dst, send, recv):
        peer = lax.rem(me + i, PLANE)
        return remote(src(peer), dst(me), send.at[i], recv.at[me], plane_device(peer))

    def plane_start(src, dst, send, recv):
        @pl.loop(1, PLANE)
        def _(i):
            plane_copy(i, src, dst, send, recv).start()

    def plane_wait_send(src, dst, send, recv):
        @pl.loop(1, PLANE)
        def _(i):
            plane_copy(i, src, dst, send, recv).wait_send()

    def plane_wait_recv(dst, send, recv):
        @pl.loop(1, PLANE)
        def _(i):
            peer = lax.rem(me + PLANE - i, PLANE)
            remote(dst(peer), dst(peer), send.at[0], recv.at[peer], plane_device(peer)).wait_recv()

    def along(h, order, i):
        if h == order:
            return z * SIDE + lax.rem(x + i, SIDE)
        return lax.rem(z + i, SIDE) * SIDE + x

    def gather_copy(ref, send, recv, h, order, j, i):
        held = along(h, 0, SIDE - j) if order == 1 else me
        return remote(
            ref.at[h, held],
            ref.at[h, held],
            send.at[h, order, j, i],
            recv.at[h, held],
            plane_device(along(h, order, i)),
        )

    def gather_wait(ref, send, recv, h, held):
        remote(
            ref.at[h, held], ref.at[h, held], send.at[0, 0, 0, 0], recv.at[h, held], sibling
        ).wait_recv()

    def gather_start(ref, send, recv):
        for order in range(2):

            @pl.loop(1, SIDE)
            def _(i):
                for h in range(2):
                    gather_copy(ref, send, recv, h, order, 0, i).start()

    def gather_relay(ref, send, recv):
        @pl.loop(1, SIDE)
        def _(j):
            for h in range(2):
                gather_wait(ref, send, recv, h, along(h, 0, SIDE - j))

                @pl.loop(1, SIDE)
                def _(i):
                    gather_copy(ref, send, recv, h, 1, j, i).start()

    def gather_wait_group(ref, send, recv, group):
        @pl.when(group != z)
        def _():
            @pl.loop(0, SIDE)
            def _(b):
                gather_wait(ref, send, recv, 0, group * SIDE + b)

        @pl.loop(1, SIDE)
        def _(i):
            gather_wait(ref, send, recv, 1, group * SIDE + lax.rem(x + i, SIDE))

    def gather_wait_send(ref, send, recv):
        @pl.loop(1, SIDE)
        def _(i):
            for h in range(2):
                gather_copy(ref, send, recv, h, 0, 0, i).wait_send()

                @pl.loop(0, SIDE)
                def _(j):
                    gather_copy(ref, send, recv, h, 1, j, i).wait_send()

    def gathered(ref, group):
        halves = []
        for h in range(2):
            blocks = [ref[h, group * SIDE + b].astype(F32) for b in range(SIDE)]
            halves.append(jnp.concatenate(blocks, axis=0).astype(BF16))
        return jnp.concatenate(halves, axis=1)

    def sum_first(group, part, got, send, recv):
        def tall():
            return remote(
                part.at[0, pl.ds(group * SIDE, SIDE)],
                got.at[0, z],
                send.at[0, 0, group],
                recv.at[0, 0, z],
                {"z": group},
            )

        def flat(i):
            other = lax.rem(x + i, SIDE)
            return remote(
                part.at[1, group * SIDE + other],
                got.at[1, x, group],
                send.at[1, i, group],
                recv.at[1, x, group],
                {"x": other},
            )

        return tall, flat

    def sum_start(group, move):
        tall, flat = sum_first(group, *move)

        @pl.when(group != z)
        def _():
            tall().start()

        @pl.loop(1, SIDE)
        def _(i):
            flat(i).start()

    def sum_wait_send(move):
        @pl.loop(1, SIDE)
        def _(i):
            sum_first(lax.rem(z + i, SIDE), *move)[0]().wait_send()

        @pl.loop(0, SIDE)
        def _(group):
            @pl.loop(1, SIDE)
            def _(i):
                sum_first(group, *move)[1](i).wait_send()

    def second_copy(h, i, passed, last, send, recv):
        own = x if h == 0 else z
        other = lax.rem(own + i, SIDE)
        return remote(
            passed.at[h, other],
            last.at[h, own],
            send.at[h, i],
            recv.at[h, own],
            {"x": other} if h == 0 else {"z": other},
        )

    def sum_finish(move, second):
        part, got, send, recv = move
        passed, last, send_two, recv_two = second

        def across(i):
            other = lax.rem(z + i, SIDE)

            @pl.loop(1, SIDE)
            def _(j):
                source = lax.rem(x + j, SIDE)
                remote(
                    got.at[1, source, other],
                    got.at[1, source, other],
                    send.at[0, 0, 0],
                    recv.at[1, source, other],
                    sibling,
                ).wait_recv()

            acc = part[1, other * SIDE + x].astype(F32)
            for j in range(1, SIDE):
                acc = acc + got[1, lax.rem(x + j, SIDE), other].astype(F32)
            passed[1, other] = acc.astype(BF16)

        @pl.loop(1, SIDE)
        def _(i):
            across(i)
            second_copy(1, i, *second).start()

        @pl.loop(1, SIDE)
        def _(i):
            other = lax.rem(z + i, SIDE)
            remote(
                got.at[0, other], got.at[0, other], send.at[0, 0, 0], recv.at[0, 0, other], sibling
            ).wait_recv()

        @pl.loop(1, SIDE + 1)
        def _(i):
            other = lax.rem(x + i, SIDE)
            acc = part[0, z * SIDE + other].astype(F32)
            for j in range(1, SIDE):
                acc = acc + got[0, lax.rem(z + j, SIDE), other].astype(F32)
            passed[0, other] = acc.astype(BF16)

            @pl.when(i < SIDE)
            def _():
                second_copy(0, i, *second).start()

        across(SIDE)

        for h in range(2):
            own = x if h == 0 else z

            @pl.loop(1, SIDE)
            def _(i):
                other = lax.rem(own + i, SIDE)
                remote(
                    last.at[h, other],
                    last.at[h, other],
                    send_two.at[h, 0],
                    recv_two.at[h, other],
                    sibling,
                ).wait_recv()

            acc = passed[h, own].astype(F32)
            for i in range(1, SIDE):
                acc = acc + last[h, lax.rem(own + i, SIDE)].astype(F32)
            total[:, h * wide : (h + 1) * wide] = acc

    def second_wait_send(second):
        @pl.loop(1, SIDE)
        def _(i):
            for h in range(2):
                second_copy(h, i, *second).wait_send()

    def normed(gain):
        values_in = total[...]
        mean = jnp.mean(values_in * values_in, axis=-1, keepdims=True)
        return values_in * lax.rsqrt(mean + NORM_EPSILON) * gain[...]

    def column_y(kind, view, i):
        other, device = y_peer(i)
        return remote(view(slot), view(slot), c_send.at[kind, i], c_recv.at[kind, slot], device)

    def column_core(kind, view, i):
        held = y_peer(i)[0] * 2 + core
        return remote(
            view(held), view(held), c_send.at[kind, SIDE + i], c_recv.at[kind, held], sibling
        )

    def column_start(kind, view):
        @pl.loop(1, SIDE)
        def _(i):
            column_y(kind, view, i).start()

        column_core(kind, view, 0).start()

    def column_wait(kind, view, held):
        remote(
            view(held), view(held), c_send.at[kind, 0], c_recv.at[kind, held], sibling
        ).wait_recv()

    def column_pass(kind, view):
        @pl.loop(1, SIDE)
        def _(i):
            column_wait(kind, view, y_peer(i)[0] * 2 + core)
            column_core(kind, view, i).start()

    def column_finish(kind, view):
        @pl.loop(0, SIDE)
        def _(i):
            column_wait(kind, view, y_peer(i)[0] * 2 + 1 - core)

    def column_wait_send(kind, view):
        @pl.loop(1, SIDE)
        def _(i):
            column_y(kind, view, i).wait_send()

        @pl.loop(0, SIDE)
        def _(i):
            column_core(kind, view, i).wait_send()

    column = (
        (0, lambda q: qkv_all.at[:, q]),
        (1, lambda q: out_all.at[q]),
        (2, lambda q: mlp_all.at[:, q]),
        (3, lambda q: down_all.at[q]),
    )
    qkv_move = (lambda p: stage_qkv.at[p], lambda p: qkv_all.at[p, slot], s_qkv, r_qkv)
    mlp_move = (lambda p: stage_mlp.at[p], lambda p: mlp_all.at[p, slot], s_mlp, r_mlp)
    sq_move = (lambda p: sq_all.at[me], lambda p: sq_all.at[p], s_sq, r_sq)
    tok_move = (tok_all, s_tok, r_tok)
    hid_move = (hid_all, s_hid, r_hid)
    one_a = (part_a, got_a, s_one_a, r_one_a)
    two_a = (pass_a, last_a, s_two_a, r_two_a)
    one_b = (part_b, got_b, s_one_b, r_one_b)
    two_b = (pass_b, last_b, s_two_b, r_two_b)

    gather_start(*tok_move)
    pl.semaphore_wait(entered, SIDE - 1)
    plane_start(*qkv_move)
    qkv_all[me, slot] = stage_qkv[me]
    for copy in fetches[5:]:
        copy.wait()
    out_all[slot] = output_w[...].astype(BF16)
    down_all[slot] = down_w[...].astype(BF16)

    def numbered(index, which):
        return index + ((index * 1639) >> 16) * rows + which * rows

    flat = lax.broadcasted_iota(jnp.int32, (set_rows, HEAD_DIM), 0)
    row = numbered(flat, yhi)
    start = jnp.zeros_like(row)
    end = jnp.int32(0)
    for r in range(lengths.shape[1]):
        end = end + lengths[0, r]
        start = start + jnp.where(row >= end, lengths[0, r], 0)
    opening[...] = start
    lane = lax.broadcasted_iota(jnp.int32, (1, HEAD_DIM), 1)
    half = HEAD_DIM // 2
    step = jnp.where(lane < half, lane, lane - half).astype(F32)
    frequency = jnp.exp(step * (-2.0 * math.log(ROPE_BASE) / HEAD_DIM))
    angle = (row - start).astype(F32) * frequency
    cosines[...] = jnp.cos(angle)
    sines[...] = jnp.sin(angle) * jnp.where(lane < half, -1.0, 1.0)
    plane_wait_recv(*qkv_move[1:])
    column_start(*column[0])
    column_start(*column[1])
    gather_relay(*tok_move)
    for p in range(PLANE):
        cols = slice(p * hidden_width, (p + 1) * hidden_width)
        for k, w in enumerate((gate_w, up_w)):
            stage_mlp[p, :, k * hidden_width : (k + 1) * hidden_width] = w[:, cols].astype(BF16)
    column_pass(*column[0])
    column_finish(*column[0])

    def chunk(i):
        return pl.ds(pl.multiple_of(i * group_rows, group_rows), group_rows)

    def rotated(values_in, gain, here):
        scaled = values_in * gain
        return (scaled * cosines[here, :] + pltpu.roll(scaled, half, 1) * sines[here, :]).astype(
            BF16
        )

    def kv_copy(group):
        here = chunk(group)
        return remote(
            kv.at[0, here], kv.at[1, here], s_kv.at[group], r_kv.at[group], partner
        )

    sq_all[me] = jnp.zeros_like(sq_all[me])

    @pl.loop(0, SIDE)
    def _(i):
        group = lax.rem(z + i, SIDE)
        here = chunk(group)
        gather_wait_group(*tok_move, group)
        made = dot(gathered(tok_all, group), qkv_all[...].reshape(features, 3 * HEAD_DIM))
        query, key = made[:, :HEAD_DIM], made[:, HEAD_DIM : 2 * HEAD_DIM]
        queries[here, :] = rotated(query, query_gain[pl.ds(me, 1), :], here)
        kv[0, here, :HEAD_DIM] = rotated(key, key_gain[pl.ds(me, 1), :], here)
        kv[0, here, HEAD_DIM:] = made[:, 2 * HEAD_DIM :].astype(BF16)
        kv_copy(group).start()
        pick = (
            lax.broadcasted_iota(jnp.int32, (8, 2 * HEAD_DIM), 1) // HEAD_DIM * SIDE + group
            == lax.broadcasted_iota(jnp.int32, (8, 2 * HEAD_DIM), 0)
        ).astype(F32)
        both = made[:, : 2 * HEAD_DIM]
        sq_all[me] += lax.dot_general(
            pick,
            both * both,
            (((1,), (1,)), ((), ())),
            precision=HIGHEST,
            preferred_element_type=F32,
        )

    plane_start(*sq_move)
    mlp_all[me, slot] = stage_mlp[me]
    column_pass(*column[1])
    plane_wait_recv(*sq_move[1:])
    sums = sq_all[0]
    for p in range(1, PLANE):
        sums = sums + sq_all[p]
    scales[0] = lax.rsqrt(sums / features + NORM_EPSILON)
    scale_copy = remote(scales.at[0], scales.at[1], s_scale, r_scale, partner)
    scale_copy.start()
    plane_start(*mlp_move)
    proj[:, :8] = jnp.transpose(scales[0]) * (1.0 / math.sqrt(HEAD_DIM))
    column_finish(*column[1])

    @pl.loop(0, SIDE)
    def _(group):
        kv_copy(group).wait_recv()

    scale_copy.wait_recv()
    for k in range(2):
        for g in range(SIDE):
            lo = k * set_rows + g * group_rows
            key_scale[:, lo : lo + group_rows] = scales[k, SIDE + g : SIDE + g + 1, :]
    column_start(*column[3])

    lane_index = lax.broadcasted_iota(jnp.int32, (1, set_rows), 1)

    @pl.loop(1, SIDE + 1)
    def _(i):
        group = lax.rem(z + i, SIDE)
        here = chunk(group)
        key_row = jnp.concatenate([numbered(lane_index, yhi), numbered(lane_index, 1 - yhi)], axis=1)
        query_lane = lax.broadcasted_iota(jnp.int32, (group_rows, 8), 1)
        query_scale = jnp.sum(
            jnp.where(query_lane == group, proj[:, :8], 0.0), axis=1, keepdims=True
        )
        own = lax.broadcasted_iota(jnp.int32, (group_rows, 1), 0) + group * group_rows
        own_row = numbered(own, yhi)
        first = opening[here, :][:, 0:1]
        scores = lax.dot_general(
            queries[here, :],
            kv[:, :, :HEAD_DIM].reshape(2 * set_rows, HEAD_DIM),
            (((1,), (1,)), ((), ())),
            preferred_element_type=F32,
        )
        scores = scores * query_scale * key_scale[...]
        scores = jnp.where((key_row >= first) & (key_row <= own_row), scores, -1e30)
        weights = jnp.exp(scores - jnp.max(scores, axis=1, keepdims=True))
        weights = weights / jnp.sum(weights, axis=1, keepdims=True)
        attended = dot(
            weights.astype(BF16), kv[:, :, HEAD_DIM:].reshape(2 * set_rows, HEAD_DIM)
        ).astype(BF16)
        summed = dot(attended, out_all[...].reshape(HEAD_DIM, features))
        for b in range(SIDE):
            for h in range(2):
                part_a[h, group * SIDE + b] = summed[
                    b * rows : (b + 1) * rows, h * wide : (h + 1) * wide
                ].astype(BF16)
        sum_start(group, one_a)

    plane_wait_recv(*mlp_move[1:])
    column_start(*column[2])
    column_pass(*column[3])
    sum_finish(one_a, two_a)
    base = jnp.concatenate([tok_all[0, me], tok_all[1, me]], axis=1).astype(F32)
    hidden = (base + normed(attn_gain)).astype(BF16)
    for h in range(2):
        hid_all[h, me] = hidden[:, h * wide : (h + 1) * wide]
    gather_start(*hid_move)
    gather_relay(*hid_move)
    column_pass(*column[2])
    column_finish(*column[2])
    column_finish(*column[3])

    @pl.loop(0, SIDE)
    def _(i):
        group = lax.rem(z + i, SIDE)
        gather_wait_group(*hid_move, group)
        values_in = gathered(hid_all, group)
        tile = 256
        for c in range(hidden_width // tile):
            lo = c * tile
            gate = dot(values_in, mlp_all[:, :, :, lo : lo + tile].reshape(features, tile))
            lo = lo + hidden_width
            up = dot(values_in, mlp_all[:, :, :, lo : lo + tile].reshape(features, tile))
            act[:, c * tile : (c + 1) * tile] = (gate / (1.0 + jnp.exp(-gate)) * up).astype(BF16)
        across = 512
        for c in range(features // across):
            cols = slice(c * across, (c + 1) * across)
            summed = dot(act[...], down_all[:, :, cols].reshape(hidden_width, across))
            h, lo = c * across // wide, c * across % wide
            for b in range(SIDE):
                part_b[h, group * SIDE + b, :, lo : lo + across] = summed[
                    b * rows : (b + 1) * rows
                ].astype(BF16)
        sum_start(group, one_b)

    sum_finish(one_b, two_b)
    base = jnp.concatenate([hid_all[0, me], hid_all[1, me]], axis=1).astype(F32)
    out[...] = (base + normed(mlp_gain)).astype(BF16)

    for move in (qkv_move, mlp_move, sq_move):
        plane_wait_send(*move)
    for move in (tok_move, hid_move):
        gather_wait_send(*move)
    for one, two in ((one_a, two_a), (one_b, two_b)):
        sum_wait_send(one)
        second_wait_send(two)
    for kind, view in column:
        column_wait_send(kind, view)
    scale_copy.wait_send()

    @pl.loop(0, SIDE)
    def _(group):
        kv_copy(group).wait_send()


def per_device(tokens, lengths, query_gain, key_gain, attn_gain, mlp_gain, *weights):
    rows, features = tokens.shape
    depth = weights[0].shape[0]
    ff = weights[4].shape[1] // PLANE
    down_depth = weights[6].shape[0]
    set_rows = rows * PLANE
    vmem = pl.BlockSpec(memory_space=pltpu.VMEM)
    anywhere = pl.BlockSpec(memory_space=pl.ANY)
    dma = pltpu.SemaphoreType.DMA
    half = (rows, features // 2)
    return pl.pallas_call(
        kernel,
        out_shape=jax.ShapeDtypeStruct(tokens.shape, BF16),
        in_specs=[pl.BlockSpec(memory_space=pltpu.SMEM)] + [anywhere] * 12,
        out_specs=vmem,
        scratch_shapes=[
            pltpu.VMEM((PLANE, HEAD_DIM), F32),
            pltpu.VMEM((PLANE, HEAD_DIM), F32),
            pltpu.VMEM((1, features), F32),
            pltpu.VMEM((1, features), F32),
        ]
        + [pltpu.VMEM(w.shape, F32) for w in weights]
        + [
            pltpu.VMEM((PLANE, depth, 3 * HEAD_DIM), BF16),
            pltpu.VMEM((PLANE, depth, 2 * ff), BF16),
            pltpu.VMEM((PLANE, COLUMN, depth, 3 * HEAD_DIM), BF16),
            pltpu.VMEM((PLANE, COLUMN, depth, 2 * ff), BF16),
            pltpu.VMEM((COLUMN, depth, features), BF16),
            pltpu.VMEM((COLUMN, down_depth, features), BF16),
            pltpu.VMEM((2, PLANE) + half, BF16),
            pltpu.VMEM((2, PLANE) + half, BF16),
            pltpu.VMEM((rows * SIDE, HEAD_DIM), F32),
            pltpu.VMEM((PLANE, 8, rows * SIDE), F32),
            pltpu.VMEM((2, 8, rows * SIDE), F32),
            pltpu.VMEM((1, 2 * set_rows), F32),
            pltpu.VMEM((2, set_rows, 2 * HEAD_DIM), BF16),
            pltpu.VMEM((set_rows, HEAD_DIM), BF16),
            pltpu.VMEM((set_rows, HEAD_DIM), F32),
            pltpu.VMEM((set_rows, HEAD_DIM), F32),
            pltpu.VMEM((set_rows, HEAD_DIM), jnp.int32),
            pltpu.VMEM((2, PLANE) + half, BF16),
            pltpu.VMEM((2, PLANE) + half, BF16),
            pltpu.VMEM((2, SIDE, SIDE) + half, BF16),
            pltpu.VMEM((2, SIDE, SIDE) + half, BF16),
            pltpu.VMEM((2, SIDE) + half, BF16),
            pltpu.VMEM((2, SIDE) + half, BF16),
            pltpu.VMEM((2, SIDE) + half, BF16),
            pltpu.VMEM((2, SIDE) + half, BF16),
            pltpu.VMEM((rows * SIDE, ff), BF16),
            pltpu.VMEM((rows, features), F32),
        ]
        + [dma((PLANE,))] * 6
        + [dma((2, 2, SIDE, SIDE)), dma((2, PLANE))] * 2
        + [dma((2, SIDE, SIDE)), dma((2, SIDE, SIDE)), dma((2, SIDE)), dma((2, SIDE))] * 2
        + [dma((4, COLUMN)), dma((4, COLUMN)), dma((SIDE,)), dma((SIDE,))]
        + [dma(()), dma(()), dma((16,)), pltpu.SemaphoreType.REGULAR],
        compiler_params=pltpu.CompilerParams(
            collective_id=0, has_side_effects=True, vmem_limit_bytes=60 << 20
        ),
    )(
        lengths,
        tokens,
        query_gain.reshape(PLANE, HEAD_DIM),
        key_gain.reshape(PLANE, HEAD_DIM),
        attn_gain[None],
        mlp_gain[None],
        *weights,
    )


def solution(mesh):
    fine = Mesh(mesh.devices.reshape(2, 2, 4, 4, 2), ("ylo", "core", "z", "x", "yhi"))
    tok = P(("ylo", "core", "z", "x", "yhi"), None)
    weight = P(("z", "x", "yhi", "ylo", "core"), None)
    return jax.shard_map(
        per_device,
        mesh=fine,
        in_specs=(tok, P(("ylo", "core"), None), P(), P(), P(), P()) + (weight,) * 7,
        out_specs=tok,
        check_vma=False,
    )
```

```python
import math

import jax
import jax.numpy as jnp
from jax import lax
from jax.experimental import pallas as pl
from jax.experimental.pallas import tpu as pltpu
from jax.sharding import Mesh, PartitionSpec as P

HEAD_DIM = 128
NORM_EPSILON = 1e-06
ROPE_BASE = 500000.0
SIDE = 4
PLANE = SIDE * SIDE
COLUMN = 8
MESH = pl.DeviceIdType.MESH
F32 = jnp.float32
BF16 = jnp.bfloat16
HIGHEST = lax.Precision.HIGHEST


def remote(src, dst, send_sem, recv_sem, device):
    return pltpu.make_async_remote_copy(
        src_ref=src,
        dst_ref=dst,
        send_sem=send_sem,
        recv_sem=recv_sem,
        device_id=device,
        device_id_type=MESH,
    )


def plane_device(place):
    return {"z": place // SIDE, "x": lax.rem(place, SIDE)}


def dot(a, b):
    return jnp.dot(a, b, preferred_element_type=F32)


def kernel(
    lengths,
    tokens,
    query_gain_in,
    key_gain_in,
    attn_gain_in,
    mlp_gain_in,
    query_in,
    key_in,
    value_in,
    output_in,
    gate_in,
    up_in,
    down_in,
    out,
    query_gain,
    key_gain,
    attn_gain,
    mlp_gain,
    query_w,
    key_w,
    value_w,
    output_w,
    gate_w,
    up_w,
    down_w,
    stage_qkv,
    stage_mlp,
    qkv_all,
    mlp_all,
    out_all,
    down_all,
    tok_all,
    hid_all,
    proj,
    sq_all,
    scales,
    key_scale,
    kv,
    queries,
    cosines,
    sines,
    opening,
    part_a,
    part_b,
    got_a,
    got_b,
    pass_a,
    pass_b,
    last_a,
    last_b,
    act,
    total,
    s_qkv,
    r_qkv,
    s_mlp,
    r_mlp,
    s_sq,
    r_sq,
    s_tok,
    r_tok,
    s_hid,
    r_hid,
    s_one_a,
    r_one_a,
    s_two_a,
    r_two_a,
    s_one_b,
    r_one_b,
    s_two_b,
    r_two_b,
    c_send,
    c_recv,
    s_kv,
    r_kv,
    s_scale,
    r_scale,
    fetch,
):
    z, x = lax.axis_index("z"), lax.axis_index("x")
    yhi, ylo, core = lax.axis_index("yhi"), lax.axis_index("ylo"), lax.axis_index("core")
    me = z * SIDE + x
    y = yhi * 2 + ylo
    slot = y * 2 + core
    rows = tokens.shape[0]
    set_rows = rows * PLANE
    group_rows = rows * SIDE
    features = tokens.shape[1]
    wide = features // 2
    hidden_width = act.shape[1]

    def y_peer(step):
        other = lax.rem(y + step, SIDE)
        return other, {"yhi": other // 2, "ylo": lax.rem(other, 2)}

    sibling = {"core": 1 - core}
    partner = {"yhi": 1 - yhi}

    barrier = pltpu.get_barrier_semaphore()

    @pl.loop(1, PLANE)
    def _(i):
        pl.semaphore_signal(
            barrier, inc=1, device_id=plane_device(lax.rem(me + i, PLANE)), device_id_type=MESH
        )

    @pl.loop(1, SIDE)
    def _(i):
        pl.semaphore_signal(barrier, inc=1, device_id=y_peer(i)[1], device_id_type=MESH)

    pl.semaphore_signal(barrier, inc=1, device_id=sibling, device_id_type=MESH)

    inputs = [(tokens.at[:, pl.ds(h * wide, wide)], tok_all.at[h, me]) for h in range(2)] + [
        (query_in, query_w),
        (key_in, key_w),
        (value_in, value_w),
        (output_in, output_w),
        (down_in, down_w),
        (query_gain_in, query_gain),
        (key_gain_in, key_gain),
        (attn_gain_in, attn_gain),
        (mlp_gain_in, mlp_gain),
        (gate_in, gate_w),
        (up_in, up_w),
    ]
    fetches = [pltpu.make_async_copy(*pair, fetch.at[i]) for i, pair in enumerate(inputs)]
    for copy in fetches:
        copy.start()

    for copy in fetches[2:5]:
        copy.wait()
    for p in range(PLANE):
        cols = slice(p * HEAD_DIM, (p + 1) * HEAD_DIM)
        for k, w in enumerate((query_w, key_w, value_w)):
            stage_qkv[p, :, k * HEAD_DIM : (k + 1) * HEAD_DIM] = w[:, cols].astype(BF16)
    for copy in fetches[:2]:
        copy.wait()
    pl.semaphore_wait(barrier, PLANE - 1 + SIDE)

    def plane_copy(i, src, dst, send, recv):
        peer = lax.rem(me + i, PLANE)
        return remote(src(peer), dst(me), send.at[i], recv.at[me], plane_device(peer))

    def plane_start(src, dst, send, recv):
        @pl.loop(1, PLANE)
        def _(i):
            plane_copy(i, src, dst, send, recv).start()

    def plane_wait_send(src, dst, send, recv):
        @pl.loop(1, PLANE)
        def _(i):
            plane_copy(i, src, dst, send, recv).wait_send()

    def plane_wait_recv(dst, send, recv):
        @pl.loop(1, PLANE)
        def _(i):
            peer = lax.rem(me + PLANE - i, PLANE)
            remote(dst(peer), dst(peer), send.at[0], recv.at[peer], plane_device(peer)).wait_recv()

    def along(h, order, i):
        if h == order:
            return z * SIDE + lax.rem(x + i, SIDE)
        return lax.rem(z + i, SIDE) * SIDE + x

    def gather_copy(ref, send, recv, h, order, j, i):
        held = along(h, 0, SIDE - j) if order == 1 else me
        return remote(
            ref.at[h, held],
            ref.at[h, held],
            send.at[h, order, j, i],
            recv.at[h, held],
            plane_device(along(h, order, i)),
        )

    def gather_wait(ref, send, recv, h, held):
        remote(
            ref.at[h, held], ref.at[h, held], send.at[0, 0, 0, 0], recv.at[h, held], sibling
        ).wait_recv()

    def gather_start(ref, send, recv):
        for i in (1, 3, 2):
            for h in range(2):
                gather_copy(ref, send, recv, h, 0, 0, i).start()
        for i in (1, 3, 2):
            for h in range(2):
                if (h, i) != (0, 2):
                    gather_copy(ref, send, recv, h, 1, 0, i).start()

    def gather_relay(ref, send, recv):
        for j in (1, 3, 2):
            for h in range(2):
                gather_wait(ref, send, recv, h, along(h, 0, SIDE - j))
                for i in (1, 3, 2):
                    if (h, i) != (0, 2):
                        gather_copy(ref, send, recv, h, 1, j, i).start()
        for j in (0, 1, 3, 2):
            gather_copy(ref, send, recv, 0, 1, j, 2).start()

    def gather_wait_group(ref, send, recv, group):
        @pl.when(group != z)
        def _():
            @pl.loop(0, SIDE)
            def _(b):
                gather_wait(ref, send, recv, 0, group * SIDE + b)

        @pl.loop(1, SIDE)
        def _(i):
            gather_wait(ref, send, recv, 1, group * SIDE + lax.rem(x + i, SIDE))

    def gather_wait_send(ref, send, recv):
        @pl.loop(1, SIDE)
        def _(i):
            for h in range(2):
                gather_copy(ref, send, recv, h, 0, 0, i).wait_send()

                @pl.loop(0, SIDE)
                def _(j):
                    gather_copy(ref, send, recv, h, 1, j, i).wait_send()

    def near_first(i):
        return lax.rem(z + i + i // 2 * (1 - 2 * lax.rem(i, 2)), SIDE)

    def gathered(ref, group):
        halves = []
        for h in range(2):
            blocks = [ref[h, group * SIDE + b].astype(F32) for b in range(SIDE)]
            halves.append(jnp.concatenate(blocks, axis=0).astype(BF16))
        return jnp.concatenate(halves, axis=1)

    def sum_first(group, part, got, send, recv):
        def tall():
            return remote(
                part.at[0, pl.ds(group * SIDE, SIDE)],
                got.at[0, z],
                send.at[0, 0, group],
                recv.at[0, 0, z],
                {"z": group},
            )

        def flat(i):
            other = lax.rem(x + i, SIDE)
            return remote(
                part.at[1, group * SIDE + other],
                got.at[1, x, group],
                send.at[1, i, group],
                recv.at[1, x, group],
                {"x": other},
            )

        return tall, flat

    def sum_start(group, move):
        tall, flat = sum_first(group, *move)

        @pl.when(group != z)
        def _():
            tall().start()

        @pl.loop(1, SIDE)
        def _(i):
            flat(i).start()

    def sum_wait_send(move):
        @pl.loop(1, SIDE)
        def _(i):
            sum_first(lax.rem(z + i, SIDE), *move)[0]().wait_send()

        @pl.loop(0, SIDE)
        def _(group):
            @pl.loop(1, SIDE)
            def _(i):
                sum_first(group, *move)[1](i).wait_send()

    def second_copy(h, i, passed, last, send, recv):
        own = x if h == 0 else z
        other = lax.rem(own + i, SIDE)
        return remote(
            passed.at[h, other],
            last.at[h, own],
            send.at[h, i],
            recv.at[h, own],
            {"x": other} if h == 0 else {"z": other},
        )

    def sum_finish(move, second):
        part, got, send, recv = move
        passed, last, send_two, recv_two = second

        @pl.loop(1, SIDE)
        def _(i):
            other = lax.rem(z + i, SIDE)
            remote(
                got.at[0, other], got.at[0, other], send.at[0, 0, 0], recv.at[0, 0, other], sibling
            ).wait_recv()

        @pl.loop(1, SIDE + 1)
        def _(i):
            other = lax.rem(x + i, SIDE)
            acc = part[0, z * SIDE + other].astype(F32)
            for j in range(1, SIDE):
                acc = acc + got[0, lax.rem(z + j, SIDE), other].astype(F32)
            passed[0, other] = acc.astype(BF16)

            @pl.when(i < SIDE)
            def _():
                second_copy(0, i, *second).start()

        @pl.loop(1, SIDE + 1)
        def _(i):
            other = lax.rem(z + i, SIDE)

            @pl.loop(1, SIDE)
            def _(j):
                source = lax.rem(x + j, SIDE)
                remote(
                    got.at[1, source, other],
                    got.at[1, source, other],
                    send.at[0, 0, 0],
                    recv.at[1, source, other],
                    sibling,
                ).wait_recv()

            acc = part[1, other * SIDE + x].astype(F32)
            for j in range(1, SIDE):
                acc = acc + got[1, lax.rem(x + j, SIDE), other].astype(F32)
            passed[1, other] = acc.astype(BF16)

            @pl.when(i < SIDE)
            def _():
                second_copy(1, i, *second).start()

        for h in range(2):
            own = x if h == 0 else z

            @pl.loop(1, SIDE)
            def _(i):
                other = lax.rem(own + i, SIDE)
                remote(
                    last.at[h, other],
                    last.at[h, other],
                    send_two.at[h, 0],
                    recv_two.at[h, other],
                    sibling,
                ).wait_recv()

            acc = passed[h, own].astype(F32)
            for i in range(1, SIDE):
                acc = acc + last[h, lax.rem(own + i, SIDE)].astype(F32)
            total[:, h * wide : (h + 1) * wide] = acc

    def second_wait_send(second):
        @pl.loop(1, SIDE)
        def _(i):
            for h in range(2):
                second_copy(h, i, *second).wait_send()

    def normed(gain):
        values_in = total[...]
        mean = jnp.mean(values_in * values_in, axis=-1, keepdims=True)
        return values_in * lax.rsqrt(mean + NORM_EPSILON) * gain[...]

    def column_y(kind, view, i):
        other, device = y_peer(i)
        return remote(view(slot), view(slot), c_send.at[kind, i], c_recv.at[kind, slot], device)

    def column_core(kind, view, i):
        held = y_peer(i)[0] * 2 + core
        return remote(
            view(held), view(held), c_send.at[kind, SIDE + i], c_recv.at[kind, held], sibling
        )

    def column_start(kind, view):
        @pl.loop(1, SIDE)
        def _(i):
            column_y(kind, view, i).start()

        column_core(kind, view, 0).start()

    def column_wait(kind, view, held):
        remote(
            view(held), view(held), c_send.at[kind, 0], c_recv.at[kind, held], sibling
        ).wait_recv()

    def column_pass(kind, view):
        @pl.loop(1, SIDE)
        def _(i):
            column_wait(kind, view, y_peer(i)[0] * 2 + core)
            column_core(kind, view, i).start()

    def column_finish(kind, view):
        @pl.loop(0, SIDE)
        def _(i):
            column_wait(kind, view, y_peer(i)[0] * 2 + 1 - core)

    def column_wait_send(kind, view):
        @pl.loop(1, SIDE)
        def _(i):
            column_y(kind, view, i).wait_send()

        @pl.loop(0, SIDE)
        def _(i):
            column_core(kind, view, i).wait_send()

    column = (
        (0, lambda q: qkv_all.at[:, q]),
        (1, lambda q: out_all.at[q]),
        (2, lambda q: mlp_all.at[:, q]),
        (3, lambda q: down_all.at[q]),
    )
    qkv_move = (lambda p: stage_qkv.at[p], lambda p: qkv_all.at[p, slot], s_qkv, r_qkv)
    mlp_move = (lambda p: stage_mlp.at[p], lambda p: mlp_all.at[p, slot], s_mlp, r_mlp)
    sq_move = (lambda p: sq_all.at[me], lambda p: sq_all.at[p], s_sq, r_sq)
    tok_move = (tok_all, s_tok, r_tok)
    hid_move = (hid_all, s_hid, r_hid)
    one_a = (part_a, got_a, s_one_a, r_one_a)
    two_a = (pass_a, last_a, s_two_a, r_two_a)
    one_b = (part_b, got_b, s_one_b, r_one_b)
    two_b = (pass_b, last_b, s_two_b, r_two_b)

    plane_start(*qkv_move)
    gather_start(*tok_move)
    qkv_all[me, slot] = stage_qkv[me]
    for copy in fetches[5:]:
        copy.wait()
    out_all[slot] = output_w[...].astype(BF16)
    down_all[slot] = down_w[...].astype(BF16)

    def numbered(index, which):
        return index + ((index * 1639) >> 16) * rows + which * rows

    flat = lax.broadcasted_iota(jnp.int32, (set_rows, HEAD_DIM), 0)
    row = numbered(flat, yhi)
    start = jnp.zeros_like(row)
    end = jnp.int32(0)
    for r in range(lengths.shape[1]):
        end = end + lengths[0, r]
        start = start + jnp.where(row >= end, lengths[0, r], 0)
    opening[...] = start
    lane = lax.broadcasted_iota(jnp.int32, (1, HEAD_DIM), 1)
    half = HEAD_DIM // 2
    step = jnp.where(lane < half, lane, lane - half).astype(F32)
    frequency = jnp.exp(step * (-2.0 * math.log(ROPE_BASE) / HEAD_DIM))
    angle = (row - start).astype(F32) * frequency
    cosines[...] = jnp.cos(angle)
    sines[...] = jnp.sin(angle) * jnp.where(lane < half, -1.0, 1.0)
    plane_wait_recv(*qkv_move[1:])
    column_start(*column[0])
    column_start(*column[1])
    gather_relay(*tok_move)
    for p in range(PLANE):
        cols = slice(p * hidden_width, (p + 1) * hidden_width)
        for k, w in enumerate((gate_w, up_w)):
            stage_mlp[p, :, k * hidden_width : (k + 1) * hidden_width] = w[:, cols].astype(BF16)
    column_pass(*column[0])
    column_finish(*column[0])

    def chunk(i):
        return pl.ds(pl.multiple_of(i * group_rows, group_rows), group_rows)

    def rotated(values_in, gain, here):
        scaled = values_in * gain
        return (scaled * cosines[here, :] + pltpu.roll(scaled, half, 1) * sines[here, :]).astype(
            BF16
        )

    def kv_copy(group):
        here = chunk(group)
        return remote(
            kv.at[0, here], kv.at[1, here], s_kv.at[group], r_kv.at[group], partner
        )

    sq_all[me] = jnp.zeros_like(sq_all[me])

    @pl.loop(0, SIDE)
    def _(i):
        group = near_first(i)
        here = chunk(group)
        gather_wait_group(*tok_move, group)
        made = dot(gathered(tok_all, group), qkv_all[...].reshape(features, 3 * HEAD_DIM))
        query, key = made[:, :HEAD_DIM], made[:, HEAD_DIM : 2 * HEAD_DIM]
        queries[here, :] = rotated(query, query_gain[pl.ds(me, 1), :], here)
        kv[0, here, :HEAD_DIM] = rotated(key, key_gain[pl.ds(me, 1), :], here)
        kv[0, here, HEAD_DIM:] = made[:, 2 * HEAD_DIM :].astype(BF16)
        kv_copy(group).start()
        pick = (
            lax.broadcasted_iota(jnp.int32, (8, 2 * HEAD_DIM), 1) // HEAD_DIM * SIDE + group
            == lax.broadcasted_iota(jnp.int32, (8, 2 * HEAD_DIM), 0)
        ).astype(F32)
        both = made[:, : 2 * HEAD_DIM]
        sq_all[me] += lax.dot_general(
            pick,
            both * both,
            (((1,), (1,)), ((), ())),
            precision=HIGHEST,
            preferred_element_type=F32,
        )

    plane_start(*sq_move)
    mlp_all[me, slot] = stage_mlp[me]
    column_pass(*column[1])
    plane_wait_recv(*sq_move[1:])
    sums = sq_all[0]
    for p in range(1, PLANE):
        sums = sums + sq_all[p]
    scales[0] = lax.rsqrt(sums / features + NORM_EPSILON)
    scale_copy = remote(scales.at[0], scales.at[1], s_scale, r_scale, partner)
    scale_copy.start()
    plane_start(*mlp_move)
    proj[:, :8] = jnp.transpose(scales[0]) * (1.0 / math.sqrt(HEAD_DIM))
    column_finish(*column[1])

    @pl.loop(0, SIDE)
    def _(group):
        kv_copy(group).wait_recv()

    scale_copy.wait_recv()
    for k in range(2):
        for g in range(SIDE):
            lo = k * set_rows + g * group_rows
            key_scale[:, lo : lo + group_rows] = scales[k, SIDE + g : SIDE + g + 1, :]
    column_start(*column[3])

    lane_index = lax.broadcasted_iota(jnp.int32, (1, set_rows), 1)

    @pl.loop(1, SIDE + 1)
    def _(i):
        group = lax.rem(z + i, SIDE)
        here = chunk(group)
        key_row = jnp.concatenate([numbered(lane_index, yhi), numbered(lane_index, 1 - yhi)], axis=1)
        query_lane = lax.broadcasted_iota(jnp.int32, (group_rows, 8), 1)
        query_scale = jnp.sum(
            jnp.where(query_lane == group, proj[:, :8], 0.0), axis=1, keepdims=True
        )
        own = lax.broadcasted_iota(jnp.int32, (group_rows, 1), 0) + group * group_rows
        own_row = numbered(own, yhi)
        first = opening[here, :][:, 0:1]
        scores = lax.dot_general(
            queries[here, :],
            kv[:, :, :HEAD_DIM].reshape(2 * set_rows, HEAD_DIM),
            (((1,), (1,)), ((), ())),
            preferred_element_type=F32,
        )
        scores = scores * query_scale * key_scale[...]
        scores = jnp.where((key_row >= first) & (key_row <= own_row), scores, -1e30)
        weights = jnp.exp(scores - jnp.max(scores, axis=1, keepdims=True))
        weights = weights / jnp.sum(weights, axis=1, keepdims=True)
        attended = dot(
            weights.astype(BF16), kv[:, :, HEAD_DIM:].reshape(2 * set_rows, HEAD_DIM)
        ).astype(BF16)
        summed = dot(attended, out_all[...].reshape(HEAD_DIM, features))
        for b in range(SIDE):
            for h in range(2):
                part_a[h, group * SIDE + b] = summed[
                    b * rows : (b + 1) * rows, h * wide : (h + 1) * wide
                ].astype(BF16)
        sum_start(group, one_a)

    plane_wait_recv(*mlp_move[1:])
    column_start(*column[2])
    column_pass(*column[3])
    sum_finish(one_a, two_a)
    base = jnp.concatenate([tok_all[0, me], tok_all[1, me]], axis=1).astype(F32)
    hidden = (base + normed(attn_gain)).astype(BF16)
    for h in range(2):
        hid_all[h, me] = hidden[:, h * wide : (h + 1) * wide]
    gather_start(*hid_move)
    gather_relay(*hid_move)
    column_pass(*column[2])
    column_finish(*column[2])
    column_finish(*column[3])

    @pl.loop(0, SIDE)
    def _(i):
        group = near_first(i)
        gather_wait_group(*hid_move, group)
        values_in = gathered(hid_all, group)
        tile = 256
        for c in range(hidden_width // tile):
            lo = c * tile
            gate = dot(values_in, mlp_all[:, :, :, lo : lo + tile].reshape(features, tile))
            lo = lo + hidden_width
            up = dot(values_in, mlp_all[:, :, :, lo : lo + tile].reshape(features, tile))
            act[:, c * tile : (c + 1) * tile] = (gate / (1.0 + jnp.exp(-gate)) * up).astype(BF16)
        across = 512
        for c in range(features // across):
            cols = slice(c * across, (c + 1) * across)
            summed = dot(act[...], down_all[:, :, cols].reshape(hidden_width, across))
            h, lo = c * across // wide, c * across % wide
            for b in range(SIDE):
                part_b[h, group * SIDE + b, :, lo : lo + across] = summed[
                    b * rows : (b + 1) * rows
                ].astype(BF16)
        sum_start(group, one_b)

    sum_finish(one_b, two_b)
    base = jnp.concatenate([hid_all[0, me], hid_all[1, me]], axis=1).astype(F32)
    out[...] = (base + normed(mlp_gain)).astype(BF16)

    for move in (qkv_move, mlp_move, sq_move):
        plane_wait_send(*move)
    for move in (tok_move, hid_move):
        gather_wait_send(*move)
    for one, two in ((one_a, two_a), (one_b, two_b)):
        sum_wait_send(one)
        second_wait_send(two)
    for kind, view in column:
        column_wait_send(kind, view)
    scale_copy.wait_send()

    @pl.loop(0, SIDE)
    def _(group):
        kv_copy(group).wait_send()


def per_device(tokens, lengths, query_gain, key_gain, attn_gain, mlp_gain, *weights):
    rows, features = tokens.shape
    depth = weights[0].shape[0]
    ff = weights[4].shape[1] // PLANE
    down_depth = weights[6].shape[0]
    set_rows = rows * PLANE
    vmem = pl.BlockSpec(memory_space=pltpu.VMEM)
    anywhere = pl.BlockSpec(memory_space=pl.ANY)
    dma = pltpu.SemaphoreType.DMA
    half = (rows, features // 2)
    return pl.pallas_call(
        kernel,
        out_shape=jax.ShapeDtypeStruct(tokens.shape, BF16),
        in_specs=[pl.BlockSpec(memory_space=pltpu.SMEM)] + [anywhere] * 12,
        out_specs=vmem,
        scratch_shapes=[
            pltpu.VMEM((PLANE, HEAD_DIM), F32),
            pltpu.VMEM((PLANE, HEAD_DIM), F32),
            pltpu.VMEM((1, features), F32),
            pltpu.VMEM((1, features), F32),
        ]
        + [pltpu.VMEM(w.shape, F32) for w in weights]
        + [
            pltpu.VMEM((PLANE, depth, 3 * HEAD_DIM), BF16),
            pltpu.VMEM((PLANE, depth, 2 * ff), BF16),
            pltpu.VMEM((PLANE, COLUMN, depth, 3 * HEAD_DIM), BF16),
            pltpu.VMEM((PLANE, COLUMN, depth, 2 * ff), BF16),
            pltpu.VMEM((COLUMN, depth, features), BF16),
            pltpu.VMEM((COLUMN, down_depth, features), BF16),
            pltpu.VMEM((2, PLANE) + half, BF16),
            pltpu.VMEM((2, PLANE) + half, BF16),
            pltpu.VMEM((rows * SIDE, HEAD_DIM), F32),
            pltpu.VMEM((PLANE, 8, rows * SIDE), F32),
            pltpu.VMEM((2, 8, rows * SIDE), F32),
            pltpu.VMEM((1, 2 * set_rows), F32),
            pltpu.VMEM((2, set_rows, 2 * HEAD_DIM), BF16),
            pltpu.VMEM((set_rows, HEAD_DIM), BF16),
            pltpu.VMEM((set_rows, HEAD_DIM), F32),
            pltpu.VMEM((set_rows, HEAD_DIM), F32),
            pltpu.VMEM((set_rows, HEAD_DIM), jnp.int32),
            pltpu.VMEM((2, PLANE) + half, BF16),
            pltpu.VMEM((2, PLANE) + half, BF16),
            pltpu.VMEM((2, SIDE, SIDE) + half, BF16),
            pltpu.VMEM((2, SIDE, SIDE) + half, BF16),
            pltpu.VMEM((2, SIDE) + half, BF16),
            pltpu.VMEM((2, SIDE) + half, BF16),
            pltpu.VMEM((2, SIDE) + half, BF16),
            pltpu.VMEM((2, SIDE) + half, BF16),
            pltpu.VMEM((rows * SIDE, ff), BF16),
            pltpu.VMEM((rows, features), F32),
        ]
        + [dma((PLANE,))] * 6
        + [dma((2, 2, SIDE, SIDE)), dma((2, PLANE))] * 2
        + [dma((2, SIDE, SIDE)), dma((2, SIDE, SIDE)), dma((2, SIDE)), dma((2, SIDE))] * 2
        + [dma((4, COLUMN)), dma((4, COLUMN)), dma((SIDE,)), dma((SIDE,))]
        + [dma(()), dma(()), dma((16,))],
        compiler_params=pltpu.CompilerParams(
            collective_id=0, has_side_effects=True, vmem_limit_bytes=60 << 20
        ),
    )(
        lengths,
        tokens,
        query_gain.reshape(PLANE, HEAD_DIM),
        key_gain.reshape(PLANE, HEAD_DIM),
        attn_gain[None],
        mlp_gain[None],
        *weights,
    )


def solution(mesh):
    fine = Mesh(mesh.devices.reshape(2, 2, 4, 4, 2), ("ylo", "core", "z", "x", "yhi"))
    tok = P(("ylo", "core", "z", "x", "yhi"), None)
    weight = P(("z", "x", "yhi", "ylo", "core"), None)
    return jax.shard_map(
        per_device,
        mesh=fine,
        in_specs=(tok, P(("ylo", "core"), None), P(), P(), P(), P()) + (weight,) * 7,
        out_specs=tok,
        check_vma=False,
    )
```

```python
import math

import jax
import jax.numpy as jnp
from jax import lax
from jax.experimental import pallas as pl
from jax.experimental.pallas import tpu as pltpu
from jax.sharding import Mesh, PartitionSpec as P

HEAD_DIM = 128
NORM_EPSILON = 1e-06
ROPE_BASE = 500000.0
SIDE = 4
PLANE = SIDE * SIDE
COLUMN = 8
MESH = pl.DeviceIdType.MESH
F32 = jnp.float32
BF16 = jnp.bfloat16
HIGHEST = lax.Precision.HIGHEST


def remote(src, dst, send_sem, recv_sem, device):
    return pltpu.make_async_remote_copy(
        src_ref=src,
        dst_ref=dst,
        send_sem=send_sem,
        recv_sem=recv_sem,
        device_id=device,
        device_id_type=MESH,
    )


def plane_device(place):
    return {"z": place // SIDE, "x": lax.rem(place, SIDE)}


def dot(a, b):
    return jnp.dot(a, b, preferred_element_type=F32)


def kernel(
    lengths,
    tokens,
    query_gain_in,
    key_gain_in,
    attn_gain_in,
    mlp_gain_in,
    query_in,
    key_in,
    value_in,
    output_in,
    gate_in,
    up_in,
    down_in,
    out,
    query_gain,
    key_gain,
    attn_gain,
    mlp_gain,
    query_w,
    key_w,
    value_w,
    output_w,
    gate_w,
    up_w,
    down_w,
    stage_qkv,
    stage_mlp,
    qkv_all,
    mlp_all,
    out_all,
    down_all,
    tok_all,
    hid_all,
    proj,
    sq_all,
    scales,
    key_scale,
    kv,
    queries,
    cosines,
    sines,
    opening,
    part_a,
    part_b,
    got_a,
    got_b,
    pass_a,
    pass_b,
    last_a,
    last_b,
    act,
    total,
    s_qkv,
    r_qkv,
    s_mlp,
    r_mlp,
    s_sq,
    r_sq,
    s_tok,
    r_tok,
    s_hid,
    r_hid,
    s_one_a,
    r_one_a,
    s_two_a,
    r_two_a,
    s_one_b,
    r_one_b,
    s_two_b,
    r_two_b,
    c_send,
    c_recv,
    s_kv,
    r_kv,
    s_scale,
    r_scale,
    fetch,
):
    z, x = lax.axis_index("z"), lax.axis_index("x")
    yhi, ylo, core = lax.axis_index("yhi"), lax.axis_index("ylo"), lax.axis_index("core")
    me = z * SIDE + x
    y = yhi * 2 + ylo
    slot = y * 2 + core
    rows = tokens.shape[0]
    set_rows = rows * PLANE
    group_rows = rows * SIDE
    features = tokens.shape[1]
    wide = features // 2
    hidden_width = act.shape[1]

    def y_peer(step):
        other = lax.rem(y + step, SIDE)
        return other, {"yhi": other // 2, "ylo": lax.rem(other, 2)}

    sibling = {"core": 1 - core}
    partner = {"yhi": 1 - yhi}

    barrier = pltpu.get_barrier_semaphore()

    @pl.loop(1, PLANE)
    def _(i):
        pl.semaphore_signal(
            barrier, inc=1, device_id=plane_device(lax.rem(me + i, PLANE)), device_id_type=MESH
        )

    @pl.loop(1, SIDE)
    def _(i):
        pl.semaphore_signal(barrier, inc=1, device_id=y_peer(i)[1], device_id_type=MESH)

    pl.semaphore_signal(barrier, inc=1, device_id=sibling, device_id_type=MESH)

    inputs = [(tokens.at[:, pl.ds(h * wide, wide)], tok_all.at[h, me]) for h in range(2)] + [
        (query_in, query_w),
        (key_in, key_w),
        (value_in, value_w),
        (output_in, output_w),
        (down_in, down_w),
        (query_gain_in, query_gain),
        (key_gain_in, key_gain),
        (attn_gain_in, attn_gain),
        (mlp_gain_in, mlp_gain),
        (gate_in, gate_w),
        (up_in, up_w),
    ]
    fetches = [pltpu.make_async_copy(*pair, fetch.at[i]) for i, pair in enumerate(inputs)]
    for copy in fetches:
        copy.start()

    for copy in fetches[2:5]:
        copy.wait()
    for p in range(PLANE):
        cols = slice(p * HEAD_DIM, (p + 1) * HEAD_DIM)
        for k, w in enumerate((query_w, key_w, value_w)):
            stage_qkv[p, :, k * HEAD_DIM : (k + 1) * HEAD_DIM] = w[:, cols].astype(BF16)
    for copy in fetches[:2]:
        copy.wait()
    pl.semaphore_wait(barrier, PLANE - 1 + SIDE)

    def plane_copy(i, src, dst, send, recv):
        peer = lax.rem(me + i, PLANE)
        return remote(src(peer), dst(me), send.at[i], recv.at[me], plane_device(peer))

    def plane_start(src, dst, send, recv):
        @pl.loop(1, PLANE)
        def _(i):
            plane_copy(i, src, dst, send, recv).start()

    def plane_wait_send(src, dst, send, recv):
        @pl.loop(1, PLANE)
        def _(i):
            plane_copy(i, src, dst, send, recv).wait_send()

    def plane_wait_recv(dst, send, recv):
        @pl.loop(1, PLANE)
        def _(i):
            peer = lax.rem(me + PLANE - i, PLANE)
            remote(dst(peer), dst(peer), send.at[0], recv.at[peer], plane_device(peer)).wait_recv()

    def along(h, order, i):
        if h == order:
            return z * SIDE + lax.rem(x + i, SIDE)
        return lax.rem(z + i, SIDE) * SIDE + x

    def gather_copy(ref, send, recv, h, order, j, i):
        held = along(h, 0, SIDE - j) if order == 1 else me
        return remote(
            ref.at[h, held],
            ref.at[h, held],
            send.at[h, order, j, i],
            recv.at[h, held],
            plane_device(along(h, order, i)),
        )

    def gather_wait(ref, send, recv, h, held):
        remote(
            ref.at[h, held], ref.at[h, held], send.at[0, 0, 0, 0], recv.at[h, held], sibling
        ).wait_recv()

    def gather_start(ref, send, recv):
        for i in (1, 3, 2):
            for h in range(2):
                gather_copy(ref, send, recv, h, 0, 0, i).start()
        for i in (1, 3, 2):
            for h in range(2):
                if (h, i) != (0, 2):
                    gather_copy(ref, send, recv, h, 1, 0, i).start()

    def gather_relay(ref, send, recv):
        for j in (1, 3, 2):
            for h in range(2):
                gather_wait(ref, send, recv, h, along(h, 0, SIDE - j))
                for i in (1, 3, 2):
                    if (h, i) != (0, 2):
                        gather_copy(ref, send, recv, h, 1, j, i).start()
        for j in (0, 1, 3, 2):
            gather_copy(ref, send, recv, 0, 1, j, 2).start()

    def gather_wait_group(ref, send, recv, group):
        @pl.when(group != z)
        def _():
            @pl.loop(0, SIDE)
            def _(b):
                gather_wait(ref, send, recv, 0, group * SIDE + b)

        @pl.loop(1, SIDE)
        def _(i):
            gather_wait(ref, send, recv, 1, group * SIDE + lax.rem(x + i, SIDE))

    def gather_wait_send(ref, send, recv):
        @pl.loop(1, SIDE)
        def _(i):
            for h in range(2):
                gather_copy(ref, send, recv, h, 0, 0, i).wait_send()

                @pl.loop(0, SIDE)
                def _(j):
                    gather_copy(ref, send, recv, h, 1, j, i).wait_send()

    def near_first(i):
        return lax.rem(z + i + i // 2 * (1 - 2 * lax.rem(i, 2)), SIDE)

    def gathered(ref, group):
        halves = []
        for h in range(2):
            blocks = [ref[h, group * SIDE + b].astype(F32) for b in range(SIDE)]
            halves.append(jnp.concatenate(blocks, axis=0).astype(BF16))
        return jnp.concatenate(halves, axis=1)

    def sum_first(group, part, got, send, recv):
        def tall():
            return remote(
                part.at[0, pl.ds(group * SIDE, SIDE)],
                got.at[0, z],
                send.at[0, 0, group],
                recv.at[0, 0, z],
                {"z": group},
            )

        def flat(i):
            other = lax.rem(x + i, SIDE)
            return remote(
                part.at[1, group * SIDE + other],
                got.at[1, x, group],
                send.at[1, i, group],
                recv.at[1, x, group],
                {"x": other},
            )

        return tall, flat

    def sum_start(group, move):
        tall, flat = sum_first(group, *move)

        @pl.when(group != z)
        def _():
            tall().start()

        @pl.loop(1, SIDE)
        def _(i):
            flat(i).start()

    def sum_wait_send(move):
        @pl.loop(1, SIDE)
        def _(i):
            sum_first(lax.rem(z + i, SIDE), *move)[0]().wait_send()

        @pl.loop(0, SIDE)
        def _(group):
            @pl.loop(1, SIDE)
            def _(i):
                sum_first(group, *move)[1](i).wait_send()

    def second_copy(h, i, passed, last, send, recv):
        own = x if h == 0 else z
        other = lax.rem(own + i, SIDE)
        return remote(
            passed.at[h, other],
            last.at[h, own],
            send.at[h, i],
            recv.at[h, own],
            {"x": other} if h == 0 else {"z": other},
        )

    def sum_finish(move, second, order):
        part, got, send, recv = move
        passed, last, send_two, recv_two = second

        def across(i):
            other = lax.rem(z + i, SIDE)

            @pl.loop(1, SIDE)
            def _(j):
                source = lax.rem(x + j, SIDE)
                remote(
                    got.at[1, source, other],
                    got.at[1, source, other],
                    send.at[0, 0, 0],
                    recv.at[1, source, other],
                    sibling,
                ).wait_recv()

            acc = part[1, other * SIDE + x].astype(F32)
            for j in range(1, SIDE):
                acc = acc + got[1, lax.rem(x + j, SIDE), other].astype(F32)
            passed[1, other] = acc.astype(BF16)
            if i:
                second_copy(1, i, *second).start()

        for i in order[:2]:
            across(i)

        @pl.loop(1, SIDE)
        def _(i):
            other = lax.rem(z + i, SIDE)
            remote(
                got.at[0, other], got.at[0, other], send.at[0, 0, 0], recv.at[0, 0, other], sibling
            ).wait_recv()

        @pl.loop(1, SIDE + 1)
        def _(i):
            other = lax.rem(x + i, SIDE)
            acc = part[0, z * SIDE + other].astype(F32)
            for j in range(1, SIDE):
                acc = acc + got[0, lax.rem(z + j, SIDE), other].astype(F32)
            passed[0, other] = acc.astype(BF16)

            @pl.when(i < SIDE)
            def _():
                second_copy(0, i, *second).start()

        for i in order[2:]:
            across(i)

        for h in range(2):
            own = x if h == 0 else z

            @pl.loop(1, SIDE)
            def _(i):
                other = lax.rem(own + i, SIDE)
                remote(
                    last.at[h, other],
                    last.at[h, other],
                    send_two.at[h, 0],
                    recv_two.at[h, other],
                    sibling,
                ).wait_recv()

            acc = passed[h, own].astype(F32)
            for i in range(1, SIDE):
                acc = acc + last[h, lax.rem(own + i, SIDE)].astype(F32)
            total[:, h * wide : (h + 1) * wide] = acc

    def second_wait_send(second):
        @pl.loop(1, SIDE)
        def _(i):
            for h in range(2):
                second_copy(h, i, *second).wait_send()

    def normed(gain):
        values_in = total[...]
        mean = jnp.mean(values_in * values_in, axis=-1, keepdims=True)
        return values_in * lax.rsqrt(mean + NORM_EPSILON) * gain[...]

    def column_y(kind, view, i):
        other, device = y_peer(i)
        return remote(view(slot), view(slot), c_send.at[kind, i], c_recv.at[kind, slot], device)

    def column_core(kind, view, i):
        held = y_peer(i)[0] * 2 + core
        return remote(
            view(held), view(held), c_send.at[kind, SIDE + i], c_recv.at[kind, held], sibling
        )

    def column_start(kind, view):
        @pl.loop(1, SIDE)
        def _(i):
            column_y(kind, view, i).start()

        column_core(kind, view, 0).start()

    def column_wait(kind, view, held):
        remote(
            view(held), view(held), c_send.at[kind, 0], c_recv.at[kind, held], sibling
        ).wait_recv()

    def column_pass(kind, view):
        @pl.loop(1, SIDE)
        def _(i):
            column_wait(kind, view, y_peer(i)[0] * 2 + core)
            column_core(kind, view, i).start()

    def column_finish(kind, view):
        @pl.loop(0, SIDE)
        def _(i):
            column_wait(kind, view, y_peer(i)[0] * 2 + 1 - core)

    def column_wait_send(kind, view):
        @pl.loop(1, SIDE)
        def _(i):
            column_y(kind, view, i).wait_send()

        @pl.loop(0, SIDE)
        def _(i):
            column_core(kind, view, i).wait_send()

    column = (
        (0, lambda q: qkv_all.at[:, q]),
        (1, lambda q: out_all.at[q]),
        (2, lambda q: mlp_all.at[:, q]),
        (3, lambda q: down_all.at[q]),
    )
    qkv_move = (lambda p: stage_qkv.at[p], lambda p: qkv_all.at[p, slot], s_qkv, r_qkv)
    mlp_move = (lambda p: stage_mlp.at[p], lambda p: mlp_all.at[p, slot], s_mlp, r_mlp)
    sq_move = (lambda p: sq_all.at[me], lambda p: sq_all.at[p], s_sq, r_sq)
    tok_move = (tok_all, s_tok, r_tok)
    hid_move = (hid_all, s_hid, r_hid)
    one_a = (part_a, got_a, s_one_a, r_one_a)
    two_a = (pass_a, last_a, s_two_a, r_two_a)
    one_b = (part_b, got_b, s_one_b, r_one_b)
    two_b = (pass_b, last_b, s_two_b, r_two_b)

    plane_start(*qkv_move)
    gather_start(*tok_move)
    qkv_all[me, slot] = stage_qkv[me]
    for copy in fetches[5:]:
        copy.wait()
    out_all[slot] = output_w[...].astype(BF16)
    down_all[slot] = down_w[...].astype(BF16)

    def numbered(index, which):
        return index + ((index * 1639) >> 16) * rows + which * rows

    flat = lax.broadcasted_iota(jnp.int32, (set_rows, HEAD_DIM), 0)
    row = numbered(flat, yhi)
    start = jnp.zeros_like(row)
    end = jnp.int32(0)
    for r in range(lengths.shape[1]):
        end = end + lengths[0, r]
        start = start + jnp.where(row >= end, lengths[0, r], 0)
    opening[...] = start
    lane = lax.broadcasted_iota(jnp.int32, (1, HEAD_DIM), 1)
    half = HEAD_DIM // 2
    step = jnp.where(lane < half, lane, lane - half).astype(F32)
    frequency = jnp.exp(step * (-2.0 * math.log(ROPE_BASE) / HEAD_DIM))
    angle = (row - start).astype(F32) * frequency
    cosines[...] = jnp.cos(angle)
    sines[...] = jnp.sin(angle) * jnp.where(lane < half, -1.0, 1.0)
    plane_wait_recv(*qkv_move[1:])
    column_start(*column[0])
    gather_relay(*tok_move)
    for p in range(PLANE):
        cols = slice(p * hidden_width, (p + 1) * hidden_width)
        for k, w in enumerate((gate_w, up_w)):
            stage_mlp[p, :, k * hidden_width : (k + 1) * hidden_width] = w[:, cols].astype(BF16)
    column_pass(*column[0])
    column_start(*column[1])
    column_finish(*column[0])

    def chunk(i):
        return pl.ds(pl.multiple_of(i * group_rows, group_rows), group_rows)

    def rotated(values_in, gain, here):
        scaled = values_in * gain
        return (scaled * cosines[here, :] + pltpu.roll(scaled, half, 1) * sines[here, :]).astype(
            BF16
        )

    def kv_copy(group):
        here = chunk(group)
        return remote(
            kv.at[0, here], kv.at[1, here], s_kv.at[group], r_kv.at[group], partner
        )

    sq_all[me] = jnp.zeros_like(sq_all[me])

    @pl.loop(0, SIDE)
    def _(i):
        group = near_first(i)
        here = chunk(group)
        gather_wait_group(*tok_move, group)
        made = dot(gathered(tok_all, group), qkv_all[...].reshape(features, 3 * HEAD_DIM))
        query, key = made[:, :HEAD_DIM], made[:, HEAD_DIM : 2 * HEAD_DIM]
        queries[here, :] = rotated(query, query_gain[pl.ds(me, 1), :], here)
        kv[0, here, :HEAD_DIM] = rotated(key, key_gain[pl.ds(me, 1), :], here)
        kv[0, here, HEAD_DIM:] = made[:, 2 * HEAD_DIM :].astype(BF16)
        kv_copy(group).start()
        pick = (
            lax.broadcasted_iota(jnp.int32, (8, 2 * HEAD_DIM), 1) // HEAD_DIM * SIDE + group
            == lax.broadcasted_iota(jnp.int32, (8, 2 * HEAD_DIM), 0)
        ).astype(F32)
        both = made[:, : 2 * HEAD_DIM]
        sq_all[me] += lax.dot_general(
            pick,
            both * both,
            (((1,), (1,)), ((), ())),
            precision=HIGHEST,
            preferred_element_type=F32,
        )

    plane_start(*sq_move)
    plane_start(*mlp_move)
    mlp_all[me, slot] = stage_mlp[me]
    column_pass(*column[1])
    plane_wait_recv(*sq_move[1:])
    sums = sq_all[0]
    for p in range(1, PLANE):
        sums = sums + sq_all[p]
    scales[0] = lax.rsqrt(sums / features + NORM_EPSILON)
    scale_copy = remote(scales.at[0], scales.at[1], s_scale, r_scale, partner)
    scale_copy.start()
    proj[:, :8] = jnp.transpose(scales[0]) * (1.0 / math.sqrt(HEAD_DIM))
    column_finish(*column[1])

    @pl.loop(0, SIDE)
    def _(group):
        kv_copy(group).wait_recv()

    scale_copy.wait_recv()
    for k in range(2):
        for g in range(SIDE):
            lo = k * set_rows + g * group_rows
            key_scale[:, lo : lo + group_rows] = scales[k, SIDE + g : SIDE + g + 1, :]
    plane_wait_recv(*mlp_move[1:])
    column_start(*column[2])

    lane_index = lax.broadcasted_iota(jnp.int32, (1, set_rows), 1)

    @pl.loop(1, SIDE + 1)
    def _(i):
        group = lax.rem(z + i, SIDE)
        here = chunk(group)
        key_row = jnp.concatenate([numbered(lane_index, yhi), numbered(lane_index, 1 - yhi)], axis=1)
        query_lane = lax.broadcasted_iota(jnp.int32, (group_rows, 8), 1)
        query_scale = jnp.sum(
            jnp.where(query_lane == group, proj[:, :8], 0.0), axis=1, keepdims=True
        )
        own = lax.broadcasted_iota(jnp.int32, (group_rows, 1), 0) + group * group_rows
        own_row = numbered(own, yhi)
        first = opening[here, :][:, 0:1]
        scores = lax.dot_general(
            queries[here, :],
            kv[:, :, :HEAD_DIM].reshape(2 * set_rows, HEAD_DIM),
            (((1,), (1,)), ((), ())),
            preferred_element_type=F32,
        )
        scores = scores * query_scale * key_scale[...]
        scores = jnp.where((key_row >= first) & (key_row <= own_row), scores, -1e30)
        weights = jnp.exp(scores - jnp.max(scores, axis=1, keepdims=True))
        weights = weights / jnp.sum(weights, axis=1, keepdims=True)
        attended = dot(
            weights.astype(BF16), kv[:, :, HEAD_DIM:].reshape(2 * set_rows, HEAD_DIM)
        ).astype(BF16)
        summed = dot(attended, out_all[...].reshape(HEAD_DIM, features))
        for b in range(SIDE):
            for h in range(2):
                part_a[h, group * SIDE + b] = summed[
                    b * rows : (b + 1) * rows, h * wide : (h + 1) * wide
                ].astype(BF16)
        sum_start(group, one_a)

    column_start(*column[3])
    sum_finish(one_a, two_a, (1, 2, 3, 0))
    base = jnp.concatenate([tok_all[0, me], tok_all[1, me]], axis=1).astype(F32)
    hidden = (base + normed(attn_gain)).astype(BF16)
    for h in range(2):
        hid_all[h, me] = hidden[:, h * wide : (h + 1) * wide]
    gather_start(*hid_move)
    gather_relay(*hid_move)
    column_pass(*column[2])
    column_pass(*column[3])
    column_finish(*column[2])
    column_finish(*column[3])

    @pl.loop(0, SIDE)
    def _(i):
        group = near_first(i)
        gather_wait_group(*hid_move, group)
        values_in = gathered(hid_all, group)
        tile = 256
        for c in range(hidden_width // tile):
            lo = c * tile
            gate = dot(values_in, mlp_all[:, :, :, lo : lo + tile].reshape(features, tile))
            lo = lo + hidden_width
            up = dot(values_in, mlp_all[:, :, :, lo : lo + tile].reshape(features, tile))
            act[:, c * tile : (c + 1) * tile] = (gate / (1.0 + jnp.exp(-gate)) * up).astype(BF16)
        across = 512
        for c in range(features // across):
            cols = slice(c * across, (c + 1) * across)
            summed = dot(act[...], down_all[:, :, cols].reshape(hidden_width, across))
            h, lo = c * across // wide, c * across % wide
            for b in range(SIDE):
                part_b[h, group * SIDE + b, :, lo : lo + across] = summed[
                    b * rows : (b + 1) * rows
                ].astype(BF16)
        sum_start(group, one_b)

    for move in (qkv_move, mlp_move, sq_move):
        plane_wait_send(*move)
    for kind, view in column:
        column_wait_send(kind, view)
    scale_copy.wait_send()

    @pl.loop(0, SIDE)
    def _(group):
        kv_copy(group).wait_send()

    gather_wait_send(*tok_move)
    sum_wait_send(one_a)
    second_wait_send(two_a)
    gather_wait_send(*hid_move)
    sum_finish(one_b, two_b, (1, 3, 2, 0))
    base = jnp.concatenate([hid_all[0, me], hid_all[1, me]], axis=1).astype(F32)
    out[...] = (base + normed(mlp_gain)).astype(BF16)

    sum_wait_send(one_b)
    second_wait_send(two_b)


def per_device(tokens, lengths, query_gain, key_gain, attn_gain, mlp_gain, *weights):
    rows, features = tokens.shape
    depth = weights[0].shape[0]
    ff = weights[4].shape[1] // PLANE
    down_depth = weights[6].shape[0]
    set_rows = rows * PLANE
    vmem = pl.BlockSpec(memory_space=pltpu.VMEM)
    anywhere = pl.BlockSpec(memory_space=pl.ANY)
    dma = pltpu.SemaphoreType.DMA
    half = (rows, features // 2)
    return pl.pallas_call(
        kernel,
        out_shape=jax.ShapeDtypeStruct(tokens.shape, BF16),
        in_specs=[pl.BlockSpec(memory_space=pltpu.SMEM)] + [anywhere] * 12,
        out_specs=vmem,
        scratch_shapes=[
            pltpu.VMEM((PLANE, HEAD_DIM), F32),
            pltpu.VMEM((PLANE, HEAD_DIM), F32),
            pltpu.VMEM((1, features), F32),
            pltpu.VMEM((1, features), F32),
        ]
        + [pltpu.VMEM(w.shape, F32) for w in weights]
        + [
            pltpu.VMEM((PLANE, depth, 3 * HEAD_DIM), BF16),
            pltpu.VMEM((PLANE, depth, 2 * ff), BF16),
            pltpu.VMEM((PLANE, COLUMN, depth, 3 * HEAD_DIM), BF16),
            pltpu.VMEM((PLANE, COLUMN, depth, 2 * ff), BF16),
            pltpu.VMEM((COLUMN, depth, features), BF16),
            pltpu.VMEM((COLUMN, down_depth, features), BF16),
            pltpu.VMEM((2, PLANE) + half, BF16),
            pltpu.VMEM((2, PLANE) + half, BF16),
            pltpu.VMEM((rows * SIDE, HEAD_DIM), F32),
            pltpu.VMEM((PLANE, 8, rows * SIDE), F32),
            pltpu.VMEM((2, 8, rows * SIDE), F32),
            pltpu.VMEM((1, 2 * set_rows), F32),
            pltpu.VMEM((2, set_rows, 2 * HEAD_DIM), BF16),
            pltpu.VMEM((set_rows, HEAD_DIM), BF16),
            pltpu.VMEM((set_rows, HEAD_DIM), F32),
            pltpu.VMEM((set_rows, HEAD_DIM), F32),
            pltpu.VMEM((set_rows, HEAD_DIM), jnp.int32),
            pltpu.VMEM((2, PLANE) + half, BF16),
            pltpu.VMEM((2, PLANE) + half, BF16),
            pltpu.VMEM((2, SIDE, SIDE) + half, BF16),
            pltpu.VMEM((2, SIDE, SIDE) + half, BF16),
            pltpu.VMEM((2, SIDE) + half, BF16),
            pltpu.VMEM((2, SIDE) + half, BF16),
            pltpu.VMEM((2, SIDE) + half, BF16),
            pltpu.VMEM((2, SIDE) + half, BF16),
            pltpu.VMEM((rows * SIDE, ff), BF16),
            pltpu.VMEM((rows, features), F32),
        ]
        + [dma((PLANE,))] * 6
        + [dma((2, 2, SIDE, SIDE)), dma((2, PLANE))] * 2
        + [dma((2, SIDE, SIDE)), dma((2, SIDE, SIDE)), dma((2, SIDE)), dma((2, SIDE))] * 2
        + [dma((4, COLUMN)), dma((4, COLUMN)), dma((SIDE,)), dma((SIDE,))]
        + [dma(()), dma(()), dma((16,))],
        compiler_params=pltpu.CompilerParams(
            collective_id=0, has_side_effects=True, vmem_limit_bytes=60 << 20
        ),
    )(
        lengths,
        tokens,
        query_gain.reshape(PLANE, HEAD_DIM),
        key_gain.reshape(PLANE, HEAD_DIM),
        attn_gain[None],
        mlp_gain[None],
        *weights,
    )


def solution(mesh):
    fine = Mesh(mesh.devices.reshape(2, 2, 4, 4, 2), ("ylo", "core", "z", "x", "yhi"))
    tok = P(("ylo", "core", "z", "x", "yhi"), None)
    weight = P(("z", "x", "yhi", "ylo", "core"), None)
    return jax.shard_map(
        per_device,
        mesh=fine,
        in_specs=(tok, P(("ylo", "core"), None), P(), P(), P(), P()) + (weight,) * 7,
        out_specs=tok,
        check_vma=False,
    )
```

```python
import math

import jax
import jax.numpy as jnp
from jax import lax
from jax.experimental import pallas as pl
from jax.experimental.pallas import tpu as pltpu
from jax.sharding import Mesh, PartitionSpec as P

HEAD_DIM = 128
NORM_EPSILON = 1e-06
ROPE_BASE = 500000.0
SIDE = 4
PLANE = SIDE * SIDE
COLUMN = 8
MESH = pl.DeviceIdType.MESH
F32 = jnp.float32
BF16 = jnp.bfloat16
HIGHEST = lax.Precision.HIGHEST


def remote(src, dst, send_sem, recv_sem, device):
    return pltpu.make_async_remote_copy(
        src_ref=src,
        dst_ref=dst,
        send_sem=send_sem,
        recv_sem=recv_sem,
        device_id=device,
        device_id_type=MESH,
    )


def plane_device(place):
    return {"z": place // SIDE, "x": lax.rem(place, SIDE)}


def dot(a, b):
    return jnp.dot(a, b, preferred_element_type=F32)


def kernel(
    lengths,
    tokens,
    query_gain_in,
    key_gain_in,
    attn_gain_in,
    mlp_gain_in,
    query_in,
    key_in,
    value_in,
    output_in,
    gate_in,
    up_in,
    down_in,
    out,
    query_gain,
    key_gain,
    attn_gain,
    mlp_gain,
    query_w,
    key_w,
    value_w,
    output_w,
    gate_w,
    up_w,
    down_w,
    stage_qkv,
    stage_mlp,
    qkv_all,
    mlp_all,
    out_all,
    down_all,
    tok_all,
    hid_all,
    proj,
    sq_all,
    scales,
    key_scale,
    kv,
    queries,
    cosines,
    sines,
    opening,
    part_a,
    part_b,
    got_a,
    got_b,
    pass_a,
    pass_b,
    last_a,
    last_b,
    act,
    total,
    s_qkv,
    r_qkv,
    s_mlp,
    r_mlp,
    s_sq,
    r_sq,
    s_tok,
    r_tok,
    s_hid,
    r_hid,
    s_one_a,
    r_one_a,
    s_two_a,
    r_two_a,
    s_one_b,
    r_one_b,
    s_two_b,
    r_two_b,
    c_send,
    c_recv,
    s_kv,
    r_kv,
    s_scale,
    r_scale,
    fetch,
    h_send,
    h_recv,
):
    z, x = lax.axis_index("z"), lax.axis_index("x")
    yhi, ylo, core = lax.axis_index("yhi"), lax.axis_index("ylo"), lax.axis_index("core")
    me = z * SIDE + x
    y = yhi * 2 + ylo
    slot = y * 2 + core
    rows = tokens.shape[0]
    set_rows = rows * PLANE
    group_rows = rows * SIDE
    features = tokens.shape[1]
    wide = features // 2
    hidden_width = act.shape[1]

    def y_peer(step):
        other = lax.rem(y + step, SIDE)
        return other, {"yhi": other // 2, "ylo": lax.rem(other, 2)}

    sibling = {"core": 1 - core}
    partner = {"yhi": 1 - yhi}

    barrier = pltpu.get_barrier_semaphore()

    @pl.loop(1, PLANE)
    def _(i):
        pl.semaphore_signal(
            barrier, inc=1, device_id=plane_device(lax.rem(me + i, PLANE)), device_id_type=MESH
        )

    @pl.loop(1, SIDE)
    def _(i):
        pl.semaphore_signal(barrier, inc=1, device_id=y_peer(i)[1], device_id_type=MESH)

    pl.semaphore_signal(barrier, inc=1, device_id=sibling, device_id_type=MESH)

    inputs = [(tokens.at[:, pl.ds(h * wide, wide)], tok_all.at[h, me]) for h in range(2)] + [
        (query_in, query_w),
        (key_in, key_w),
        (value_in, value_w),
        (output_in, output_w),
        (down_in, down_w),
        (query_gain_in, query_gain),
        (key_gain_in, key_gain),
        (attn_gain_in, attn_gain),
        (mlp_gain_in, mlp_gain),
        (gate_in, gate_w),
        (up_in, up_w),
    ]
    fetches = [pltpu.make_async_copy(*pair, fetch.at[i]) for i, pair in enumerate(inputs)]
    for copy in fetches:
        copy.start()

    for copy in fetches[2:5]:
        copy.wait()
    for p in range(PLANE):
        cols = slice(p * HEAD_DIM, (p + 1) * HEAD_DIM)
        for k, w in enumerate((query_w, key_w, value_w)):
            stage_qkv[p, :, k * HEAD_DIM : (k + 1) * HEAD_DIM] = w[:, cols].astype(BF16)
    for copy in fetches[:2]:
        copy.wait()
    pl.semaphore_wait(barrier, PLANE - 1 + SIDE)

    def plane_copy(i, src, dst, send, recv):
        peer = lax.rem(me + i, PLANE)
        return remote(src(peer), dst(me), send.at[i], recv.at[me], plane_device(peer))

    def plane_start(src, dst, send, recv):
        @pl.loop(1, PLANE)
        def _(i):
            plane_copy(i, src, dst, send, recv).start()

    def plane_wait_send(src, dst, send, recv):
        @pl.loop(1, PLANE)
        def _(i):
            plane_copy(i, src, dst, send, recv).wait_send()

    def plane_wait_recv(dst, send, recv):
        @pl.loop(1, PLANE)
        def _(i):
            peer = lax.rem(me + PLANE - i, PLANE)
            remote(dst(peer), dst(peer), send.at[0], recv.at[peer], plane_device(peer)).wait_recv()

    def along(h, order, i):
        if h == order:
            return z * SIDE + lax.rem(x + i, SIDE)
        return lax.rem(z + i, SIDE) * SIDE + x

    def gather_copy(ref, send, recv, h, order, j, i):
        held = along(h, 0, SIDE - j) if order == 1 else me
        return remote(
            ref.at[h, held],
            ref.at[h, held],
            send.at[h, order, j, i],
            recv.at[h, held],
            plane_device(along(h, order, i)),
        )

    def gather_wait(ref, send, recv, h, held):
        remote(
            ref.at[h, held], ref.at[h, held], send.at[0, 0, 0, 0], recv.at[h, held], sibling
        ).wait_recv()

    def gather_start(ref, send, recv):
        for i in (1, 3, 2):
            for h in range(2):
                gather_copy(ref, send, recv, h, 0, 0, i).start()
        for i in (1, 3, 2):
            for h in range(2):
                if (h, i) != (0, 2):
                    gather_copy(ref, send, recv, h, 1, 0, i).start()

    def gather_relay(ref, send, recv):
        for j in (1, 3, 2):
            for h in range(2):
                gather_wait(ref, send, recv, h, along(h, 0, SIDE - j))
                for i in (1, 3, 2):
                    if (h, i) != (0, 2):
                        gather_copy(ref, send, recv, h, 1, j, i).start()
        for j in (0, 1, 3, 2):
            gather_copy(ref, send, recv, 0, 1, j, 2).start()

    def gather_wait_group(ref, send, recv, group):
        @pl.when(group != z)
        def _():
            @pl.loop(0, SIDE)
            def _(b):
                gather_wait(ref, send, recv, 0, group * SIDE + b)

        @pl.loop(1, SIDE)
        def _(i):
            gather_wait(ref, send, recv, 1, group * SIDE + lax.rem(x + i, SIDE))

    def gather_wait_send(ref, send, recv):
        @pl.loop(1, SIDE)
        def _(i):
            for h in range(2):
                gather_copy(ref, send, recv, h, 0, 0, i).wait_send()

                @pl.loop(0, SIDE)
                def _(j):
                    gather_copy(ref, send, recv, h, 1, j, i).wait_send()

    def near_first(i):
        return lax.rem(z + i + i // 2 * (1 - 2 * lax.rem(i, 2)), SIDE)

    def gathered(ref, group):
        halves = []
        for h in range(2):
            blocks = [ref[h, group * SIDE + b].astype(F32) for b in range(SIDE)]
            halves.append(jnp.concatenate(blocks, axis=0).astype(BF16))
        return jnp.concatenate(halves, axis=1)

    def sum_first(group, part, got, send, recv):
        def tall():
            return remote(
                part.at[0, pl.ds(group * SIDE, SIDE)],
                got.at[0, z],
                send.at[0, 0, group],
                recv.at[0, 0, z],
                {"z": group},
            )

        def flat(i):
            other = lax.rem(x + i, SIDE)
            return remote(
                part.at[1, group * SIDE + other],
                got.at[1, x, group],
                send.at[1, i, group],
                recv.at[1, x, group],
                {"x": other},
            )

        return tall, flat

    def sum_start(group, move):
        tall, flat = sum_first(group, *move)

        @pl.when(group != z)
        def _():
            tall().start()

        @pl.loop(1, SIDE)
        def _(i):
            flat(i).start()

    def sum_wait_send(move):
        @pl.loop(1, SIDE)
        def _(i):
            sum_first(lax.rem(z + i, SIDE), *move)[0]().wait_send()

        @pl.loop(0, SIDE)
        def _(group):
            @pl.loop(1, SIDE)
            def _(i):
                sum_first(group, *move)[1](i).wait_send()

    def second_copy(h, i, passed, last, send, recv):
        own = x if h == 0 else z
        other = lax.rem(own + i, SIDE)
        return remote(
            passed.at[h, other],
            last.at[h, own],
            send.at[h, i],
            recv.at[h, own],
            {"x": other} if h == 0 else {"z": other},
        )

    def sum_finish(move, second, order):
        part, got, send, recv = move
        passed, last, send_two, recv_two = second

        def across(i):
            other = lax.rem(z + i, SIDE)

            @pl.loop(1, SIDE)
            def _(j):
                source = lax.rem(x + j, SIDE)
                remote(
                    got.at[1, source, other],
                    got.at[1, source, other],
                    send.at[0, 0, 0],
                    recv.at[1, source, other],
                    sibling,
                ).wait_recv()

            acc = part[1, other * SIDE + x].astype(F32)
            for j in range(1, SIDE):
                acc = acc + got[1, lax.rem(x + j, SIDE), other].astype(F32)
            passed[1, other] = acc.astype(BF16)
            if i:
                second_copy(1, i, *second).start()

        for i in order[:2]:
            across(i)

        @pl.loop(1, SIDE)
        def _(i):
            other = lax.rem(z + i, SIDE)
            remote(
                got.at[0, other], got.at[0, other], send.at[0, 0, 0], recv.at[0, 0, other], sibling
            ).wait_recv()

        @pl.loop(1, SIDE + 1)
        def _(i):
            other = lax.rem(x + i, SIDE)
            acc = part[0, z * SIDE + other].astype(F32)
            for j in range(1, SIDE):
                acc = acc + got[0, lax.rem(z + j, SIDE), other].astype(F32)
            passed[0, other] = acc.astype(BF16)

            @pl.when(i < SIDE)
            def _():
                second_copy(0, i, *second).start()

        for i in order[2:]:
            across(i)

        for h in range(2):
            own = x if h == 0 else z

            @pl.loop(1, SIDE)
            def _(i):
                other = lax.rem(own + i, SIDE)
                remote(
                    last.at[h, other],
                    last.at[h, other],
                    send_two.at[h, 0],
                    recv_two.at[h, other],
                    sibling,
                ).wait_recv()

            acc = passed[h, own].astype(F32)
            for i in range(1, SIDE):
                acc = acc + last[h, lax.rem(own + i, SIDE)].astype(F32)
            total[:, h * wide : (h + 1) * wide] = acc

    def second_wait_send(second):
        @pl.loop(1, SIDE)
        def _(i):
            for h in range(2):
                second_copy(h, i, *second).wait_send()

    def normed(gain):
        values_in = total[...]
        mean = jnp.mean(values_in * values_in, axis=-1, keepdims=True)
        return values_in * lax.rsqrt(mean + NORM_EPSILON) * gain[...]

    def column_y(kind, view, i):
        other, device = y_peer(i)
        return remote(view(slot), view(slot), c_send.at[kind, i], c_recv.at[kind, slot], device)

    def column_core(kind, view, i):
        held = y_peer(i)[0] * 2 + core
        return remote(
            view(held), view(held), c_send.at[kind, SIDE + i], c_recv.at[kind, held], sibling
        )

    def column_start(kind, view):
        @pl.loop(1, SIDE)
        def _(i):
            column_y(kind, view, i).start()

        column_core(kind, view, 0).start()

    def column_wait(kind, view, held):
        remote(
            view(held), view(held), c_send.at[kind, 0], c_recv.at[kind, held], sibling
        ).wait_recv()

    def column_pass(kind, view):
        @pl.loop(1, SIDE)
        def _(i):
            column_wait(kind, view, y_peer(i)[0] * 2 + core)
            column_core(kind, view, i).start()

    def column_finish(kind, view):
        @pl.loop(0, SIDE)
        def _(i):
            column_wait(kind, view, y_peer(i)[0] * 2 + 1 - core)

    def column_wait_send(kind, view):
        @pl.loop(1, SIDE)
        def _(i):
            column_y(kind, view, i).wait_send()

        @pl.loop(0, SIDE)
        def _(i):
            column_core(kind, view, i).wait_send()

    def half_view(k, held, e):
        if k == 0:
            return mlp_all.at[pl.ds(e * PLANE // 2, PLANE // 2), held]
        depth = down_all.shape[1] // 2
        return down_all.at[held, pl.ds(e * depth, depth)]

    SIDES = ((SIDE - 1, 0, 1), (1, 1, SIDE - 1))

    def half_copy(k, held, e, to):
        piece = half_view(k, held, e)
        return remote(piece, piece, h_send.at[k, e], h_recv.at[k, e], y_peer(to)[1])

    def column_near(kind, view):
        for i in (1, SIDE - 1):
            column_y(kind, view, i).start()
        column_core(kind, view, 0).start()

    def column_relay(kind, view):
        for off, e, to in SIDES:
            held = y_peer(off)[0] * 2 + core
            column_wait(kind, view, held)
            half_copy(kind - 2, held, e, to).start()
            column_core(kind, view, off).start()

    def column_far(kind, view):
        held = y_peer(2)[0] * 2 + core
        for _, e, to in SIDES:
            half_copy(kind - 2, held, e, to).wait_recv()
        column_core(kind, view, 2).start()

    def column_near_wait_send(kind, view):
        for off, e, to in SIDES:
            column_y(kind, view, off).wait_send()
            half_copy(kind - 2, y_peer(off)[0] * 2 + core, e, to).wait_send()
        for i in range(SIDE):
            column_core(kind, view, i).wait_send()

    column = (
        (0, lambda q: qkv_all.at[:, q]),
        (1, lambda q: out_all.at[q]),
        (2, lambda q: mlp_all.at[:, q]),
        (3, lambda q: down_all.at[q]),
    )
    qkv_move = (lambda p: stage_qkv.at[p], lambda p: qkv_all.at[p, slot], s_qkv, r_qkv)
    mlp_move = (lambda p: stage_mlp.at[p], lambda p: mlp_all.at[p, slot], s_mlp, r_mlp)
    sq_move = (lambda p: sq_all.at[me], lambda p: sq_all.at[p], s_sq, r_sq)
    tok_move = (tok_all, s_tok, r_tok)
    hid_move = (hid_all, s_hid, r_hid)
    one_a = (part_a, got_a, s_one_a, r_one_a)
    two_a = (pass_a, last_a, s_two_a, r_two_a)
    one_b = (part_b, got_b, s_one_b, r_one_b)
    two_b = (pass_b, last_b, s_two_b, r_two_b)

    plane_start(*qkv_move)
    gather_start(*tok_move)
    qkv_all[me, slot] = stage_qkv[me]
    for copy in fetches[5:]:
        copy.wait()
    out_all[slot] = output_w[...].astype(BF16)
    down_all[slot] = down_w[...].astype(BF16)

    def numbered(index, which):
        return index + ((index * 1639) >> 16) * rows + which * rows

    flat = lax.broadcasted_iota(jnp.int32, (set_rows, HEAD_DIM), 0)
    row = numbered(flat, yhi)
    start = jnp.zeros_like(row)
    end = jnp.int32(0)
    for r in range(lengths.shape[1]):
        end = end + lengths[0, r]
        start = start + jnp.where(row >= end, lengths[0, r], 0)
    opening[...] = start
    lane = lax.broadcasted_iota(jnp.int32, (1, HEAD_DIM), 1)
    half = HEAD_DIM // 2
    step = jnp.where(lane < half, lane, lane - half).astype(F32)
    frequency = jnp.exp(step * (-2.0 * math.log(ROPE_BASE) / HEAD_DIM))
    angle = (row - start).astype(F32) * frequency
    cosines[...] = jnp.cos(angle)
    sines[...] = jnp.sin(angle) * jnp.where(lane < half, -1.0, 1.0)
    plane_wait_recv(*qkv_move[1:])
    column_start(*column[0])
    gather_relay(*tok_move)
    for p in range(PLANE):
        cols = slice(p * hidden_width, (p + 1) * hidden_width)
        for k, w in enumerate((gate_w, up_w)):
            stage_mlp[p, :, k * hidden_width : (k + 1) * hidden_width] = w[:, cols].astype(BF16)
    column_pass(*column[0])
    column_start(*column[1])
    column_finish(*column[0])

    def chunk(i):
        return pl.ds(pl.multiple_of(i * group_rows, group_rows), group_rows)

    def rotated(values_in, gain, here):
        scaled = values_in * gain
        return (scaled * cosines[here, :] + pltpu.roll(scaled, half, 1) * sines[here, :]).astype(
            BF16
        )

    def kv_copy(group):
        here = chunk(group)
        return remote(
            kv.at[0, here], kv.at[1, here], s_kv.at[group], r_kv.at[group], partner
        )

    sq_all[me] = jnp.zeros_like(sq_all[me])

    @pl.loop(0, SIDE)
    def _(i):
        group = near_first(i)
        here = chunk(group)
        gather_wait_group(*tok_move, group)
        made = dot(gathered(tok_all, group), qkv_all[...].reshape(features, 3 * HEAD_DIM))
        query, key = made[:, :HEAD_DIM], made[:, HEAD_DIM : 2 * HEAD_DIM]
        queries[here, :] = rotated(query, query_gain[pl.ds(me, 1), :], here)
        kv[0, here, :HEAD_DIM] = rotated(key, key_gain[pl.ds(me, 1), :], here)
        kv[0, here, HEAD_DIM:] = made[:, 2 * HEAD_DIM :].astype(BF16)
        kv_copy(group).start()
        pick = (
            lax.broadcasted_iota(jnp.int32, (8, 2 * HEAD_DIM), 1) // HEAD_DIM * SIDE + group
            == lax.broadcasted_iota(jnp.int32, (8, 2 * HEAD_DIM), 0)
        ).astype(F32)
        both = made[:, : 2 * HEAD_DIM]
        sq_all[me] += lax.dot_general(
            pick,
            both * both,
            (((1,), (1,)), ((), ())),
            precision=HIGHEST,
            preferred_element_type=F32,
        )

    plane_start(*sq_move)
    plane_start(*mlp_move)
    mlp_all[me, slot] = stage_mlp[me]
    column_pass(*column[1])
    plane_wait_recv(*sq_move[1:])
    sums = sq_all[0]
    for p in range(1, PLANE):
        sums = sums + sq_all[p]
    scales[0] = lax.rsqrt(sums / features + NORM_EPSILON)
    scale_copy = remote(scales.at[0], scales.at[1], s_scale, r_scale, partner)
    scale_copy.start()
    proj[:, :8] = jnp.transpose(scales[0]) * (1.0 / math.sqrt(HEAD_DIM))
    column_finish(*column[1])

    @pl.loop(0, SIDE)
    def _(group):
        kv_copy(group).wait_recv()

    scale_copy.wait_recv()
    for k in range(2):
        for g in range(SIDE):
            lo = k * set_rows + g * group_rows
            key_scale[:, lo : lo + group_rows] = scales[k, SIDE + g : SIDE + g + 1, :]
    column_near(*column[3])

    lane_index = lax.broadcasted_iota(jnp.int32, (1, set_rows), 1)

    @pl.loop(1, SIDE + 1)
    def _(i):
        group = lax.rem(z + i, SIDE)
        here = chunk(group)
        key_row = jnp.concatenate([numbered(lane_index, yhi), numbered(lane_index, 1 - yhi)], axis=1)
        query_lane = lax.broadcasted_iota(jnp.int32, (group_rows, 8), 1)
        query_scale = jnp.sum(
            jnp.where(query_lane == group, proj[:, :8], 0.0), axis=1, keepdims=True
        )
        own = lax.broadcasted_iota(jnp.int32, (group_rows, 1), 0) + group * group_rows
        own_row = numbered(own, yhi)
        first = opening[here, :][:, 0:1]
        scores = lax.dot_general(
            queries[here, :],
            kv[:, :, :HEAD_DIM].reshape(2 * set_rows, HEAD_DIM),
            (((1,), (1,)), ((), ())),
            preferred_element_type=F32,
        )
        scores = scores * query_scale * key_scale[...]
        scores = jnp.where((key_row >= first) & (key_row <= own_row), scores, -1e30)
        weights = jnp.exp(scores - jnp.max(scores, axis=1, keepdims=True))
        weights = weights / jnp.sum(weights, axis=1, keepdims=True)
        attended = dot(
            weights.astype(BF16), kv[:, :, HEAD_DIM:].reshape(2 * set_rows, HEAD_DIM)
        ).astype(BF16)
        summed = dot(attended, out_all[...].reshape(HEAD_DIM, features))
        for b in range(SIDE):
            for h in range(2):
                part_a[h, group * SIDE + b] = summed[
                    b * rows : (b + 1) * rows, h * wide : (h + 1) * wide
                ].astype(BF16)
        sum_start(group, one_a)

    plane_wait_recv(*mlp_move[1:])
    column_near(*column[2])
    sum_finish(one_a, two_a, (1, 2, 3, 0))
    base = jnp.concatenate([tok_all[0, me], tok_all[1, me]], axis=1).astype(F32)
    hidden = (base + normed(attn_gain)).astype(BF16)
    for h in range(2):
        hid_all[h, me] = hidden[:, h * wide : (h + 1) * wide]
    gather_start(*hid_move)
    column_relay(*column[2])
    column_relay(*column[3])
    gather_relay(*hid_move)
    column_far(*column[2])
    column_far(*column[3])
    column_finish(*column[2])
    column_finish(*column[3])

    @pl.loop(0, SIDE)
    def _(i):
        group = near_first(i)
        gather_wait_group(*hid_move, group)
        values_in = gathered(hid_all, group)
        tile = 256
        for c in range(hidden_width // tile):
            lo = c * tile
            gate = dot(values_in, mlp_all[:, :, :, lo : lo + tile].reshape(features, tile))
            lo = lo + hidden_width
            up = dot(values_in, mlp_all[:, :, :, lo : lo + tile].reshape(features, tile))
            act[:, c * tile : (c + 1) * tile] = (gate / (1.0 + jnp.exp(-gate)) * up).astype(BF16)
        across = 512
        for c in range(features // across):
            cols = slice(c * across, (c + 1) * across)
            summed = dot(act[...], down_all[:, :, cols].reshape(hidden_width, across))
            h, lo = c * across // wide, c * across % wide
            for b in range(SIDE):
                part_b[h, group * SIDE + b, :, lo : lo + across] = summed[
                    b * rows : (b + 1) * rows
                ].astype(BF16)
        sum_start(group, one_b)

    for move in (qkv_move, mlp_move, sq_move):
        plane_wait_send(*move)
    for kind, view in column[:2]:
        column_wait_send(kind, view)
    for kind, view in column[2:]:
        column_near_wait_send(kind, view)
    scale_copy.wait_send()

    @pl.loop(0, SIDE)
    def _(group):
        kv_copy(group).wait_send()

    gather_wait_send(*tok_move)
    sum_wait_send(one_a)
    second_wait_send(two_a)
    gather_wait_send(*hid_move)
    sum_finish(one_b, two_b, (1, 3, 2, 0))
    base = jnp.concatenate([hid_all[0, me], hid_all[1, me]], axis=1).astype(F32)
    out[...] = (base + normed(mlp_gain)).astype(BF16)

    sum_wait_send(one_b)
    second_wait_send(two_b)


def per_device(tokens, lengths, query_gain, key_gain, attn_gain, mlp_gain, *weights):
    rows, features = tokens.shape
    depth = weights[0].shape[0]
    ff = weights[4].shape[1] // PLANE
    down_depth = weights[6].shape[0]
    set_rows = rows * PLANE
    vmem = pl.BlockSpec(memory_space=pltpu.VMEM)
    anywhere = pl.BlockSpec(memory_space=pl.ANY)
    dma = pltpu.SemaphoreType.DMA
    half = (rows, features // 2)
    return pl.pallas_call(
        kernel,
        out_shape=jax.ShapeDtypeStruct(tokens.shape, BF16),
        in_specs=[pl.BlockSpec(memory_space=pltpu.SMEM)] + [anywhere] * 12,
        out_specs=vmem,
        scratch_shapes=[
            pltpu.VMEM((PLANE, HEAD_DIM), F32),
            pltpu.VMEM((PLANE, HEAD_DIM), F32),
            pltpu.VMEM((1, features), F32),
            pltpu.VMEM((1, features), F32),
        ]
        + [pltpu.VMEM(w.shape, F32) for w in weights]
        + [
            pltpu.VMEM((PLANE, depth, 3 * HEAD_DIM), BF16),
            pltpu.VMEM((PLANE, depth, 2 * ff), BF16),
            pltpu.VMEM((PLANE, COLUMN, depth, 3 * HEAD_DIM), BF16),
            pltpu.VMEM((PLANE, COLUMN, depth, 2 * ff), BF16),
            pltpu.VMEM((COLUMN, depth, features), BF16),
            pltpu.VMEM((COLUMN, down_depth, features), BF16),
            pltpu.VMEM((2, PLANE) + half, BF16),
            pltpu.VMEM((2, PLANE) + half, BF16),
            pltpu.VMEM((rows * SIDE, HEAD_DIM), F32),
            pltpu.VMEM((PLANE, 8, rows * SIDE), F32),
            pltpu.VMEM((2, 8, rows * SIDE), F32),
            pltpu.VMEM((1, 2 * set_rows), F32),
            pltpu.VMEM((2, set_rows, 2 * HEAD_DIM), BF16),
            pltpu.VMEM((set_rows, HEAD_DIM), BF16),
            pltpu.VMEM((set_rows, HEAD_DIM), F32),
            pltpu.VMEM((set_rows, HEAD_DIM), F32),
            pltpu.VMEM((set_rows, HEAD_DIM), jnp.int32),
            pltpu.VMEM((2, PLANE) + half, BF16),
            pltpu.VMEM((2, PLANE) + half, BF16),
            pltpu.VMEM((2, SIDE, SIDE) + half, BF16),
            pltpu.VMEM((2, SIDE, SIDE) + half, BF16),
            pltpu.VMEM((2, SIDE) + half, BF16),
            pltpu.VMEM((2, SIDE) + half, BF16),
            pltpu.VMEM((2, SIDE) + half, BF16),
            pltpu.VMEM((2, SIDE) + half, BF16),
            pltpu.VMEM((rows * SIDE, ff), BF16),
            pltpu.VMEM((rows, features), F32),
        ]
        + [dma((PLANE,))] * 6
        + [dma((2, 2, SIDE, SIDE)), dma((2, PLANE))] * 2
        + [dma((2, SIDE, SIDE)), dma((2, SIDE, SIDE)), dma((2, SIDE)), dma((2, SIDE))] * 2
        + [dma((4, COLUMN)), dma((4, COLUMN)), dma((SIDE,)), dma((SIDE,))]
        + [dma(()), dma(()), dma((16,)), dma((2, 2)), dma((2, 2))],
        compiler_params=pltpu.CompilerParams(
            collective_id=0, has_side_effects=True, vmem_limit_bytes=60 << 20
        ),
    )(
        lengths,
        tokens,
        query_gain.reshape(PLANE, HEAD_DIM),
        key_gain.reshape(PLANE, HEAD_DIM),
        attn_gain[None],
        mlp_gain[None],
        *weights,
    )


def solution(mesh):
    fine = Mesh(mesh.devices.reshape(2, 2, 4, 4, 2), ("ylo", "core", "z", "x", "yhi"))
    tok = P(("ylo", "core", "z", "x", "yhi"), None)
    weight = P(("z", "x", "yhi", "ylo", "core"), None)
    return jax.shard_map(
        per_device,
        mesh=fine,
        in_specs=(tok, P(("ylo", "core"), None), P(), P(), P(), P()) + (weight,) * 7,
        out_specs=tok,
        check_vma=False,
    )
```

```python
import math

import jax
import jax.numpy as jnp
from jax import lax
from jax.experimental import pallas as pl
from jax.experimental.pallas import tpu as pltpu
from jax.sharding import Mesh, PartitionSpec as P

HEAD_DIM = 128
NORM_EPSILON = 1e-06
ROPE_BASE = 500000.0
SIDE = 4
PLANE = SIDE * SIDE
COLUMN = 8
MESH = pl.DeviceIdType.MESH
F32 = jnp.float32
BF16 = jnp.bfloat16
HIGHEST = lax.Precision.HIGHEST


def remote(src, dst, send_sem, recv_sem, device):
    return pltpu.make_async_remote_copy(
        src_ref=src,
        dst_ref=dst,
        send_sem=send_sem,
        recv_sem=recv_sem,
        device_id=device,
        device_id_type=MESH,
    )


def plane_device(place):
    return {"z": place // SIDE, "x": lax.rem(place, SIDE)}


def dot(a, b):
    return jnp.dot(a, b, preferred_element_type=F32)


def kernel(
    lengths,
    tokens,
    query_gain_in,
    key_gain_in,
    attn_gain_in,
    mlp_gain_in,
    query_in,
    key_in,
    value_in,
    output_in,
    gate_in,
    up_in,
    down_in,
    out,
    query_gain,
    key_gain,
    attn_gain,
    mlp_gain,
    query_w,
    key_w,
    value_w,
    output_w,
    gate_w,
    up_w,
    down_w,
    stage_qkv,
    stage_mlp,
    qkv_all,
    mlp_all,
    out_all,
    down_all,
    tok_all,
    hid_all,
    proj,
    sq_all,
    scales,
    key_scale,
    kv,
    queries,
    cosines,
    sines,
    opening,
    part_a,
    part_b,
    got_a,
    got_b,
    pass_a,
    pass_b,
    last_a,
    last_b,
    act,
    total,
    s_qkv,
    r_qkv,
    s_mlp,
    r_mlp,
    s_sq,
    r_sq,
    s_tok,
    r_tok,
    s_hid,
    r_hid,
    s_one_a,
    r_one_a,
    s_two_a,
    r_two_a,
    s_one_b,
    r_one_b,
    s_two_b,
    r_two_b,
    c_send,
    c_recv,
    s_kv,
    r_kv,
    s_scale,
    r_scale,
    fetch,
    h_send,
    h_recv,
):
    z, x = lax.axis_index("z"), lax.axis_index("x")
    yhi, ylo, core = lax.axis_index("yhi"), lax.axis_index("ylo"), lax.axis_index("core")
    me = z * SIDE + x
    y = yhi * 2 + ylo
    slot = y * 2 + core
    rows = tokens.shape[0]
    set_rows = rows * PLANE
    group_rows = rows * SIDE
    features = tokens.shape[1]
    wide = features // 2
    hidden_width = act.shape[1]

    def y_peer(step):
        other = lax.rem(y + step, SIDE)
        return other, {"yhi": other // 2, "ylo": lax.rem(other, 2)}

    sibling = {"core": 1 - core}
    partner = {"yhi": 1 - yhi}

    barrier = pltpu.get_barrier_semaphore()

    @pl.loop(1, PLANE)
    def _(i):
        pl.semaphore_signal(
            barrier, inc=1, device_id=plane_device(lax.rem(me + i, PLANE)), device_id_type=MESH
        )

    @pl.loop(1, SIDE)
    def _(i):
        pl.semaphore_signal(barrier, inc=1, device_id=y_peer(i)[1], device_id_type=MESH)

    pl.semaphore_signal(barrier, inc=1, device_id=sibling, device_id_type=MESH)

    inputs = [(tokens.at[:, pl.ds(h * wide, wide)], tok_all.at[h, me]) for h in range(2)] + [
        (query_in, query_w),
        (key_in, key_w),
        (value_in, value_w),
        (output_in, output_w),
        (down_in, down_w),
        (query_gain_in, query_gain),
        (key_gain_in, key_gain),
        (attn_gain_in, attn_gain),
        (mlp_gain_in, mlp_gain),
        (gate_in, gate_w),
        (up_in, up_w),
    ]
    fetches = [pltpu.make_async_copy(*pair, fetch.at[i]) for i, pair in enumerate(inputs)]
    for copy in fetches:
        copy.start()

    for copy in fetches[2:5]:
        copy.wait()
    for p in range(PLANE):
        cols = slice(p * HEAD_DIM, (p + 1) * HEAD_DIM)
        for k, w in enumerate((query_w, key_w, value_w)):
            stage_qkv[p, :, k * HEAD_DIM : (k + 1) * HEAD_DIM] = w[:, cols].astype(BF16)
    for copy in fetches[:2]:
        copy.wait()
    pl.semaphore_wait(barrier, PLANE - 1 + SIDE)

    def plane_copy(i, src, dst, send, recv):
        peer = lax.rem(me + i, PLANE)
        return remote(src(peer), dst(me), send.at[i], recv.at[me], plane_device(peer))

    def plane_start(src, dst, send, recv):
        @pl.loop(1, PLANE)
        def _(i):
            plane_copy(i, src, dst, send, recv).start()

    def plane_wait_send(src, dst, send, recv):
        @pl.loop(1, PLANE)
        def _(i):
            plane_copy(i, src, dst, send, recv).wait_send()

    def plane_wait_recv(dst, send, recv):
        @pl.loop(1, PLANE)
        def _(i):
            peer = lax.rem(me + PLANE - i, PLANE)
            remote(dst(peer), dst(peer), send.at[0], recv.at[peer], plane_device(peer)).wait_recv()

    def along(h, order, i):
        if h == order:
            return z * SIDE + lax.rem(x + i, SIDE)
        return lax.rem(z + i, SIDE) * SIDE + x

    def gather_copy(ref, send, recv, h, order, j, i):
        held = along(h, 0, SIDE - j) if order == 1 else me
        return remote(
            ref.at[h, held],
            ref.at[h, held],
            send.at[h, order, j, i],
            recv.at[h, held],
            plane_device(along(h, order, i)),
        )

    def gather_wait(ref, send, recv, h, held):
        remote(
            ref.at[h, held], ref.at[h, held], send.at[0, 0, 0, 0], recv.at[h, held], sibling
        ).wait_recv()

    def gather_start(ref, send, recv):
        for i in (1, 3, 2):
            for h in range(2):
                gather_copy(ref, send, recv, h, 0, 0, i).start()
        for i in (1, 3, 2):
            for h in range(2):
                if (h, i) != (0, 2):
                    gather_copy(ref, send, recv, h, 1, 0, i).start()

    def gather_relay(ref, send, recv):
        for j in (1, 3, 2):
            for h in range(2):
                gather_wait(ref, send, recv, h, along(h, 0, SIDE - j))
                for i in (1, 3, 2):
                    if (h, i) != (0, 2):
                        gather_copy(ref, send, recv, h, 1, j, i).start()
        for j in (0, 1, 3, 2):
            gather_copy(ref, send, recv, 0, 1, j, 2).start()

    def gather_wait_group(ref, send, recv, group):
        @pl.when(group != z)
        def _():
            @pl.loop(0, SIDE)
            def _(b):
                gather_wait(ref, send, recv, 0, group * SIDE + b)

        @pl.loop(1, SIDE)
        def _(i):
            gather_wait(ref, send, recv, 1, group * SIDE + lax.rem(x + i, SIDE))

    def gather_wait_send(ref, send, recv):
        @pl.loop(1, SIDE)
        def _(i):
            for h in range(2):
                gather_copy(ref, send, recv, h, 0, 0, i).wait_send()

                @pl.loop(0, SIDE)
                def _(j):
                    gather_copy(ref, send, recv, h, 1, j, i).wait_send()

    def near_first(i):
        return lax.rem(z + i + i // 2 * (1 - 2 * lax.rem(i, 2)), SIDE)

    def gathered(ref, group):
        halves = []
        for h in range(2):
            blocks = [ref[h, group * SIDE + b].astype(F32) for b in range(SIDE)]
            halves.append(jnp.concatenate(blocks, axis=0).astype(BF16))
        return jnp.concatenate(halves, axis=1)

    def sum_first(group, part, got, send, recv):
        def tall():
            return remote(
                part.at[0, pl.ds(group * SIDE, SIDE)],
                got.at[0, z],
                send.at[0, 0, group],
                recv.at[0, 0, z],
                {"z": group},
            )

        def flat(i):
            other = lax.rem(x + i, SIDE)
            return remote(
                part.at[1, group * SIDE + other],
                got.at[1, x, group],
                send.at[1, i, group],
                recv.at[1, x, group],
                {"x": other},
            )

        return tall, flat

    def sum_start_tall(group, move):
        @pl.when(group != z)
        def _():
            sum_first(group, *move)[0]().start()

    def sum_start_flat(group, move):
        @pl.loop(1, SIDE)
        def _(i):
            sum_first(group, *move)[1](i).start()

    def sum_wait_send(move):
        @pl.loop(1, SIDE)
        def _(i):
            sum_first(lax.rem(z + i, SIDE), *move)[0]().wait_send()

        @pl.loop(0, SIDE)
        def _(group):
            @pl.loop(1, SIDE)
            def _(i):
                sum_first(group, *move)[1](i).wait_send()

    def second_copy(h, i, passed, last, send, recv):
        own = x if h == 0 else z
        other = lax.rem(own + i, SIDE)
        return remote(
            passed.at[h, other],
            last.at[h, own],
            send.at[h, i],
            recv.at[h, own],
            {"x": other} if h == 0 else {"z": other},
        )

    def sum_finish(move, second, order):
        part, got, send, recv = move
        passed, last, send_two, recv_two = second

        def across(i):
            other = lax.rem(z + i, SIDE)

            @pl.loop(1, SIDE)
            def _(j):
                source = lax.rem(x + j, SIDE)
                remote(
                    got.at[1, source, other],
                    got.at[1, source, other],
                    send.at[0, 0, 0],
                    recv.at[1, source, other],
                    sibling,
                ).wait_recv()

            acc = part[1, other * SIDE + x].astype(F32)
            for j in range(1, SIDE):
                acc = acc + got[1, lax.rem(x + j, SIDE), other].astype(F32)
            passed[1, other] = acc.astype(BF16)
            if i:
                second_copy(1, i, *second).start()

        for i in order[:2]:
            across(i)

        @pl.loop(1, SIDE)
        def _(i):
            other = lax.rem(z + i, SIDE)
            remote(
                got.at[0, other], got.at[0, other], send.at[0, 0, 0], recv.at[0, 0, other], sibling
            ).wait_recv()

        @pl.loop(1, SIDE + 1)
        def _(i):
            other = lax.rem(x + i, SIDE)
            acc = part[0, z * SIDE + other].astype(F32)
            for j in range(1, SIDE):
                acc = acc + got[0, lax.rem(z + j, SIDE), other].astype(F32)
            passed[0, other] = acc.astype(BF16)

            @pl.when(i < SIDE)
            def _():
                second_copy(0, i, *second).start()

        for i in order[2:]:
            across(i)

        sum_wait_send(move)

        for h in range(2):
            own = x if h == 0 else z

            @pl.loop(1, SIDE)
            def _(i):
                other = lax.rem(own + i, SIDE)
                remote(
                    last.at[h, other],
                    last.at[h, other],
                    send_two.at[h, 0],
                    recv_two.at[h, other],
                    sibling,
                ).wait_recv()

            acc = passed[h, own].astype(F32)
            for i in range(1, SIDE):
                acc = acc + last[h, lax.rem(own + i, SIDE)].astype(F32)
            total[:, h * wide : (h + 1) * wide] = acc

    def second_wait_send(second):
        @pl.loop(1, SIDE)
        def _(i):
            for h in range(2):
                second_copy(h, i, *second).wait_send()

    def normed(gain):
        values_in = total[...]
        mean = jnp.mean(values_in * values_in, axis=-1, keepdims=True)
        return values_in * lax.rsqrt(mean + NORM_EPSILON) * gain[...]

    def column_y(kind, view, i):
        other, device = y_peer(i)
        return remote(view(slot), view(slot), c_send.at[kind, i], c_recv.at[kind, slot], device)

    def column_core(kind, view, i):
        held = y_peer(i)[0] * 2 + core
        return remote(
            view(held), view(held), c_send.at[kind, SIDE + i], c_recv.at[kind, held], sibling
        )

    def column_start(kind, view):
        @pl.loop(1, SIDE)
        def _(i):
            column_y(kind, view, i).start()

        column_core(kind, view, 0).start()

    def column_wait(kind, view, held):
        remote(
            view(held), view(held), c_send.at[kind, 0], c_recv.at[kind, held], sibling
        ).wait_recv()

    def column_pass(kind, view):
        @pl.loop(1, SIDE)
        def _(i):
            column_wait(kind, view, y_peer(i)[0] * 2 + core)
            column_core(kind, view, i).start()

    def column_finish(kind, view):
        @pl.loop(0, SIDE)
        def _(i):
            column_wait(kind, view, y_peer(i)[0] * 2 + 1 - core)

    def column_wait_send(kind, view):
        @pl.loop(1, SIDE)
        def _(i):
            column_y(kind, view, i).wait_send()

        @pl.loop(0, SIDE)
        def _(i):
            column_core(kind, view, i).wait_send()

    def half_view(k, held, e):
        if k == 0:
            return mlp_all.at[pl.ds(e * PLANE // 2, PLANE // 2), held]
        depth = down_all.shape[1] // 2
        return down_all.at[held, pl.ds(e * depth, depth)]

    SIDES = ((SIDE - 1, 0, 1), (1, 1, SIDE - 1))

    def half_copy(k, held, e, to):
        piece = half_view(k, held, e)
        return remote(piece, piece, h_send.at[k, e], h_recv.at[k, e], y_peer(to)[1])

    def column_near(kind, view):
        for i in (1, SIDE - 1):
            column_y(kind, view, i).start()
        column_core(kind, view, 0).start()

    def column_relay(kind, view):
        for off, e, to in SIDES:
            held = y_peer(off)[0] * 2 + core
            column_wait(kind, view, held)
            half_copy(kind - 2, held, e, to).start()
            column_core(kind, view, off).start()

    def column_far(kind, view):
        held = y_peer(2)[0] * 2 + core
        for _, e, to in SIDES:
            half_copy(kind - 2, held, e, to).wait_recv()
        column_core(kind, view, 2).start()

    def column_near_wait_send(kind, view):
        for off, e, to in SIDES:
            column_y(kind, view, off).wait_send()
            half_copy(kind - 2, y_peer(off)[0] * 2 + core, e, to).wait_send()
        for i in range(SIDE):
            column_core(kind, view, i).wait_send()

    column = (
        (0, lambda q: qkv_all.at[:, q]),
        (1, lambda q: out_all.at[q]),
        (2, lambda q: mlp_all.at[:, q]),
        (3, lambda q: down_all.at[q]),
    )
    qkv_move = (lambda p: stage_qkv.at[p], lambda p: qkv_all.at[p, slot], s_qkv, r_qkv)
    mlp_move = (lambda p: stage_mlp.at[p], lambda p: mlp_all.at[p, slot], s_mlp, r_mlp)
    sq_move = (lambda p: sq_all.at[me], lambda p: sq_all.at[p], s_sq, r_sq)
    tok_move = (tok_all, s_tok, r_tok)
    hid_move = (hid_all, s_hid, r_hid)
    one_a = (part_a, got_a, s_one_a, r_one_a)
    two_a = (pass_a, last_a, s_two_a, r_two_a)
    one_b = (part_b, got_b, s_one_b, r_one_b)
    two_b = (pass_b, last_b, s_two_b, r_two_b)

    plane_start(*qkv_move)
    gather_start(*tok_move)
    qkv_all[me, slot] = stage_qkv[me]
    for copy in fetches[5:]:
        copy.wait()
    out_all[slot] = output_w[...].astype(BF16)
    down_all[slot] = down_w[...].astype(BF16)

    def numbered(index, which):
        return index + ((index * 1639) >> 16) * rows + which * rows

    flat = lax.broadcasted_iota(jnp.int32, (set_rows, HEAD_DIM), 0)
    row = numbered(flat, yhi)
    start = jnp.zeros_like(row)
    end = jnp.int32(0)
    for r in range(lengths.shape[1]):
        end = end + lengths[0, r]
        start = start + jnp.where(row >= end, lengths[0, r], 0)
    opening[...] = start
    lane = lax.broadcasted_iota(jnp.int32, (1, HEAD_DIM), 1)
    half = HEAD_DIM // 2
    step = jnp.where(lane < half, lane, lane - half).astype(F32)
    frequency = jnp.exp(step * (-2.0 * math.log(ROPE_BASE) / HEAD_DIM))
    angle = (row - start).astype(F32) * frequency
    cosines[...] = jnp.cos(angle)
    sines[...] = jnp.sin(angle) * jnp.where(lane < half, -1.0, 1.0)
    plane_wait_recv(*qkv_move[1:])
    column_start(*column[0])
    gather_relay(*tok_move)
    for p in range(PLANE):
        cols = slice(p * hidden_width, (p + 1) * hidden_width)
        for k, w in enumerate((gate_w, up_w)):
            stage_mlp[p, :, k * hidden_width : (k + 1) * hidden_width] = w[:, cols].astype(BF16)
    column_pass(*column[0])
    column_start(*column[1])
    column_finish(*column[0])

    def chunk(i):
        return pl.ds(pl.multiple_of(i * group_rows, group_rows), group_rows)

    def rotated(values_in, gain, here):
        scaled = values_in * gain
        return (scaled * cosines[here, :] + pltpu.roll(scaled, half, 1) * sines[here, :]).astype(
            BF16
        )

    def kv_copy(group):
        here = chunk(group)
        return remote(
            kv.at[0, here], kv.at[1, here], s_kv.at[group], r_kv.at[group], partner
        )

    sq_all[me] = jnp.zeros_like(sq_all[me])

    @pl.loop(0, SIDE)
    def _(i):
        group = near_first(i)
        here = chunk(group)
        gather_wait_group(*tok_move, group)
        made = dot(gathered(tok_all, group), qkv_all[...].reshape(features, 3 * HEAD_DIM))
        query, key = made[:, :HEAD_DIM], made[:, HEAD_DIM : 2 * HEAD_DIM]
        queries[here, :] = rotated(query, query_gain[pl.ds(me, 1), :], here)
        kv[0, here, :HEAD_DIM] = rotated(key, key_gain[pl.ds(me, 1), :], here)
        kv[0, here, HEAD_DIM:] = made[:, 2 * HEAD_DIM :].astype(BF16)
        kv_copy(group).start()
        pick = (
            lax.broadcasted_iota(jnp.int32, (8, 2 * HEAD_DIM), 1) // HEAD_DIM * SIDE + group
            == lax.broadcasted_iota(jnp.int32, (8, 2 * HEAD_DIM), 0)
        ).astype(F32)
        both = made[:, : 2 * HEAD_DIM]
        sq_all[me] += lax.dot_general(
            pick,
            both * both,
            (((1,), (1,)), ((), ())),
            precision=HIGHEST,
            preferred_element_type=F32,
        )

    plane_start(*sq_move)
    plane_start(*mlp_move)
    mlp_all[me, slot] = stage_mlp[me]
    column_pass(*column[1])
    plane_wait_recv(*sq_move[1:])
    sums = sq_all[0]
    for p in range(1, PLANE):
        sums = sums + sq_all[p]
    scales[0] = lax.rsqrt(sums / features + NORM_EPSILON)
    scale_copy = remote(scales.at[0], scales.at[1], s_scale, r_scale, partner)
    scale_copy.start()
    proj[:, :8] = jnp.transpose(scales[0]) * (1.0 / math.sqrt(HEAD_DIM))
    column_finish(*column[1])

    @pl.loop(0, SIDE)
    def _(group):
        kv_copy(group).wait_recv()

    scale_copy.wait_recv()
    for k in range(2):
        for g in range(SIDE):
            lo = k * set_rows + g * group_rows
            key_scale[:, lo : lo + group_rows] = scales[k, SIDE + g : SIDE + g + 1, :]
    column_near(*column[3])

    lane_index = lax.broadcasted_iota(jnp.int32, (1, set_rows), 1)

    @pl.loop(1, SIDE + 1)
    def _(i):
        group = lax.rem(z + i, SIDE)
        here = chunk(group)
        key_row = jnp.concatenate([numbered(lane_index, yhi), numbered(lane_index, 1 - yhi)], axis=1)
        query_lane = lax.broadcasted_iota(jnp.int32, (group_rows, 8), 1)
        query_scale = jnp.sum(
            jnp.where(query_lane == group, proj[:, :8], 0.0), axis=1, keepdims=True
        )
        own = lax.broadcasted_iota(jnp.int32, (group_rows, 1), 0) + group * group_rows
        own_row = numbered(own, yhi)
        first = opening[here, :][:, 0:1]
        scores = lax.dot_general(
            queries[here, :],
            kv[:, :, :HEAD_DIM].reshape(2 * set_rows, HEAD_DIM),
            (((1,), (1,)), ((), ())),
            preferred_element_type=F32,
        )
        scores = scores * query_scale * key_scale[...]
        scores = jnp.where((key_row >= first) & (key_row <= own_row), scores, -1e30)
        weights = jnp.exp(scores - jnp.max(scores, axis=1, keepdims=True))
        weights = weights / jnp.sum(weights, axis=1, keepdims=True)
        attended = dot(
            weights.astype(BF16), kv[:, :, HEAD_DIM:].reshape(2 * set_rows, HEAD_DIM)
        ).astype(BF16)
        summed = dot(attended, out_all[...].reshape(HEAD_DIM, features))
        for b in range(SIDE):
            for h in range(2):
                part_a[h, group * SIDE + b] = summed[
                    b * rows : (b + 1) * rows, h * wide : (h + 1) * wide
                ].astype(BF16)
        sum_start_tall(group, one_a)
        sum_start_flat(group, one_a)

    plane_wait_recv(*mlp_move[1:])
    column_near(*column[2])
    sum_finish(one_a, two_a, (1, 2, 3, 0))
    base = jnp.concatenate([tok_all[0, me], tok_all[1, me]], axis=1).astype(F32)
    hidden = (base + normed(attn_gain)).astype(BF16)
    for h in range(2):
        hid_all[h, me] = hidden[:, h * wide : (h + 1) * wide]
    gather_start(*hid_move)
    column_relay(*column[3])
    column_relay(*column[2])
    gather_relay(*hid_move)
    column_far(*column[2])
    column_far(*column[3])
    column_finish(*column[2])
    column_finish(*column[3])

    @pl.loop(0, SIDE)
    def _(i):
        group = near_first(lax.rem(i + 1, SIDE))
        gather_wait_group(*hid_move, group)
        values_in = gathered(hid_all, group)
        tile = 256
        for c in range(hidden_width // tile):
            lo = c * tile
            gate = dot(values_in, mlp_all[:, :, :, lo : lo + tile].reshape(features, tile))
            lo = lo + hidden_width
            up = dot(values_in, mlp_all[:, :, :, lo : lo + tile].reshape(features, tile))
            act[:, c * tile : (c + 1) * tile] = (gate / (1.0 + jnp.exp(-gate)) * up).astype(BF16)
        across = 512
        for c in range(features // across):
            cols = slice(c * across, (c + 1) * across)
            summed = dot(act[...], down_all[:, :, cols].reshape(hidden_width, across))
            h, lo = c * across // wide, c * across % wide
            for b in range(SIDE):
                part_b[h, group * SIDE + b, :, lo : lo + across] = summed[
                    b * rows : (b + 1) * rows
                ].astype(BF16)
            if h == 0 and lo + across == wide:
                sum_start_tall(group, one_b)
        sum_start_flat(group, one_b)

    for move in (qkv_move, mlp_move, sq_move):
        plane_wait_send(*move)
    for kind, view in column[:2]:
        column_wait_send(kind, view)
    for kind, view in column[2:]:
        column_near_wait_send(kind, view)
    scale_copy.wait_send()

    @pl.loop(0, SIDE)
    def _(group):
        kv_copy(group).wait_send()

    gather_wait_send(*tok_move)
    second_wait_send(two_a)
    gather_wait_send(*hid_move)
    sum_finish(one_b, two_b, (1, 3, 2, 0))
    base = jnp.concatenate([hid_all[0, me], hid_all[1, me]], axis=1).astype(F32)
    out[...] = (base + normed(mlp_gain)).astype(BF16)

    second_wait_send(two_b)


def per_device(tokens, lengths, query_gain, key_gain, attn_gain, mlp_gain, *weights):
    rows, features = tokens.shape
    depth = weights[0].shape[0]
    ff = weights[4].shape[1] // PLANE
    down_depth = weights[6].shape[0]
    set_rows = rows * PLANE
    vmem = pl.BlockSpec(memory_space=pltpu.VMEM)
    anywhere = pl.BlockSpec(memory_space=pl.ANY)
    dma = pltpu.SemaphoreType.DMA
    half = (rows, features // 2)
    return pl.pallas_call(
        kernel,
        out_shape=jax.ShapeDtypeStruct(tokens.shape, BF16),
        in_specs=[pl.BlockSpec(memory_space=pltpu.SMEM)] + [anywhere] * 12,
        out_specs=vmem,
        scratch_shapes=[
            pltpu.VMEM((PLANE, HEAD_DIM), F32),
            pltpu.VMEM((PLANE, HEAD_DIM), F32),
            pltpu.VMEM((1, features), F32),
            pltpu.VMEM((1, features), F32),
        ]
        + [pltpu.VMEM(w.shape, F32) for w in weights]
        + [
            pltpu.VMEM((PLANE, depth, 3 * HEAD_DIM), BF16),
            pltpu.VMEM((PLANE, depth, 2 * ff), BF16),
            pltpu.VMEM((PLANE, COLUMN, depth, 3 * HEAD_DIM), BF16),
            pltpu.VMEM((PLANE, COLUMN, depth, 2 * ff), BF16),
            pltpu.VMEM((COLUMN, depth, features), BF16),
            pltpu.VMEM((COLUMN, down_depth, features), BF16),
            pltpu.VMEM((2, PLANE) + half, BF16),
            pltpu.VMEM((2, PLANE) + half, BF16),
            pltpu.VMEM((rows * SIDE, HEAD_DIM), F32),
            pltpu.VMEM((PLANE, 8, rows * SIDE), F32),
            pltpu.VMEM((2, 8, rows * SIDE), F32),
            pltpu.VMEM((1, 2 * set_rows), F32),
            pltpu.VMEM((2, set_rows, 2 * HEAD_DIM), BF16),
            pltpu.VMEM((set_rows, HEAD_DIM), BF16),
            pltpu.VMEM((set_rows, HEAD_DIM), F32),
            pltpu.VMEM((set_rows, HEAD_DIM), F32),
            pltpu.VMEM((set_rows, HEAD_DIM), jnp.int32),
            pltpu.VMEM((2, PLANE) + half, BF16),
            pltpu.VMEM((2, PLANE) + half, BF16),
            pltpu.VMEM((2, SIDE, SIDE) + half, BF16),
            pltpu.VMEM((2, SIDE, SIDE) + half, BF16),
            pltpu.VMEM((2, SIDE) + half, BF16),
            pltpu.VMEM((2, SIDE) + half, BF16),
            pltpu.VMEM((2, SIDE) + half, BF16),
            pltpu.VMEM((2, SIDE) + half, BF16),
            pltpu.VMEM((rows * SIDE, ff), BF16),
            pltpu.VMEM((rows, features), F32),
        ]
        + [dma((PLANE,))] * 6
        + [dma((2, 2, SIDE, SIDE)), dma((2, PLANE))] * 2
        + [dma((2, SIDE, SIDE)), dma((2, SIDE, SIDE)), dma((2, SIDE)), dma((2, SIDE))] * 2
        + [dma((4, COLUMN)), dma((4, COLUMN)), dma((SIDE,)), dma((SIDE,))]
        + [dma(()), dma(()), dma((16,)), dma((2, 2)), dma((2, 2))],
        compiler_params=pltpu.CompilerParams(
            collective_id=0, has_side_effects=True, vmem_limit_bytes=60 << 20
        ),
    )(
        lengths,
        tokens,
        query_gain.reshape(PLANE, HEAD_DIM),
        key_gain.reshape(PLANE, HEAD_DIM),
        attn_gain[None],
        mlp_gain[None],
        *weights,
    )


def solution(mesh):
    fine = Mesh(mesh.devices.reshape(2, 2, 4, 4, 2), ("ylo", "core", "z", "x", "yhi"))
    tok = P(("ylo", "core", "z", "x", "yhi"), None)
    weight = P(("z", "x", "yhi", "ylo", "core"), None)
    return jax.shard_map(
        per_device,
        mesh=fine,
        in_specs=(tok, P(("ylo", "core"), None), P(), P(), P(), P()) + (weight,) * 7,
        out_specs=tok,
        check_vma=False,
    )
```
